32 devices in a mesh: fsdp: 8 (over y, x, core), dp: 4 (over z).
Axes of the slice: x: 2, y: 2, z: 4, core: 2. Of those that a mesh axis runs over, the one named last changes fastest.
Arguments:
- patches: bfloat16 [32, 1024, 192], P(('fsdp', 'dp')), may hold values from -6 to 6
- segments: int32 [32, 1024], P(('fsdp', 'dp')), may hold values from 0 to 31, never falling along the last dimension, each value on 1 to 256 neighbouring positions
- validity: int32 [32, 1024], P(('fsdp', 'dp')), may hold values from 0 to 1, as said below
- image_ids: int32 [32, 1024], P(('fsdp', 'dp')), may hold values from 0 to 1
- code_ids: int32 [32, 1024], P(('fsdp', 'dp')), may hold values from 0 to 8191
- attn_weights: float32 [2, 512, 2048], P(None, 'fsdp'), may hold values from -0.375 to 0.375
- mlp_weights: float32 [2, 512, 4096], P(None, 'fsdp'), may hold values from -0.25 to 0.25
- layer_gains: float32 [2, 9, 512], P(None, None, 'fsdp')
- edge_weights: float32 [512, 450], P('fsdp')
- codebook: float32 [8192, 32], P('fsdp'), may hold values from -1.5 to 1.5
- critic_weights: float32 [194, 512], replicated
- attn_first: float32 [2, 512, 2048], P(None, 'fsdp')
- attn_second: float32 [2, 512, 2048], P(None, 'fsdp')
- mlp_first: float32 [2, 512, 4096], P(None, 'fsdp')
- mlp_second: float32 [2, 512, 4096], P(None, 'fsdp')
- gains_first: float32 [2, 9, 512], P(None, None, 'fsdp')
- gains_second: float32 [2, 9, 512], P(None, None, 'fsdp')
- edges_first: float32 [512, 450], P('fsdp')
- edges_second: float32 [512, 450], P('fsdp')
- codebook_first: float32 [8192, 32], P('fsdp')
- codebook_second: float32 [8192, 32], P('fsdp')
- critic_first: float32 [194, 512], replicated
- critic_second: float32 [194, 512], replicated
Outputs:
- new_attn: float32 [2, 512, 2048], P(None, 'fsdp')
- new_attn_first: float32 [2, 512, 2048], P(None, 'fsdp')
- new_attn_second: float32 [2, 512, 2048], P(None, 'fsdp')
- new_mlp: float32 [2, 512, 4096], P(None, 'fsdp')
- new_mlp_first: float32 [2, 512, 4096], P(None, 'fsdp')
- new_mlp_second: float32 [2, 512, 4096], P(None, 'fsdp')
- new_gains: float32 [2, 9, 512], P(None, None, 'fsdp')
- new_gains_first: float32 [2, 9, 512], P(None, None, 'fsdp')
- new_gains_second: float32 [2, 9, 512], P(None, None, 'fsdp')
- new_edges: float32 [512, 450], P('fsdp')
- new_edges_first: float32 [512, 450], P('fsdp')
- new_edges_second: float32 [512, 450], P('fsdp')
- new_codebook: float32 [8192, 32], P('fsdp')
- new_codebook_first: float32 [8192, 32], P('fsdp')
- new_codebook_second: float32 [8192, 32], P('fsdp')
- new_critic: float32 [194, 512], replicated
- new_critic_first: float32 [194, 512], replicated
- new_critic_second: float32 [194, 512], replicated
- losses: float32 [2], replicated
- grad_norm: float32 [], replicated
- attn_low: bfloat16 [2, 512, 2048], P(None, 'fsdp')
- mlp_low: bfloat16 [2, 512, 4096], P(None, 'fsdp')
- edges_low: bfloat16 [512, 450], P('fsdp')
- codes_low: bfloat16 [8192, 32], P('fsdp')
The draws below stay inside these ranges and needn't reach their ends.
Inputs may be any that keep to these rules, and one draw needn't show every extreme that they name: `validity`: in each row the valid slots come first; the last row is all valid.
All inputs are finite; a program needn't handle non-finite values.
Results may differ from the reference program's by a relative error of at most 0.018.
Values may be sent and summed in bfloat16 or wider, within the bound.
A program may use at most 256 MiB of HBM per device.

```python
import math
import jax
import jax.numpy as jnp
import numpy as np
from jax import lax

D = 512
HEADS = 8
HEAD = 64
FF = 2048
LAT = 32
CODES = 8192
PIX = 192
LAYERS = 2
ROW = 1024
ROWS = 32
EDGE = 450


def noise_field(key, shape):
    return jax.random.normal(key, shape, jnp.float32)


def first_moment(key, shape, size_one):
    return 0.11 * size_one * jax.random.normal(key, shape, jnp.float32)


def second_moment(key, shape, size_one):
    spread = jnp.exp(jax.random.uniform(key, shape, jnp.float32, 0.0, math.log(4.0)))
    return 0.053 * size_one * size_one * spread


def gen_size():
    total = LAYERS * (D * (4 * D + 2 * FF) + 9 * D) + D * EDGE + CODES * LAT
    return 0.5 / math.sqrt(total)


def code_size():
    return 0.25 * gen_size() * math.sqrt(ROW * ROWS) / CODES


def critic_size():
    row_ids = jnp.arange(PIX + 2)[:, None]
    matrix_size = 0.001 + 0.05 / math.sqrt(ROW * ROWS)
    return jnp.where(row_ids < PIX, matrix_size, jnp.where(row_ids == PIX, 0.01, 0.07)).astype(jnp.float32)


def draw_validity(key, part):
    row_ids = jnp.arange(ROWS, dtype=jnp.int32)
    low_len = ROW // 3
    lengths = low_len + (ROW - low_len) * row_ids // (ROWS - 1)
    jitter = jax.random.randint(key, (ROWS,), 0, ROW // 16 + 1)
    lengths = jnp.where(row_ids == ROWS - 1, ROW, jnp.maximum(lengths - jitter, 1))
    return (jnp.arange(ROW, dtype=jnp.int32)[None, :] < lengths[:, None]).astype(jnp.int32)


def draw_layer_gains(key, part):
    noise_draw = noise_field(key, (LAYERS, 9, D))
    row_ids = jnp.arange(9)[None, :, None]
    is_gain = (row_ids == 0) | (row_ids == 2)
    return jnp.where(is_gain, 1.0 + 0.1 * noise_draw, 0.2 * noise_draw)


def draw_edge_weights(key, part):
    noise_draw = noise_field(key, (D, EDGE))
    column = jnp.arange(EDGE)[None, :]
    scaling = jnp.where(column < PIX, PIX ** (-0.5), jnp.where(column < 2 * PIX + LAT, D ** (-0.5), jnp.where(column < 2 * PIX + 2 * LAT, 1.0, 0.2)))
    return jnp.where(column == 2 * PIX + 2 * LAT, 1.0 + 0.1 * noise_draw, scaling * noise_draw)


def draw_critic_weights(key, part):
    noise_draw = noise_field(key, (PIX + 2, D))
    row_ids = jnp.arange(PIX + 2)[:, None]
    scaling = jnp.where(row_ids < PIX, PIX ** (-0.5), jnp.where(row_ids == PIX, 0.2, 1.5 * D ** (-0.5)))
    return scaling * noise_draw


def draw_attn_first(key, part):
    return first_moment(key, (LAYERS, D, 4 * D), gen_size())


def draw_attn_second(key, part):
    return second_moment(key, (LAYERS, D, 4 * D), gen_size())


def draw_mlp_first(key, part):
    return first_moment(key, (LAYERS, D, 2 * FF), gen_size())


def draw_mlp_second(key, part):
    return second_moment(key, (LAYERS, D, 2 * FF), gen_size())


def draw_gains_first(key, part):
    return first_moment(key, (LAYERS, 9, D), gen_size())


def draw_gains_second(key, part):
    return second_moment(key, (LAYERS, 9, D), gen_size())


def draw_edges_first(key, part):
    return first_moment(key, (D, EDGE), gen_size())


def draw_edges_second(key, part):
    return second_moment(key, (D, EDGE), gen_size())


def draw_codebook_first(key, part):
    return first_moment(key, (CODES, LAT), code_size())


def draw_codebook_second(key, part):
    return second_moment(key, (CODES, LAT), code_size())


def draw_critic_first(key, part):
    return first_moment(key, (PIX + 2, D), critic_size())


def draw_critic_second(key, part):
    return second_moment(key, (PIX + 2, D), critic_size())


def with_ends(drawn, stream_key, low, high):
    extent = drawn.shape
    place = [jax.random.randint(jax.random.fold_in(stream_key, axis), (), 0, extent[axis]) for axis in range(len(extent))]
    drawn = drawn.at[tuple(place)].set(low)
    longest = extent.index(max(extent))
    place[longest] = (place[longest] + 1) % extent[longest]
    return drawn.at[tuple(place)].set(high)


def block_levels(stream_key, dims, pieces, least, high):
    level = 1.0
    for dim, blocks in pieces:
        heights = jax.random.uniform(jax.random.fold_in(jax.random.fold_in(stream_key, 6), dim), (blocks,), jnp.float32, least / len(pieces), high / len(pieces))
        level = level * jnp.repeat(jnp.exp(heights), dims[dim] // blocks).reshape((-1,) + (1,) * (len(dims) - 1 - dim))
    return level


def length_profile(count, total, reach, slope):
    weights = [(1 << 20) // math.isqrt(rank ** slope) + 1 for rank in range(2, count + 1)]
    rest, given = total - reach - (count - 1), [1] * (count - 1)
    while rest > 0:
        free = [i for i in range(count - 1) if given[i] < reach]
        pool, left = sum([weights[i] for i in free]), rest
        for i in free:
            addition = min(reach - given[i], max(1, left * weights[i] // pool), rest)
            given[i] = given[i] + addition
            rest = rest - addition
    return np.array([reach] + given)


def uneven(own_key, count, total, reach, skew):
    if count == 2:
        one = jax.random.randint(own_key, (), max(1, total - reach), min(reach, total - 1) + 1)
        return jnp.stack([one, total - one])
    tallies = jnp.asarray(length_profile(count, total, reach, skew), jnp.int32)
    couples = (count - 1) // 2
    donor, taker = tallies[1:1 + 2 * couples:2], tallies[2:2 + 2 * couples:2]
    margin = jnp.minimum(donor - 1, reach - taker)
    passed = jax.random.randint(jax.random.fold_in(own_key, 1), (couples,), 0, 1 << 20) % (margin + 1)
    tallies = tallies.at[1:1 + 2 * couples:2].set(donor - passed).at[2:2 + 2 * couples:2].set(taker + passed)
    return tallies[jax.random.permutation(jax.random.fold_in(own_key, 2), count)]


def scatter_about(own_key, shape, deviation, bound, shards=(), kind=jnp.bfloat16):
    entries = deviation * jax.random.normal(own_key, shape, jnp.float32)
    if shards:
        entries = entries * block_levels(own_key, shape, shards, -0.22, 0.18)
    return jnp.clip(entries, -bound, bound).astype(kind)


def setup_inputs(seed: int = 0) -> dict:
    streams_of = jax.random.split(jax.random.key(seed), 24)
    patches = scatter_about(streams_of[0], (ROWS, ROW, PIX), 1.0, 6.0, ((0, 32),))
    segments = jax.vmap(lambda own: jnp.searchsorted(jnp.cumsum(uneven(own, max(6, ROW // 32), ROW, max(8, ROW // 4), 2)), jnp.arange(ROW), side="right"))(jax.random.split(streams_of[1], ROWS)).reshape((ROWS, ROW)).astype(jnp.int32)
    validity = draw_validity(jax.random.fold_in(streams_of[23], 71), 0)
    image_ids = with_ends(jax.random.randint(streams_of[3], (ROWS, ROW), 0, 2), jax.random.fold_in(streams_of[3], 1), 0, 1).astype(jnp.int32)
    code_ids = with_ends(jax.random.randint(streams_of[4], (ROWS, ROW), 0, CODES), jax.random.fold_in(streams_of[4], 1), 0, CODES - 1).astype(jnp.int32)
    attn_weights = scatter_about(streams_of[5], (LAYERS, D, 4 * D), (D // 2) ** -0.5, 0.375, ((1, 8),), jnp.float32)
    mlp_weights = scatter_about(streams_of[6], (LAYERS, D, 2 * FF), D ** -0.5, 0.25, ((1, 8),), jnp.float32)
    layer_gains = draw_layer_gains(jax.random.fold_in(streams_of[23], 71), 0)
    edge_weights = draw_edge_weights(jax.random.fold_in(streams_of[23], 71), 0)
    codebook = scatter_about(streams_of[9], (CODES, LAT), 0.25, 1.5, ((0, 8),), jnp.float32)
    critic_weights = draw_critic_weights(jax.random.fold_in(streams_of[23], 71), 0)
    attn_first = draw_attn_first(jax.random.fold_in(streams_of[23], 71), 0)
    attn_second = draw_attn_second(jax.random.fold_in(streams_of[23], 71), 0)
    mlp_first = draw_mlp_first(jax.random.fold_in(streams_of[23], 71), 0)
    mlp_second = draw_mlp_second(jax.random.fold_in(streams_of[23], 71), 0)
    gains_first = draw_gains_first(jax.random.fold_in(streams_of[23], 71), 0)
    gains_second = draw_gains_second(jax.random.fold_in(streams_of[23], 71), 0)
    edges_first = draw_edges_first(jax.random.fold_in(streams_of[23], 71), 0)
    edges_second = draw_edges_second(jax.random.fold_in(streams_of[23], 71), 0)
    codebook_first = draw_codebook_first(jax.random.fold_in(streams_of[23], 71), 0)
    codebook_second = draw_codebook_second(jax.random.fold_in(streams_of[23], 71), 0)
    critic_first = draw_critic_first(jax.random.fold_in(streams_of[23], 71), 0)
    critic_second = draw_critic_second(jax.random.fold_in(streams_of[23], 71), 0)
    return dict(patches=patches, segments=segments, validity=validity, image_ids=image_ids, code_ids=code_ids, attn_weights=attn_weights, mlp_weights=mlp_weights, layer_gains=layer_gains, edge_weights=edge_weights, codebook=codebook, critic_weights=critic_weights, attn_first=attn_first, attn_second=attn_second, mlp_first=mlp_first, mlp_second=mlp_second, gains_first=gains_first, gains_second=gains_second, edges_first=edges_first, edges_second=edges_second, codebook_first=codebook_first, codebook_second=codebook_second, critic_first=critic_first, critic_second=critic_second)


@jax.custom_vjp
def low(v):
    return lax.optimization_barrier(v.astype(jnp.bfloat16)).astype(jnp.float32)

@jax.custom_vjp
def low_back(v):
    return v

def low_keep(v):
    return (low(v), None)

def low_pass(kept, grad):
    return (grad,)

def back_keep(v):
    return (v, None)

def back_low(kept, grad):
    return (low(grad),)
low.defvjp(low_keep, low_pass)
low_back.defvjp(back_keep, back_low)
beta_one = 0.9
beta_two = 0.95
adam_eps = 1e-08
decay_rate = 0.1
learn_rate = 0.2
clip_norm = 0.5
commit_weight = 0.25
adverse_weight = 0.2
adam_step = 10.0
norm_eps = 1e-05
masked_score = -1000000000.0

def high_dot(left_side, right_side):
    return jnp.dot(left_side, right_side, precision=lax.Precision.HIGHEST, preferred_element_type=jnp.float32)

def layer_norm(values, gain, shift):
    center = values - lax.optimization_barrier(jnp.mean(values, axis=-1, keepdims=True))
    spread = lax.optimization_barrier(jnp.mean(center * center, axis=-1, keepdims=True))
    return center * lax.rsqrt(spread + norm_eps) * gain + shift

def gelu_tanh(values):
    cubic_term = values + 0.044715 * values * values * values
    return 0.5 * values * (1.0 + jnp.tanh(0.7978845608028654 * cubic_term))

def normalize_rows(values):
    return values * lax.rsqrt(lax.optimization_barrier(jnp.sum(values * values, axis=-1, keepdims=True)) + 1.0)

def feature_table():
    pixel_idx = jnp.arange(PIX, dtype=jnp.float32)[:, None]
    frequency = jnp.arange(PIX, dtype=jnp.float32)[None, :]
    return jnp.cos(math.pi * (pixel_idx + 0.5) * frequency / PIX) * (math.sqrt(2.0 / PIX) / (1.0 + frequency / 16.0))

def attend(hidden, weights, segment, valid_row):
    length = hidden.shape[0]
    mixed_qkv = low_back(low(high_dot(hidden, weights[:, :3 * D])))
    queries = mixed_qkv[:, :D].reshape(length, HEADS, HEAD)
    keys_all = mixed_qkv[:, D:2 * D].reshape(length, HEADS, HEAD)
    values_all = mixed_qkv[:, 2 * D:].reshape(length, HEADS, HEAD)
    scores = jnp.einsum('qhd,khd->hqk', queries, keys_all, precision=lax.Precision.HIGHEST) * HEAD ** (-0.5)
    scores = low_back(scores)
    position = jnp.arange(length)
    allowed = (segment[:, None] == segment[None, :]) & ((valid_row[None, :] > 0) | (position[:, None] == position[None, :]))
    attn_probs = low(jax.nn.softmax(jnp.where(allowed[None], scores, masked_score), axis=-1))
    context = jnp.einsum('hqk,khd->qhd', attn_probs, values_all, precision=lax.Precision.HIGHEST).reshape(length, D)
    context = low_back(low(context))
    return low_back(high_dot(context, weights[:, 3 * D:]))

def block_apply(stream, attn_w, mlp_w, gain_rows, segment, valid_row):
    hidden = low(layer_norm(stream, gain_rows[0], gain_rows[1]))
    stream = stream + attend(hidden, attn_w, segment, valid_row)
    hidden = low(layer_norm(stream, gain_rows[2], gain_rows[3]))
    inner_pre = low_back(high_dot(hidden, mlp_w[:, :FF]) + gain_rows[5:9].reshape(FF))
    active = low(gelu_tanh(inner_pre))
    return stream + low_back(high_dot(active, mlp_w[:, FF:].T) + gain_rows[4])

def lowered_params(params):
    attn_w, mlp_w, gain_all, edges, codes = params
    return (low(attn_w), low(mlp_w), low(gain_all), low(edges), normalize_rows(low(codes)))

def critic_logit(inputs, critic_parts):
    matrix, bias_row, readout = critic_parts
    pre_act = low_back(high_dot(inputs, matrix) + bias_row)
    return lax.optimization_barrier(jnp.sum(gelu_tanh(pre_act) * readout, axis=-1))

def encode_part(lowered, patch_row, segment, valid_row):
    attn_w, mlp_w, gain_all, edges, encoded = lowered
    stream = low_back(high_dot(patch_row, edges[:, :PIX].T))
    for layer_idx in range(LAYERS // 2):
        stream = block_apply(stream, attn_w[layer_idx], mlp_w[layer_idx], gain_all[layer_idx], segment, valid_row)
    latent = low_back(high_dot(low(stream), edges[:, 2 * PIX:2 * PIX + LAT]))
    return normalize_rows(latent)

def row_loss(lowered, critic_parts, patch_row, segment, valid_row, code_row, delta_row):
    attn_w, mlp_w, gain_all, edges, encoded = lowered
    valid_mask = valid_row.astype(jnp.float32)
    unit_latent = encode_part(lowered, patch_row, segment, valid_row)
    chosen = jnp.take(encoded, code_row, axis=0)
    commit_gap = unit_latent - chosen
    commit = jnp.sum(valid_mask * lax.optimization_barrier(jnp.sum(commit_gap * commit_gap, axis=-1)))
    stream = low_back(high_dot(low(unit_latent + delta_row), edges[:, 2 * PIX + LAT:2 * PIX + 2 * LAT].T))
    for layer_idx in range(LAYERS // 2, LAYERS):
        stream = block_apply(stream, attn_w[layer_idx], mlp_w[layer_idx], gain_all[layer_idx], segment, valid_row)
    normed = low(layer_norm(stream, edges[:, 2 * PIX + 2 * LAT], edges[:, 2 * PIX + 2 * LAT + 1]))
    rebuilt = low_back(high_dot(normed, edges[:, PIX:2 * PIX]))
    feat_diff = high_dot(rebuilt - patch_row, feature_table())
    feature = jnp.sum(valid_mask * lax.optimization_barrier(jnp.mean(feat_diff * feat_diff, axis=-1)))
    adverse = jnp.sum(valid_mask * jax.nn.softplus(-critic_logit(low(rebuilt), critic_parts)))
    return (feature + adverse_weight * adverse + commit_weight * commit, rebuilt)

def adam_update(weight, gradient, first_state, second_state):
    first_state = beta_one * first_state + (1.0 - beta_one) * gradient
    second_state = beta_two * second_state + (1.0 - beta_two) * gradient * gradient
    step_size = first_state / (1.0 - beta_one ** adam_step) / (jnp.sqrt(second_state / (1.0 - beta_two ** adam_step)) + adam_eps)
    return (weight - learn_rate * (step_size + decay_rate * weight), first_state, second_state)

def reference(patches, segments, validity, image_ids, code_ids, attn_weights, mlp_weights, layer_gains, edge_weights, codebook, critic_weights, attn_first, attn_second, mlp_first, mlp_second, gains_first, gains_second, edges_first, edges_second, codebook_first, codebook_second, critic_first, critic_second):
    patch_all = patches.astype(jnp.float32)
    critic_parts = (low(critic_weights[:PIX]), critic_weights[PIX], critic_weights[PIX + 1])
    params = (attn_weights, mlp_weights, layer_gains, edge_weights, codebook)
    fixed_params = lowered_params(params)

    def delta_row(inputs):
        patch_row, segment, valid_row, code_row = inputs
        unit_latent = encode_part(fixed_params, patch_row, segment, valid_row)
        return jnp.take(fixed_params[4], code_row, axis=0) - unit_latent
    delta_all = lax.map(delta_row, (patch_all, segments, validity, code_ids))

    def total_loss(params):
        lowered = lowered_params(params)

        def step_row(running, inputs):
            row_value, rebuilt = jax.checkpoint(row_loss)(lowered, critic_parts, *inputs)
            return (running + row_value, rebuilt)
        return lax.scan(step_row, jnp.zeros((), jnp.float32), (patch_all, segments, validity, code_ids, delta_all))
    gen_sum, pullback, rebuilt_all = jax.vjp(total_loss, params, has_aux=True)
    gen_grads, = pullback(jnp.ones((), jnp.float32))
    valid_mask = validity.astype(jnp.float32).reshape(-1)

    def critic_loss(critic):
        parts = (low(critic[:PIX]), critic[PIX], critic[PIX + 1])
        real_logits = critic_logit(patch_all.reshape(-1, PIX), parts)
        fake_logits = critic_logit(low(rebuilt_all.reshape(-1, PIX)), parts)
        return jnp.sum(valid_mask * (jax.nn.softplus(-real_logits) + jax.nn.softplus(fake_logits)))
    critic_sum, critic_pull = jax.vjp(critic_loss, critic_weights)
    critic_grad, = critic_pull(jnp.ones((), jnp.float32))
    change = jnp.concatenate([jnp.ones((image_ids.shape[0], 1), bool), image_ids[:, 1:] != image_ids[:, :-1]], axis=1)
    images = jnp.sum(jnp.where(change & (validity > 0), 1.0, 0.0).astype(jnp.float32))
    scaled = [gradient / images for gradient in gen_grads]
    grad_norm = jnp.sqrt(sum((jnp.sum(gradient * gradient) for gradient in scaled)))
    factor = jnp.minimum(1.0, clip_norm / grad_norm)
    new_attn = adam_update(attn_weights, scaled[0] * factor, attn_first, attn_second)
    new_mlp = adam_update(mlp_weights, scaled[1] * factor, mlp_first, mlp_second)
    new_gains = adam_update(layer_gains, scaled[2] * factor, gains_first, gains_second)
    new_edges = adam_update(edge_weights, scaled[3] * factor, edges_first, edges_second)
    new_codes = adam_update(codebook, scaled[4] * factor, codebook_first, codebook_second)
    new_critic = adam_update(critic_weights, critic_grad / images, critic_first, critic_second)
    losses = jnp.stack([gen_sum / images, critic_sum / images])
    return (new_attn[0], new_attn[1], new_attn[2], new_mlp[0], new_mlp[1], new_mlp[2], new_gains[0], new_gains[1], new_gains[2], new_edges[0], new_edges[1], new_edges[2], new_codes[0], new_codes[1], new_codes[2], new_critic[0], new_critic[1], new_critic[2], losses, grad_norm, new_attn[0].astype(jnp.bfloat16), new_mlp[0].astype(jnp.bfloat16), new_edges[0].astype(jnp.bfloat16), new_codes[0].astype(jnp.bfloat16))
```

```python
import functools
import math

import jax
import jax.numpy as jnp
from jax import lax
from jax.experimental import pallas as pl
from jax.experimental.pallas import tpu as pltpu
from jax.sharding import PartitionSpec as P

MESH = pl.DeviceIdType.MESH
D = 512
HEADS = 8
HEAD = 64
FF = 2048
LAT = 32
CODES = 8192
PIX = 192
LAYERS = 2


beta_one = 0.9
beta_two = 0.95
adam_eps = 1e-08
decay_rate = 0.1
learn_rate = 0.2
clip_norm = 0.5
commit_weight = 0.25
adverse_weight = 0.2
adam_step = 10.0
norm_eps = 1e-05
masked_score = -1000000000.0


def layer_norm(values, gain, shift):
    center = values - jnp.mean(values, axis=-1, keepdims=True)
    spread = jnp.mean(center * center, axis=-1, keepdims=True)
    return center * lax.rsqrt(spread + norm_eps) * gain + shift


def gelu_tanh(values):
    cubic_term = values + 0.044715 * values * values * values
    return 0.5 * values * (1.0 + jnp.tanh(0.7978845608028654 * cubic_term))


def normalize_rows(values):
    return values * lax.rsqrt(jnp.sum(values * values, axis=-1, keepdims=True) + 1.0)


def feature_table():
    pixel_idx = jnp.arange(PIX, dtype=jnp.float32)[:, None]
    frequency = jnp.arange(PIX, dtype=jnp.float32)[None, :]
    return jnp.cos(math.pi * (pixel_idx + 0.5) * frequency / PIX) * (
        math.sqrt(2.0 / PIX) / (1.0 + frequency / 16.0)
    )


def low_dot(left_side, right_side):
    return jnp.dot(left_side, right_side, preferred_element_type=jnp.float32)


def split_heads(mixed_qkv):
    length = mixed_qkv.shape[0]
    return (
        mixed_qkv[:, :D].reshape(length, HEADS, HEAD),
        mixed_qkv[:, D : 2 * D].reshape(length, HEADS, HEAD),
        mixed_qkv[:, 2 * D :].reshape(length, HEADS, HEAD),
    )


def block_mask(row_start, block_rows, segment, valid_row):
    rows_here = row_start + jnp.arange(block_rows)
    columns = jnp.arange(segment.shape[0])
    seg_rows = lax.dynamic_slice_in_dim(segment, row_start, block_rows)
    return (seg_rows[:, None] == segment[None, :]) & (
        (valid_row[None, :] > 0) | (rows_here[:, None] == columns[None, :])
    )


def head_scores(query_rows, keys_all, allowed):
    scores = jnp.einsum(
        "qhd,khd->hqk", query_rows, keys_all, preferred_element_type=jnp.float32
    ) * HEAD ** (-0.5)
    return jnp.where(allowed[None], scores, masked_score)


def attend_forward(queries, keys_all, values_all, segment, valid_row):
    length = queries.shape[0]
    block_rows = min(512, length)

    def one_block(block_idx):
        row_start = block_idx * block_rows
        query_rows = lax.dynamic_slice_in_dim(queries, row_start, block_rows)
        scores = head_scores(
            query_rows, keys_all, block_mask(row_start, block_rows, segment, valid_row)
        )
        row_peak = jnp.max(scores, axis=-1, keepdims=True)
        exp_scores = jnp.exp(scores - row_peak)
        totals = jnp.sum(exp_scores, axis=-1, keepdims=True)
        attn_probs = (exp_scores / totals).astype(jnp.bfloat16)
        context = jnp.einsum(
            "hqk,khd->qhd", attn_probs, values_all, preferred_element_type=jnp.float32
        )
        return (context.astype(jnp.bfloat16), (row_peak + jnp.log(totals))[:, :, 0])

    context, logsum = lax.map(one_block, jnp.arange(length // block_rows))
    return (context.reshape(length, D), logsum)


def attend_backward(queries, keys_all, values_all, logsum, grad_context, segment, valid_row):
    length = queries.shape[0]
    block_rows = min(512, length)
    scaling = HEAD ** (-0.5)

    def one_block(running, block_idx):
        grad_keys, grad_values = running
        row_start = block_idx * block_rows
        query_rows = lax.dynamic_slice_in_dim(queries, row_start, block_rows)
        grad_rows = lax.dynamic_slice_in_dim(grad_context, row_start, block_rows)
        scores = head_scores(
            query_rows, keys_all, block_mask(row_start, block_rows, segment, valid_row)
        )
        attn_probs = jnp.exp(scores - logsum[block_idx][:, :, None])
        grad_values = grad_values + jnp.einsum(
            "hqk,qhd->khd",
            attn_probs.astype(jnp.bfloat16),
            grad_rows,
            preferred_element_type=jnp.float32,
        )
        grad_probs = jnp.einsum(
            "qhd,khd->hqk", grad_rows, values_all, preferred_element_type=jnp.float32
        )
        grad_scores = (
            attn_probs * (grad_probs - jnp.sum(attn_probs * grad_probs, axis=-1, keepdims=True))
        ).astype(jnp.bfloat16)
        grad_query = (
            jnp.einsum("hqk,khd->qhd", grad_scores, keys_all, preferred_element_type=jnp.float32)
            * scaling
        )
        grad_keys = (
            grad_keys
            + jnp.einsum(
                "hqk,qhd->khd", grad_scores, query_rows, preferred_element_type=jnp.float32
            )
            * scaling
        )
        return ((grad_keys, grad_values), grad_query)

    empty = jnp.zeros((length, HEADS, HEAD), jnp.float32)
    (grad_keys, grad_values), grad_queries = lax.scan(
        one_block, (empty, empty), jnp.arange(length // block_rows)
    )
    return jnp.concatenate(
        [
            grad_queries.reshape(length, D),
            grad_keys.reshape(length, D),
            grad_values.reshape(length, D),
        ],
        axis=1,
    )


def layer_forward(stream, weights, segment, valid_row):
    attn_low, mlp_low, gains_low = weights
    gain_rows = gains_low.astype(jnp.float32)
    hidden = layer_norm(stream, gain_rows[0], gain_rows[1]).astype(jnp.bfloat16)
    mixed_qkv = low_dot(hidden, attn_low[:, : 3 * D]).astype(jnp.bfloat16)
    queries, keys_all, values_all = split_heads(mixed_qkv)
    context, logsum = attend_forward(queries, keys_all, values_all, segment, valid_row)
    middle = stream + low_dot(context, attn_low[:, 3 * D :])
    hidden_mlp = layer_norm(middle, gain_rows[2], gain_rows[3]).astype(jnp.bfloat16)
    inner_pre = low_dot(hidden_mlp, mlp_low[:, :FF]) + gain_rows[5:9].reshape(FF)
    active = gelu_tanh(inner_pre).astype(jnp.bfloat16)
    output = (
        middle
        + jnp.einsum("tf,df->td", active, mlp_low[:, FF:], preferred_element_type=jnp.float32)
        + gain_rows[4]
    )
    return (output, (stream, mixed_qkv, context, logsum, middle, inner_pre))


def layer_backward(saved, weights, grad_stream, segment, valid_row):
    stream, mixed_qkv, context, logsum, middle, inner_pre = saved
    attn_low, mlp_low, gains_low = weights
    gain_rows = gains_low.astype(jnp.float32)
    grad_branch = grad_stream.astype(jnp.bfloat16)
    active, slope_back = jax.vjp(gelu_tanh, inner_pre)
    active_low = active.astype(jnp.bfloat16)
    grad_down = jnp.einsum("td,tf->df", grad_branch, active_low, preferred_element_type=jnp.float32)
    grad_active = jnp.einsum(
        "td,df->tf", grad_branch, mlp_low[:, FF:], preferred_element_type=jnp.float32
    )
    (grad_inner,) = slope_back(grad_active)
    grad_inner_low = grad_inner.astype(jnp.bfloat16)
    normed_mlp, mlp_norm_back = jax.vjp(layer_norm, middle, gain_rows[2], gain_rows[3])
    hidden_mlp = normed_mlp.astype(jnp.bfloat16)
    grad_up = jnp.einsum(
        "td,tf->df", hidden_mlp, grad_inner_low, preferred_element_type=jnp.float32
    )
    grad_hidden = jnp.einsum(
        "tf,df->td", grad_inner_low, mlp_low[:, :FF], preferred_element_type=jnp.float32
    )
    grad_middle, grad_gain_two, grad_shift_two = mlp_norm_back(grad_hidden)
    grad_middle = grad_middle + grad_stream
    grad_attn_out = grad_middle.astype(jnp.bfloat16)
    grad_out_proj = jnp.einsum(
        "te,td->ed", context, grad_attn_out, preferred_element_type=jnp.float32
    )
    grad_context = jnp.einsum(
        "td,ed->te", grad_attn_out, attn_low[:, 3 * D :], preferred_element_type=jnp.float32
    ).astype(jnp.bfloat16)
    queries, keys_all, values_all = split_heads(mixed_qkv)
    grad_mixed = attend_backward(
        queries,
        keys_all,
        values_all,
        logsum,
        grad_context.reshape(-1, HEADS, HEAD),
        segment,
        valid_row,
    ).astype(jnp.bfloat16)
    normed_attn, attn_norm_back = jax.vjp(layer_norm, stream, gain_rows[0], gain_rows[1])
    hidden_attn = normed_attn.astype(jnp.bfloat16)
    grad_qkv = jnp.einsum("td,te->de", hidden_attn, grad_mixed, preferred_element_type=jnp.float32)
    grad_hidden_attn = jnp.einsum(
        "te,de->td", grad_mixed, attn_low[:, : 3 * D], preferred_element_type=jnp.float32
    )
    grad_input, grad_gain_one, grad_shift_one = attn_norm_back(grad_hidden_attn)
    grad_input = grad_input + grad_middle
    grad_attn = jnp.concatenate([grad_qkv, grad_out_proj], axis=1)
    grad_mlp = jnp.concatenate([grad_up, grad_down], axis=1)
    small_rows = jnp.stack(
        [
            grad_gain_one,
            grad_shift_one,
            grad_gain_two,
            grad_shift_two,
            jnp.sum(grad_branch.astype(jnp.float32), axis=0),
        ]
    )
    grad_gains = jnp.concatenate(
        [small_rows, jnp.sum(grad_inner_low.astype(jnp.float32), axis=0).reshape(4, D)], axis=0
    )
    return (grad_input, (grad_attn, grad_mlp, grad_gains))


def fetch_layer(attn_weights, mlp_weights, layer_gains, layer_idx):
    return (
        lax.all_gather(attn_weights[layer_idx].astype(jnp.bfloat16), "fsdp", axis=0, tiled=True),
        lax.all_gather(mlp_weights[layer_idx].astype(jnp.bfloat16), "fsdp", axis=0, tiled=True),
        lax.all_gather(layer_gains[layer_idx].astype(jnp.bfloat16), "fsdp", axis=1, tiled=True),
    )


def fetch_again(attn_weights, mlp_weights, layer_gains, layer_idx):
    return (
        lax.all_gather(attn_weights[layer_idx].astype(jnp.bfloat16), "fsdp", axis=0, tiled=True),
        lax.all_gather(mlp_weights[layer_idx].astype(jnp.bfloat16), "fsdp", axis=0, tiled=True),
        lax.all_gather(layer_gains[layer_idx].astype(jnp.bfloat16), "fsdp", axis=1, tiled=True),
    )


def adam_update(weight, gradient, first_state, second_state):
    first_state = beta_one * first_state + (1.0 - beta_one) * gradient
    second_state = beta_two * second_state + (1.0 - beta_two) * gradient * gradient
    step_size = (
        first_state
        / (1.0 - beta_one**adam_step)
        / (jnp.sqrt(second_state / (1.0 - beta_two**adam_step)) + adam_eps)
    )
    return (weight - learn_rate * (step_size + decay_rate * weight), first_state, second_state)


def add_parts(terms):
    total = terms[0].astype(jnp.float32)
    for term in terms[1:]:
        total = total + term.astype(jnp.float32)
    return total.astype(jnp.bfloat16)

def reduce_kernel(count, n_chip, n_dp, order, *refs):
    ins = refs[:count]
    outs = refs[count:2 * count]
    rest = refs[2 * count:]
    pair_in = rest[:count]
    sums = rest[count:2 * count]
    chip_in = rest[2 * count:3 * count]
    part = rest[3 * count:4 * count]
    copy_in = rest[4 * count:5 * count]
    (pair_send, pair_recv, local_sem, chip_send, chip_recv, rs_send, rs_recv, ag_send, ag_recv) = rest[5 * count:]
    place = lax.axis_index("fsdp")
    plane = lax.axis_index("dp")
    core = lax.rem(place, 2)
    chip = lax.div(place, 2)
    sibling = place + 1 - 2 * core
    barrier = pltpu.get_barrier_semaphore()
    pl.semaphore_signal(barrier, inc=1, device_id={"fsdp": sibling}, device_id_type=MESH)
    for j in range(1, n_chip):
        pl.semaphore_signal(barrier, inc=1, device_id={"fsdp": lax.rem(chip + j, n_chip) * 2 + core}, device_id_type=MESH)
    for t in range(1, n_dp):
        pl.semaphore_signal(barrier, inc=1, device_id={"dp": lax.rem(plane + t, n_dp)}, device_id_type=MESH)
    pl.semaphore_wait(barrier, n_chip + n_dp - 1)

    def pair_copy(a):
        return pltpu.make_async_remote_copy(
            src_ref=ins[a].at[:, 1 - core], dst_ref=pair_in[a], send_sem=pair_send.at[a], recv_sem=pair_recv.at[a],
            device_id={"fsdp": sibling}, device_id_type=MESH)

    def local_copy(a):
        return pltpu.make_async_copy(ins[a].at[:, core], sums[a], local_sem.at[a])

    def chip_copy(a, j):
        there = lax.rem(chip + j, n_chip)
        return pltpu.make_async_remote_copy(
            src_ref=sums[a].at[there], dst_ref=chip_in[a].at[j - 1], send_sem=chip_send.at[a, j - 1],
            recv_sem=chip_recv.at[a, j - 1], device_id={"fsdp": there * 2 + core}, device_id_type=MESH)

    def rs_copy(a, t):
        there = lax.rem(plane + t, n_dp)
        return pltpu.make_async_remote_copy(
            src_ref=part[a].at[there], dst_ref=copy_in[a].at[t - 1], send_sem=rs_send.at[a, t - 1],
            recv_sem=rs_recv.at[a, t - 1], device_id={"dp": there}, device_id_type=MESH)

    def ag_copy(a, t):
        there = lax.rem(plane + t, n_dp)
        return pltpu.make_async_remote_copy(
            src_ref=outs[a].at[plane], dst_ref=outs[a].at[plane], send_sem=ag_send.at[a, t - 1],
            recv_sem=ag_recv.at[a, t - 1], device_id={"dp": there}, device_id_type=MESH)

    for a in range(count):
        pair_copy(a).start()
        local_copy(a).start()

    def stage_a(a):
        pair_copy(a).wait()
        local_copy(a).wait()
        def body(i, carry):
            c, d = lax.div(i, n_dp), lax.rem(i, n_dp)
            sums[a][c, d] = add_parts([sums[a][c, d], pair_in[a][c, d]])
            return carry
        lax.fori_loop(0, n_chip * n_dp, body, 0)
        for j in range(1, n_chip):
            chip_copy(a, j).start()

    def stage_b(a):
        for j in range(1, n_chip):
            chip_copy(a, j).wait()
        def body(d, carry):
            part[a][d] = add_parts([sums[a][chip, d]] + [chip_in[a][j, d] for j in range(n_chip - 1)])
            return carry
        lax.fori_loop(0, n_dp, body, 0)
        for t in range(1, n_dp):
            rs_copy(a, t).start()

    def stage_c(a):
        for t in range(1, n_dp):
            rs_copy(a, t).wait()
        outs[a][plane] = add_parts([part[a][plane]] + [copy_in[a][t] for t in range(n_dp - 1)])
        for t in range(1, n_dp):
            ag_copy(a, t).start()

    def stage_d(a):
        for t in range(1, n_dp):
            ag_copy(a, t).wait()

    stages = (stage_a, stage_b, stage_c, stage_d)
    for step, a in order:
        stages[step](a)


def schedule(count):
    order = [(0, 0), (0, 1)]
    for turn in range(count + 2):
        for step in (1, 2, 3):
            if 0 <= turn - (step - 1) < count:
                order.append((step, turn - (step - 1)))
        if turn + 2 < count:
            order.append((0, turn + 2))
    return order


def reduce_all(arrays, n_chip, n_dp):
    count = len(arrays)
    tails = [a.shape[3:] for a in arrays]
    vm = lambda *s: pltpu.VMEM(s, jnp.bfloat16)
    scratch = ([vm(n_chip, n_dp, *t) for t in tails] + [vm(n_chip, n_dp, *t) for t in tails]
               + [vm(n_chip - 1, n_dp, *t) for t in tails] + [vm(n_dp, *t) for t in tails] + [vm(n_dp - 1, *t) for t in tails]
               + [pltpu.SemaphoreType.DMA((count,))] * 3 + [pltpu.SemaphoreType.DMA((count, n_chip - 1))] * 2
               + [pltpu.SemaphoreType.DMA((count, n_dp - 1))] * 4)
    return pl.pallas_call(
        functools.partial(reduce_kernel, count, n_chip, n_dp, schedule(count)),
        out_shape=[jax.ShapeDtypeStruct((n_dp,) + t, jnp.bfloat16) for t in tails],
        in_specs=[pl.BlockSpec(memory_space=pl.ANY)] * count,
        out_specs=[pl.BlockSpec(memory_space=pltpu.VMEM)] * count,
        scratch_shapes=scratch,
        compiler_params=pltpu.CompilerParams(collective_id=3, has_side_effects=True, vmem_limit_bytes=48 << 20),
    )(*arrays)


def split_owners(gradient, n_chip, n_dp):
    rows, columns = gradient.shape
    owned = rows // (2 * n_chip)
    if owned % (16 * n_dp) == 0:
        return gradient.reshape(n_chip, 2, n_dp, owned // n_dp, columns)
    if columns % (128 * n_dp) == 0:
        parts = gradient.reshape(n_chip, 2, owned, n_dp, columns // n_dp)
        return parts.transpose(0, 1, 3, 2, 4)
    return gradient.reshape(n_chip, 2, n_dp, owned // n_dp, columns)


def join_owned(parts, owned, columns):
    n_dp = parts.shape[0]
    if parts.shape[2] == columns:
        return parts.reshape(owned, columns)
    return parts.transpose(1, 0, 2).reshape(owned, columns)


def per_device(
    mesh,
    patches,
    segments,
    validity,
    image_ids,
    code_ids,
    attn_weights,
    mlp_weights,
    layer_gains,
    edge_weights,
    codebook,
    critic_weights,
    attn_first,
    attn_second,
    mlp_first,
    mlp_second,
    gains_first,
    gains_second,
    edges_first,
    edges_second,
    codebook_first,
    codebook_second,
    critic_first,
    critic_second,
):
    patch_low = patches[0]
    patch_row = patch_low.astype(jnp.float32)
    segment = segments[0]
    valid_row = validity[0]
    valid_mask = valid_row.astype(jnp.float32)
    code_row = code_ids[0]
    image_row = image_ids[0]
    half_layers = LAYERS // 2
    edges_all, codes_low = (
        lax.all_gather(edge_weights.astype(jnp.bfloat16), "fsdp", axis=0, tiled=True),
        lax.all_gather(codebook.astype(jnp.bfloat16), "fsdp", axis=0, tiled=True),
    )
    embed_in = edges_all[:, :PIX]
    head_out = edges_all[:, PIX : 2 * PIX]
    down_proj = edges_all[:, 2 * PIX : 2 * PIX + LAT]
    up_proj = edges_all[:, 2 * PIX + LAT : 2 * PIX + 2 * LAT]
    final_gain = edges_all[:, 2 * PIX + 2 * LAT].astype(jnp.float32)
    final_shift = edges_all[:, 2 * PIX + 2 * LAT + 1].astype(jnp.float32)
    critic_mat = critic_weights[:PIX].astype(jnp.bfloat16)
    critic_bias = critic_weights[PIX]
    readout = critic_weights[PIX + 1]
    stream = jnp.einsum("tp,dp->td", patch_low, embed_in, preferred_element_type=jnp.float32)
    kept_weights = []
    saved_all = []
    for layer_idx in range(LAYERS):
        if layer_idx == half_layers:
            encoder_low = stream.astype(jnp.bfloat16)
            latent = jnp.einsum(
                "td,dl->tl", encoder_low, down_proj, preferred_element_type=jnp.float32
            )
            unit_latent, unit_back = jax.vjp(normalize_rows, latent)
            encoded, encoded_back = jax.vjp(normalize_rows, codes_low.astype(jnp.float32))
            chosen = jnp.take(encoded, code_row, axis=0)
            commit_gap = unit_latent - chosen
            commit = jnp.sum(valid_mask * jnp.sum(commit_gap * commit_gap, axis=-1))
            quant_low = (unit_latent + (chosen - unit_latent)).astype(jnp.bfloat16)
            stream = jnp.einsum("tl,dl->td", quant_low, up_proj, preferred_element_type=jnp.float32)
        weights = fetch_layer(attn_weights, mlp_weights, layer_gains, layer_idx)
        kept_weights.append(weights)
        stream, saved = layer_forward(stream, weights, segment, valid_row)
        saved_all.append(saved)
    final_normed, final_back = jax.vjp(layer_norm, stream, final_gain, final_shift)
    final_low = final_normed.astype(jnp.bfloat16)
    rebuilt = jnp.einsum("td,dp->tp", final_low, head_out, preferred_element_type=jnp.float32)
    feat_table = feature_table()
    feat_diff = jnp.dot(
        rebuilt - patch_row,
        feat_table,
        precision=lax.Precision.HIGHEST,
        preferred_element_type=jnp.float32,
    )
    feature = jnp.sum(valid_mask * jnp.mean(feat_diff * feat_diff, axis=-1))
    rebuilt_low = rebuilt.astype(jnp.bfloat16)
    pre_fake = low_dot(rebuilt_low, critic_mat) + critic_bias
    act_fake, fake_back = jax.vjp(gelu_tanh, pre_fake)
    fake_logits = jnp.sum(act_fake * readout, axis=-1)
    adverse = jnp.sum(valid_mask * jax.nn.softplus(-fake_logits))
    gen_local = feature + adverse_weight * adverse + commit_weight * commit
    pre_real = low_dot(patch_low, critic_mat) + critic_bias
    act_real, real_back = jax.vjp(gelu_tanh, pre_real)
    real_logits = jnp.sum(act_real * readout, axis=-1)
    critic_local = jnp.sum(
        valid_mask * (jax.nn.softplus(-real_logits) + jax.nn.softplus(fake_logits))
    )
    change = jnp.concatenate([jnp.ones((1,), bool), image_row[1:] != image_row[:-1]])
    starts = jnp.sum(jnp.where(change & (valid_row > 0), 1.0, 0.0).astype(jnp.float32))
    images, gen_total, critic_total = lax.psum((starts, gen_local, critic_local), ("fsdp", "dp"))
    grad_feature = jnp.dot(
        valid_mask[:, None] * (2.0 / PIX) * feat_diff,
        feat_table.T,
        precision=lax.Precision.HIGHEST,
        preferred_element_type=jnp.float32,
    )
    grad_logits = -adverse_weight * valid_mask * jax.nn.sigmoid(-fake_logits)
    (grad_pre,) = fake_back(grad_logits[:, None] * readout)
    grad_pre_low = grad_pre.astype(jnp.bfloat16)
    grad_rebuilt = grad_feature + jnp.einsum(
        "th,ph->tp", grad_pre_low, critic_mat, preferred_element_type=jnp.float32
    )
    grad_rebuilt_low = grad_rebuilt.astype(jnp.bfloat16)
    grad_head = jnp.einsum(
        "td,tp->dp", final_low, grad_rebuilt_low, preferred_element_type=jnp.float32
    )
    grad_final = jnp.einsum(
        "tp,dp->td", grad_rebuilt_low, head_out, preferred_element_type=jnp.float32
    )
    grad_stream, grad_final_gain, grad_final_shift = final_back(grad_final)
    layer_parts = [None] * LAYERS
    for layer_idx in reversed(range(LAYERS)):
        weights = fetch_again(attn_weights, mlp_weights, layer_gains, layer_idx)
        grad_stream, layer_local = layer_backward(
            saved_all[layer_idx], weights, grad_stream, segment, valid_row
        )
        layer_parts[layer_idx] = layer_local
        if layer_idx == half_layers:
            grad_quant_low = grad_stream.astype(jnp.bfloat16)
            grad_upw = jnp.einsum(
                "tl,td->dl", quant_low, grad_quant_low, preferred_element_type=jnp.float32
            )
            grad_quant = jnp.einsum(
                "td,dl->tl", grad_quant_low, up_proj, preferred_element_type=jnp.float32
            )
            commit_grad = valid_mask[:, None] * (2.0 * commit_weight) * commit_gap
            (grad_latent,) = unit_back(grad_quant + commit_grad)
            grad_latent_low = grad_latent.astype(jnp.bfloat16)
            grad_downw = jnp.einsum(
                "td,tl->dl", encoder_low, grad_latent_low, preferred_element_type=jnp.float32
            )
            grad_stream = jnp.einsum(
                "tl,dl->td", grad_latent_low, down_proj, preferred_element_type=jnp.float32
            )
            grad_encoded = jax.ops.segment_sum(-commit_grad, code_row, num_segments=CODES)
            (grad_codes,) = encoded_back(grad_encoded)
    grad_embed_low = grad_stream.astype(jnp.bfloat16)
    grad_embed = jnp.einsum(
        "tp,td->dp", patch_low, grad_embed_low, preferred_element_type=jnp.float32
    )
    grad_edges = jnp.concatenate(
        [
            grad_embed,
            grad_head,
            grad_downw,
            grad_upw,
            grad_final_gain[:, None],
            grad_final_shift[:, None],
        ],
        axis=1,
    )
    n_chip, n_dp = mesh.shape["fsdp"] // 2, mesh.shape["dp"]
    gains_rows = jnp.concatenate([parts[2] for parts in layer_parts], axis=0).T
    width = 2 * PIX + 2 * LAT + 2
    extra = 512 - width - gains_rows.shape[1]
    edge_block = jnp.concatenate(
        [grad_edges, gains_rows, jnp.zeros((D, extra), jnp.float32)], axis=1
    ).astype(jnp.bfloat16)
    code_block = grad_codes.astype(jnp.bfloat16).reshape(-1, 128)
    blocks = []
    for layer_idx in reversed(range(LAYERS)):
        blocks += [layer_parts[layer_idx][0], layer_parts[layer_idx][1]]
    blocks += [edge_block, code_block]
    reduced_parts = reduce_all([split_owners(block.astype(jnp.bfloat16), n_chip, n_dp) for block in blocks], n_chip, n_dp)
    joined = [
        join_owned(parts, block.shape[0] // (2 * n_chip), block.shape[1]).astype(jnp.float32)
        for parts, block in zip(reduced_parts, blocks)
    ]
    edge_shard = joined[2 * LAYERS]
    reduced = (
        jnp.stack([joined[2 * (LAYERS - 1 - layer_idx)] for layer_idx in range(LAYERS)]),
        jnp.stack([joined[2 * (LAYERS - 1 - layer_idx) + 1] for layer_idx in range(LAYERS)]),
        edge_shard[:, width : width + gains_rows.shape[1]].T.reshape(LAYERS, 9, -1),
        edge_shard[:, :width],
        joined[2 * LAYERS + 1].reshape(-1, LAT),
    )
    gpr_low = real_back((-valid_mask * jax.nn.sigmoid(-real_logits))[:, None] * readout)[0].astype(
        jnp.bfloat16
    )
    gpf_low = fake_back((valid_mask * jax.nn.sigmoid(fake_logits))[:, None] * readout)[0].astype(
        jnp.bfloat16
    )
    grad_mat = jnp.einsum(
        "tp,th->ph", patch_low, gpr_low, preferred_element_type=jnp.float32
    ) + jnp.einsum("tp,th->ph", rebuilt_low, gpf_low, preferred_element_type=jnp.float32)
    grad_bias = jnp.sum(gpr_low.astype(jnp.float32), axis=0) + jnp.sum(
        gpf_low.astype(jnp.float32), axis=0
    )
    grad_readout = jnp.sum(
        (-valid_mask * jax.nn.sigmoid(-real_logits))[:, None] * act_real
        + (valid_mask * jax.nn.sigmoid(fake_logits))[:, None] * act_fake,
        axis=0,
    )
    critic_grad = lax.psum(
        jnp.concatenate([grad_mat, grad_bias[None], grad_readout[None]], axis=0), ("fsdp", "dp")
    )
    scaled = [gradient / images for gradient in reduced]
    local_square = sum((jnp.sum(gradient * gradient) for gradient in scaled))
    grad_norm = jnp.sqrt(lax.psum(local_square, "fsdp"))
    factor = jnp.minimum(1.0, clip_norm / grad_norm)
    new_attn = adam_update(attn_weights, scaled[0] * factor, attn_first, attn_second)
    new_mlp = adam_update(mlp_weights, scaled[1] * factor, mlp_first, mlp_second)
    new_gains = adam_update(layer_gains, scaled[2] * factor, gains_first, gains_second)
    new_edges = adam_update(edge_weights, scaled[3] * factor, edges_first, edges_second)
    new_codes = adam_update(codebook, scaled[4] * factor, codebook_first, codebook_second)
    new_critic = adam_update(critic_weights, critic_grad / images, critic_first, critic_second)
    losses = jnp.stack([gen_total / images, critic_total / images])
    return (
        new_attn[0],
        new_attn[1],
        new_attn[2],
        new_mlp[0],
        new_mlp[1],
        new_mlp[2],
        new_gains[0],
        new_gains[1],
        new_gains[2],
        new_edges[0],
        new_edges[1],
        new_edges[2],
        new_codes[0],
        new_codes[1],
        new_codes[2],
        new_critic[0],
        new_critic[1],
        new_critic[2],
        losses,
        grad_norm,
        new_attn[0].astype(jnp.bfloat16),
        new_mlp[0].astype(jnp.bfloat16),
        new_edges[0].astype(jnp.bfloat16),
        new_codes[0].astype(jnp.bfloat16),
    )


def solution(mesh):
    return jax.shard_map(
        functools.partial(per_device, mesh),
        mesh=mesh,
        in_specs=(
            P(("fsdp", "dp"), None, None),
            P(("fsdp", "dp"), None),
            P(("fsdp", "dp"), None),
            P(("fsdp", "dp"), None),
            P(("fsdp", "dp"), None),
            P(None, "fsdp", None),
            P(None, "fsdp", None),
            P(None, None, "fsdp"),
            P("fsdp", None),
            P("fsdp", None),
            P(),
            P(None, "fsdp", None),
            P(None, "fsdp", None),
            P(None, "fsdp", None),
            P(None, "fsdp", None),
            P(None, None, "fsdp"),
            P(None, None, "fsdp"),
            P("fsdp", None),
            P("fsdp", None),
            P("fsdp", None),
            P("fsdp", None),
            P(),
            P(),
        ),
        out_specs=(
            P(None, "fsdp", None),
            P(None, "fsdp", None),
            P(None, "fsdp", None),
            P(None, "fsdp", None),
            P(None, "fsdp", None),
            P(None, "fsdp", None),
            P(None, None, "fsdp"),
            P(None, None, "fsdp"),
            P(None, None, "fsdp"),
            P("fsdp", None),
            P("fsdp", None),
            P("fsdp", None),
            P("fsdp", None),
            P("fsdp", None),
            P("fsdp", None),
            P(),
            P(),
            P(),
            P(),
            P(),
            P(None, "fsdp", None),
            P(None, "fsdp", None),
            P("fsdp", None),
            P("fsdp", None),
        ),
        check_vma=False,
    )
```

```python
import functools
import math

import jax
import jax.numpy as jnp
from jax import lax
from jax.experimental import pallas as pl
from jax.experimental.pallas import tpu as pltpu
from jax.sharding import PartitionSpec as P

MESH = pl.DeviceIdType.MESH
D = 512
HEADS = 8
HEAD = 64
FF = 2048
LAT = 32
CODES = 8192
PIX = 192
LAYERS = 2
TILE = 256
REACH = 256
PAIRS = HEADS // 2
EDGE = 2 * PIX + 2 * LAT + 2
EDGE_WIDE = 512


beta_one = 0.9
beta_two = 0.95
adam_eps = 1e-08
decay_rate = 0.1
learn_rate = 0.2
clip_norm = 0.5
commit_weight = 0.25
adverse_weight = 0.2
adam_step = 10.0
norm_eps = 1e-05
excluded = -1e30
kernel_vmem = 58 << 20


def layer_norm(values, gain, shift):
    center = values - jnp.mean(values, axis=-1, keepdims=True)
    spread = jnp.mean(center * center, axis=-1, keepdims=True)
    return center * lax.rsqrt(spread + norm_eps) * gain + shift


def dot_nn(left_side, right_side):
    return lax.dot_general(left_side, right_side, (((1,), (0,)), ((), ())), preferred_element_type=jnp.float32)


def dot_nt(left_side, right_side):
    return lax.dot_general(left_side, right_side, (((1,), (1,)), ((), ())), preferred_element_type=jnp.float32)


def dot_tn(left_side, right_side):
    return lax.dot_general(left_side, right_side, (((0,), (0,)), ((), ())), preferred_element_type=jnp.float32)


def center_rows(values):
    center = values - jnp.mean(values, axis=-1, keepdims=True)
    spread = jnp.mean(center * center, axis=-1, keepdims=True)
    scale = lax.rsqrt(spread + norm_eps)
    return center * scale, scale


def norm_rows_back(grad, unit, scale, gain):
    grad_unit = grad * gain
    mean_grad = jnp.mean(grad_unit, axis=-1, keepdims=True)
    mean_along = jnp.mean(grad_unit * unit, axis=-1, keepdims=True)
    return scale * (grad_unit - mean_grad - unit * mean_along)


def gelu_tanh(values):
    cubic_term = values + 0.044715 * values * values * values
    return 0.5 * values * (1.0 + jnp.tanh(0.7978845608028654 * cubic_term))


def gelu_slope(values):
    square = values * values
    bend = jnp.tanh(0.7978845608028654 * values * (1.0 + 0.044715 * square))
    active = 0.5 * values * (1.0 + bend)
    slope = 0.5 * (1.0 + bend) + 0.5 * values * (1.0 - bend * bend) * (
        0.7978845608028654 * (1.0 + 3.0 * 0.044715 * square)
    )
    return active, slope


def key_window(tile_idx, length):
    start = tile_idx * TILE
    return max(0, start - REACH), min(length, start + TILE + REACH)


def rows_at(tile_idx):
    return pl.ds(pl.multiple_of(tile_idx * TILE, TILE), TILE)


def lane_half(array):
    return lax.broadcasted_iota(jnp.int32, array.shape, 1) < HEAD


def split_pair(array):
    low_half = lane_half(array)
    zero = jnp.zeros_like(array)
    return jnp.where(low_half, array, zero), jnp.where(low_half, zero, array)


def forward_kernel(
    stream, attn_low, mlp_low, gains, marks_row, marks_col, output, mixed, context, logsum, middle, bias, active
):
    length = stream.shape[0]
    tiles = length // TILE

    def mix_tile(t, carry):
        unit, _ = center_rows(stream[rows_at(t), :])
        hidden = (unit * gains[0:1, :] + gains[1:2, :]).astype(jnp.bfloat16)
        for part in range(3):
            columns = pl.ds(part * D, D)
            mixed[rows_at(t), columns] = dot_nn(hidden, attn_low[:, columns]).astype(jnp.bfloat16)
        return carry

    lax.fori_loop(0, tiles, mix_tile, 0)

    for t in range(tiles):
        first, last = key_window(t, length)
        span = last - first
        rows = pl.ds(t * TILE, TILE)
        window = pl.ds(first, span)
        row_place = t * TILE + lax.broadcasted_iota(jnp.int32, (TILE, span), 0)
        key_place = first + lax.broadcasted_iota(jnp.int32, (TILE, span), 1)
        allowed = (marks_col[rows, 0:1] == marks_row[1:2, window]) | (row_place == key_place)
        bias[:, 0:span] = jnp.where(allowed, 0.0, excluded)

        def pair_step(pair, sums):
            lanes = pl.ds(pl.multiple_of(pair * 128, 128), 128)
            key_lanes = pl.ds(pl.multiple_of(D + pair * 128, 128), 128)
            value_lanes = pl.ds(pl.multiple_of(2 * D + pair * 128, 128), 128)
            queries = split_pair(mixed[rows, lanes] * jnp.bfloat16(HEAD**-0.5))
            keys = mixed[window, key_lanes]
            values = split_pair(mixed[window, value_lanes])
            total = None
            lane_ids = lax.broadcasted_iota(jnp.int32, (TILE, 128), 1)
            for half in range(2):
                scores = dot_nt(queries[half], keys) + bias[:, 0:span]
                peak = jnp.max(scores, axis=-1, keepdims=True)
                powers = jnp.exp(scores - peak)
                weight = jnp.sum(powers, axis=-1, keepdims=True)
                probs = (powers * (1.0 / weight)).astype(jnp.bfloat16)
                part = dot_nn(probs, values[half])
                total = part if total is None else total + part
                sums = jnp.where(lane_ids == 2 * pair + half, peak + jnp.log(weight), sums)
            context[rows, lanes] = total.astype(jnp.bfloat16)
            return sums

        logsum[rows, :] = lax.fori_loop(0, PAIRS, pair_step, jnp.zeros((TILE, 128), jnp.float32))

    def mlp_tile(t, carry):
        rows = rows_at(t)
        mid = stream[rows, :] + dot_nn(context[rows, :], attn_low[:, 3 * D : 4 * D])
        middle[rows, :] = mid
        unit, _ = center_rows(mid)
        hidden = (unit * gains[2:3, :] + gains[3:4, :]).astype(jnp.bfloat16)
        for part in range(FF // D):
            columns = pl.ds(part * D, D)
            inner = dot_nn(hidden, mlp_low[:, columns]) + gains[5 + part : 6 + part, :]
            active[:, columns] = gelu_tanh(inner).astype(jnp.bfloat16)
        output[rows, :] = mid + dot_nt(active[...], mlp_low[:, FF:]) + gains[4:5, :]
        return carry

    lax.fori_loop(0, tiles, mlp_tile, 0)


def whole_vmem(count):
    return [pl.BlockSpec(memory_space=pltpu.VMEM)] * count


def layer_forward(stream, weights, marks):
    attn_low, mlp_low, gains = weights
    length = stream.shape[0]
    return pl.pallas_call(
        forward_kernel,
        out_shape=[
            jax.ShapeDtypeStruct((length, D), jnp.float32),
            jax.ShapeDtypeStruct((length, 3 * D), jnp.bfloat16),
            jax.ShapeDtypeStruct((length, D), jnp.bfloat16),
            jax.ShapeDtypeStruct((length, 128), jnp.float32),
            jax.ShapeDtypeStruct((length, D), jnp.float32),
        ],
        in_specs=whole_vmem(6),
        out_specs=whole_vmem(5),
        scratch_shapes=[pltpu.VMEM((TILE, TILE + 2 * REACH), jnp.float32), pltpu.VMEM((TILE, FF), jnp.bfloat16)],
        compiler_params=pltpu.CompilerParams(vmem_limit_bytes=kernel_vmem),
    )(stream, attn_low, mlp_low, gains, *marks)


def backward_kernel(
    stream, mixed, context, logsum, middle, attn_low, mlp_low, gains, marks_row, marks_col, grad_stream,
    grad_input, grad_attn, grad_mlp, grad_gains,
    branch, active, grad_inner, hidden_low, grad_out, grad_context, grad_mixed, bias, grad_keys, grad_values,
):
    length = stream.shape[0]
    tiles = length // TILE
    grad_gains[...] = jnp.zeros_like(grad_gains)

    def add_row(place, rows):
        grad_gains[place : place + 1, :] += jnp.sum(rows, axis=0, keepdims=True)

    def mlp_tile(t, carry):
        rows = rows_at(t)
        upper = grad_stream[rows, :]
        upper_low = upper.astype(jnp.bfloat16)
        branch[rows, :] = upper_low
        add_row(4, upper_low.astype(jnp.float32))
        unit, scale = center_rows(middle[rows, :])
        hidden = (unit * gains[2:3, :] + gains[3:4, :]).astype(jnp.bfloat16)
        hidden_low[rows, :] = hidden
        grad_hidden = jnp.zeros((TILE, D), jnp.float32)
        for part in range(FF // D):
            columns = pl.ds(part * D, D)
            inner = dot_nn(hidden, mlp_low[:, columns]) + gains[5 + part : 6 + part, :]
            act, slope = gelu_slope(inner)
            active[rows, columns] = act.astype(jnp.bfloat16)
            pre_grad = (dot_nn(upper_low, mlp_low[:, pl.ds(FF + part * D, D)]) * slope).astype(jnp.bfloat16)
            grad_inner[rows, columns] = pre_grad
            add_row(5 + part, pre_grad.astype(jnp.float32))
            grad_hidden = grad_hidden + dot_nt(pre_grad, mlp_low[:, columns])
        add_row(2, grad_hidden * unit)
        add_row(3, grad_hidden)
        grad_mid = norm_rows_back(grad_hidden, unit, scale, gains[2:3, :]) + upper
        grad_input[rows, :] = grad_mid
        mid_low = grad_mid.astype(jnp.bfloat16)
        grad_out[rows, :] = mid_low
        grad_context[rows, :] = dot_nt(mid_low, attn_low[:, 3 * D : 4 * D]).astype(jnp.bfloat16)
        return carry

    lax.fori_loop(0, tiles, mlp_tile, 0)

    for part in range(FF // D):
        columns = pl.ds(part * D, D)
        grad_mlp[:, columns] = dot_tn(hidden_low[...], grad_inner[:, columns]).astype(jnp.bfloat16)
        grad_mlp[:, pl.ds(FF + part * D, D)] = dot_tn(branch[...], active[:, columns]).astype(jnp.bfloat16)
    grad_attn[:, 3 * D : 4 * D] = dot_tn(context[...], grad_out[...]).astype(jnp.bfloat16)

    for t in range(tiles):
        first, last = key_window(t, length)
        span = last - first
        key_place = first + lax.broadcasted_iota(jnp.int32, (span, TILE), 0)
        row_place = t * TILE + lax.broadcasted_iota(jnp.int32, (span, TILE), 1)
        allowed = (marks_col[pl.ds(first, span), 1:2] == marks_row[0:1, pl.ds(t * TILE, TILE)]) | (row_place == key_place)
        bias[t, 0:span, :] = jnp.where(allowed, 0.0, excluded)
    sums_t = [logsum[pl.ds(t * TILE, TILE), :].T[0:8, :] for t in range(tiles)]

    def pair_step(pair, carry):
        lanes = pl.ds(pl.multiple_of(pair * 128, 128), 128)
        key_lanes = pl.ds(pl.multiple_of(D + pair * 128, 128), 128)
        value_lanes = pl.ds(pl.multiple_of(2 * D + pair * 128, 128), 128)
        grad_keys[...] = jnp.zeros_like(grad_keys)
        grad_values[...] = jnp.zeros_like(grad_values)
        for t in range(tiles):
            first, last = key_window(t, length)
            span = last - first
            rows = pl.ds(t * TILE, TILE)
            window = pl.ds(first, span)
            queries = split_pair(mixed[rows, lanes] * jnp.bfloat16(HEAD**-0.5))
            grads = split_pair(grad_context[rows, lanes])
            keys = mixed[window, key_lanes]
            values = mixed[window, value_lanes]
            key_halves = split_pair(keys)
            head_ids = lax.broadcasted_iota(jnp.int32, (8, TILE), 0)
            add_keys, add_values, add_queries = None, None, None
            for half in range(2):
                sums = jnp.sum(jnp.where(head_ids == 2 * pair + half, sums_t[t], 0.0), axis=0, keepdims=True)
                probs = jnp.exp(dot_nt(keys, queries[half]) + bias[t, 0:span, :] - sums)
                grad_probs = dot_nt(values, grads[half])
                weighted = probs * grad_probs
                grad_scores = (weighted - probs * jnp.sum(weighted, axis=0, keepdims=True)).astype(jnp.bfloat16)
                to_keys = dot_nn(grad_scores, queries[half])
                to_values = dot_nn(probs.astype(jnp.bfloat16), grads[half])
                to_queries = dot_tn(grad_scores, key_halves[half])
                if half == 0:
                    add_keys, add_values, add_queries = to_keys, to_values, to_queries
                else:
                    add_keys, add_values, add_queries = add_keys + to_keys, add_values + to_values, add_queries + to_queries
            grad_keys[window, :] += add_keys
            grad_values[window, :] += add_values
            grad_mixed[rows, lanes] = (add_queries * HEAD**-0.5).astype(jnp.bfloat16)
        grad_mixed[:, key_lanes] = grad_keys[...].astype(jnp.bfloat16)
        grad_mixed[:, value_lanes] = grad_values[...].astype(jnp.bfloat16)
        return carry

    lax.fori_loop(0, PAIRS, pair_step, 0)

    def input_tile(t, carry):
        rows = rows_at(t)
        unit, scale = center_rows(stream[rows, :])
        hidden_low[rows, :] = (unit * gains[0:1, :] + gains[1:2, :]).astype(jnp.bfloat16)
        grad_hidden = dot_nt(grad_mixed[rows, :], attn_low[:, 0 : 3 * D])
        add_row(0, grad_hidden * unit)
        add_row(1, grad_hidden)
        grad_input[rows, :] += norm_rows_back(grad_hidden, unit, scale, gains[0:1, :])
        return carry

    lax.fori_loop(0, tiles, input_tile, 0)
    for part in range(3):
        columns = pl.ds(part * D, D)
        grad_attn[:, columns] = dot_tn(hidden_low[...], grad_mixed[:, columns]).astype(jnp.bfloat16)


def layer_backward(saved, weights, grad_stream, marks):
    stream, mixed, context, logsum, middle = saved
    attn_low, mlp_low, gains = weights
    length = stream.shape[0]
    low = lambda *shape: pltpu.VMEM(shape, jnp.bfloat16)
    return pl.pallas_call(
        backward_kernel,
        out_shape=[
            jax.ShapeDtypeStruct((length, D), jnp.float32),
            jax.ShapeDtypeStruct((D, 4 * D), jnp.bfloat16),
            jax.ShapeDtypeStruct((D, 2 * FF), jnp.bfloat16),
            jax.ShapeDtypeStruct((16, D), jnp.float32),
        ],
        in_specs=whole_vmem(11),
        out_specs=whole_vmem(4),
        scratch_shapes=[
            low(length, D), low(length, FF), low(length, FF), low(length, D), low(length, D), low(length, D),
            low(length, 3 * D), pltpu.VMEM((length // TILE, TILE + 2 * REACH, TILE), jnp.float32),
            pltpu.VMEM((length, 128), jnp.float32), pltpu.VMEM((length, 128), jnp.float32),
        ],
        compiler_params=pltpu.CompilerParams(vmem_limit_bytes=kernel_vmem),
    )(stream, mixed, context, logsum, middle, attn_low, mlp_low, gains, *marks, grad_stream)


def normalize_rows(values):
    return values * lax.rsqrt(jnp.sum(values * values, axis=-1, keepdims=True) + 1.0)


def feature_table():
    pixel_idx = jnp.arange(PIX, dtype=jnp.float32)[:, None]
    frequency = jnp.arange(PIX, dtype=jnp.float32)[None, :]
    return jnp.cos(math.pi * (pixel_idx + 0.5) * frequency / PIX) * (
        math.sqrt(2.0 / PIX) / (1.0 + frequency / 16.0)
    )


def low_dot(left_side, right_side):
    return jnp.dot(left_side, right_side, preferred_element_type=jnp.float32)


def add_parts(terms, kind=jnp.bfloat16):
    total = terms[0].astype(jnp.float32)
    for term in terms[1:]:
        total = total + term.astype(jnp.float32)
    return total.astype(kind)


def gather_kernel(count, n_chip, *refs):
    shards, outs = refs[:count], refs[count : 2 * count]
    local_sem, chip_send, chip_recv, pair_send, pair_recv = refs[2 * count :]
    place = lax.axis_index("fsdp")
    core = lax.rem(place, 2)
    chip = lax.div(place, 2)
    sibling = place + 1 - 2 * core
    barrier = pltpu.get_barrier_semaphore()
    pl.semaphore_signal(barrier, inc=1, device_id={"fsdp": sibling}, device_id_type=MESH)
    for j in range(1, n_chip):
        there = lax.rem(chip + j, n_chip) * 2 + core
        pl.semaphore_signal(barrier, inc=1, device_id={"fsdp": there}, device_id_type=MESH)
    pl.semaphore_wait(barrier, n_chip)

    def local_copy(a):
        return pltpu.make_async_copy(shards[a], outs[a].at[chip, core], local_sem.at[a])

    def chip_copy(a, j):
        return pltpu.make_async_remote_copy(
            src_ref=shards[a],
            dst_ref=outs[a].at[chip, core],
            send_sem=chip_send.at[a, j - 1],
            recv_sem=chip_recv.at[a, j - 1],
            device_id={"fsdp": lax.rem(chip + j, n_chip) * 2 + core},
            device_id_type=MESH,
        )

    def pair_copy(a, j):
        owner = lax.rem(chip + n_chip - j, n_chip)
        return pltpu.make_async_remote_copy(
            src_ref=shards[a] if j == 0 else outs[a].at[owner, core],
            dst_ref=outs[a].at[owner, core],
            send_sem=pair_send.at[a, j],
            recv_sem=pair_recv.at[a, j],
            device_id={"fsdp": sibling},
            device_id_type=MESH,
        )

    for a in range(count):
        for j in range(1, n_chip):
            chip_copy(a, j).start()
        pair_copy(a, 0).start()
        local_copy(a).start()
    for a in range(count):
        for j in range(1, n_chip):
            chip_copy(a, j).wait_recv()
            pair_copy(a, j).start()
    for a in range(count):
        local_copy(a).wait()
        for j in range(n_chip):
            pair_copy(a, j).wait()
            if j > 0:
                chip_copy(a, j).wait_send()


def gather_all(shards, n_chip, collective_id):
    count = len(shards)
    dma = pltpu.SemaphoreType.DMA
    gathered = pl.pallas_call(
        functools.partial(gather_kernel, count, n_chip),
        out_shape=[jax.ShapeDtypeStruct((n_chip, 2) + s.shape, s.dtype) for s in shards],
        in_specs=[pl.BlockSpec(memory_space=pl.ANY)] * count,
        out_specs=[pl.BlockSpec(memory_space=pl.ANY)] * count,
        scratch_shapes=[dma((count,))] + [dma((count, n_chip - 1))] * 2 + [dma((count, n_chip))] * 2,
        compiler_params=pltpu.CompilerParams(collective_id=collective_id, has_side_effects=True),
    )(*shards)
    return [g.reshape((-1,) + s.shape[1:]) for g, s in zip(gathered, shards)]


def reduce_kernel(count, n_chip, n_dp, *refs):
    ins, totals = refs[:count], refs[count : 2 * count - 1]
    critic_out, norm_out = refs[2 * count - 1 : 2 * count + 1]
    rest = refs[2 * count + 1 :]
    pair_in, sums, chip_in, part, copy_in = (rest[i * count : (i + 1) * count] for i in range(5))
    outs = totals + (rest[5 * count],)
    norm_mine, norm_dp, norm_fsdp = rest[5 * count + 1 : 5 * count + 4]
    (pair_send, pair_recv, local_sem, chip_send, chip_recv, rs_send, rs_recv, ag_send, ag_recv) = rest[
        5 * count + 4 : 5 * count + 13
    ]
    spread_send, spread_recv, mirror_send, mirror_recv, n1_send, n1_recv, n2_send, n2_recv = rest[5 * count + 13 :]
    place = lax.axis_index("fsdp")
    plane = lax.axis_index("dp")
    core = lax.rem(place, 2)
    chip = lax.div(place, 2)
    n_place = 2 * n_chip
    sibling = place + 1 - 2 * core
    last = count - 1
    barrier = pltpu.get_barrier_semaphore()
    for j in range(1, n_place):
        there = lax.rem(place + j, n_place)
        pl.semaphore_signal(barrier, inc=1, device_id={"fsdp": there}, device_id_type=MESH)
    for t in range(1, n_dp):
        there = lax.rem(plane + t, n_dp)
        pl.semaphore_signal(barrier, inc=1, device_id={"dp": there}, device_id_type=MESH)
    pl.semaphore_wait(barrier, n_place + n_dp - 2)

    def remote(source, target, send, recv, device):
        return pltpu.make_async_remote_copy(
            src_ref=source, dst_ref=target, send_sem=send, recv_sem=recv, device_id=device, device_id_type=MESH
        )

    def pair_copy(a):
        return remote(ins[a].at[:, 1 - core], pair_in[a], pair_send.at[a], pair_recv.at[a], {"fsdp": sibling})

    def local_copy(a):
        return pltpu.make_async_copy(ins[a].at[:, core], sums[a], local_sem.at[a])

    def chip_copy(a, j):
        there = lax.rem(chip + j, n_chip)
        return remote(
            sums[a].at[there],
            chip_in[a].at[j - 1],
            chip_send.at[a, j - 1],
            chip_recv.at[a, j - 1],
            {"fsdp": there * 2 + core},
        )

    def rs_copy(a, t):
        there = lax.rem(plane + t, n_dp)
        return remote(
            part[a].at[there], copy_in[a].at[t - 1], rs_send.at[a, t - 1], rs_recv.at[a, t - 1], {"dp": there}
        )

    def ag_copy(a, t):
        there = lax.rem(plane + t, n_dp)
        return remote(
            outs[a].at[plane], outs[a].at[plane], ag_send.at[a, t - 1], ag_recv.at[a, t - 1], {"dp": there}
        )

    def spread_copy(j):
        there = lax.rem(chip + j, n_chip)
        return remote(
            outs[last],
            critic_out.at[chip, core],
            spread_send.at[j - 1],
            spread_recv.at[j - 1],
            {"fsdp": there * 2 + core},
        )

    def mirror_copy():
        return remote(critic_out.at[:, core], critic_out.at[:, core], mirror_send, mirror_recv, {"fsdp": sibling})

    def norm_dp_copy(t):
        there = lax.rem(plane + t, n_dp)
        return remote(norm_mine, norm_dp.at[t - 1], n1_send.at[t - 1], n1_recv.at[t - 1], {"dp": there})

    def norm_fsdp_copy(j):
        there = lax.rem(place + j, n_place)
        return remote(norm_out, norm_fsdp.at[j - 1], n2_send.at[j - 1], n2_recv.at[j - 1], {"fsdp": there})

    def start_pair(a):
        pair_copy(a).start()
        local_copy(a).start()

    def stage_pair(a):
        pair_copy(a).wait()
        local_copy(a).wait()

        def body(i, carry):
            c, d = lax.div(i, n_dp), lax.rem(i, n_dp)
            sums[a][c, d] = add_parts([sums[a][c, d], pair_in[a][c, d]], ins[a].dtype)
            return carry

        lax.fori_loop(0, n_chip * n_dp, body, 0)
        for j in range(1, n_chip):
            chip_copy(a, j).start()

    def stage_chip(a):
        for j in range(1, n_chip):
            chip_copy(a, j).wait()

        def body(d, carry):
            terms = [sums[a][chip, d]] + [chip_in[a][j, d] for j in range(n_chip - 1)]
            part[a][d] = add_parts(terms, ins[a].dtype)
            return carry

        lax.fori_loop(0, n_dp, body, 0)
        for t in range(1, n_dp):
            rs_copy(a, t).start()

    def stage_dp(a):
        for t in range(1, n_dp):
            rs_copy(a, t).wait()
        total = add_parts([part[a][plane]] + [copy_in[a][t] for t in range(n_dp - 1)], ins[a].dtype)
        outs[a][plane] = total
        for t in range(1, n_dp):
            ag_copy(a, t).start()
        if a != last:
            square = total.astype(jnp.float32) * total.astype(jnp.float32)
            norm_mine[0:1, :] += jnp.sum(jnp.sum(square, axis=0, keepdims=True), axis=1, keepdims=True)

    def stage_end(a):
        for t in range(1, n_dp):
            ag_copy(a, t).wait()
        if a == last:
            critic_out[chip, core] = outs[last][...]
            for j in range(1, n_chip):
                spread_copy(j).start()

    norm_mine[...] = jnp.zeros_like(norm_mine)
    sequence = [last] + list(range(last))
    start_pair(sequence[0])
    start_pair(sequence[1])
    for turn in range(count + 2):
        for depth, stage in enumerate((stage_pair, stage_chip, stage_dp)):
            if 0 <= turn - depth < count:
                stage(sequence[turn - depth])
                if depth == 0 and turn + 2 < count:
                    start_pair(sequence[turn + 2])
        if turn == 4:
            stage_end(last)
    for t in range(1, n_dp):
        norm_dp_copy(t).start()
    for j in range(1, n_chip):
        spread_copy(j).wait()
    mirror_copy().start()
    for t in range(1, n_dp):
        norm_dp_copy(t).wait()
    norm_out[...] = norm_mine[...]
    for t in range(n_dp - 1):
        norm_out[...] += norm_dp[t]
    for j in range(1, n_place):
        norm_fsdp_copy(j).start()
    for a in range(last):
        stage_end(a)
    mirror_copy().wait()
    for j in range(1, n_place):
        norm_fsdp_copy(j).wait()
    total = norm_out[...]
    for j in range(n_place - 1):
        total = total + norm_fsdp[j]
    norm_out[...] = total


def split_owners(gradient, n_chip, n_dp):
    rows, columns = gradient.shape
    owned = rows // (2 * n_chip)
    if owned % (16 * n_dp) == 0:
        return gradient.reshape(n_chip, 2, n_dp, owned // n_dp, columns)
    if columns % (128 * n_dp) == 0:
        parts = gradient.reshape(n_chip, 2, owned, n_dp, columns // n_dp)
        return parts.transpose(0, 1, 3, 2, 4)
    return gradient.reshape(n_chip, 2, n_dp, owned // n_dp, columns)


def join_owned(parts, owned, columns):
    if parts.shape[2] == columns:
        return parts.reshape(owned, columns)
    return parts.transpose(1, 0, 2).reshape(owned, columns)


def reduce_all(blocks, critic_block, n_chip, n_dp, collective_id):
    rows = critic_block.shape[0]
    share = -(-rows // (2 * n_chip * n_dp))
    critic_parts = jnp.pad(critic_block, ((0, share * 2 * n_chip * n_dp - rows), (0, 0)))
    critic_parts = critic_parts.reshape(n_chip, 2, n_dp, share, -1)
    arrays = [split_owners(block, n_chip, n_dp) for block in blocks] + [critic_parts]
    count = len(arrays)
    tails = [a.shape[3:] for a in arrays]
    kinds = [a.dtype for a in arrays]
    dma = pltpu.SemaphoreType.DMA
    scratch = [pltpu.VMEM((n_chip, n_dp) + t, k) for t, k in zip(tails, kinds)] * 2
    scratch += [pltpu.VMEM((n_chip - 1, n_dp) + t, k) for t, k in zip(tails, kinds)]
    scratch += [pltpu.VMEM((n_dp,) + t, k) for t, k in zip(tails, kinds)]
    scratch += [pltpu.VMEM((n_dp - 1,) + t, k) for t, k in zip(tails, kinds)]
    scratch += [pltpu.VMEM((n_dp,) + tails[-1], kinds[-1])]
    scratch += [pltpu.VMEM((8, 128), jnp.float32)]
    scratch += [pltpu.VMEM((n_dp - 1, 8, 128), jnp.float32), pltpu.VMEM((2 * n_chip - 1, 8, 128), jnp.float32)]
    scratch += [dma((count,))] * 3 + [dma((count, n_chip - 1))] * 2 + [dma((count, n_dp - 1))] * 4
    scratch += [dma((n_chip - 1,))] * 2 + [dma(())] * 2 + [dma((n_dp - 1,))] * 2 + [dma((2 * n_chip - 1,))] * 2
    results = pl.pallas_call(
        functools.partial(reduce_kernel, count, n_chip, n_dp),
        out_shape=[jax.ShapeDtypeStruct((n_dp,) + t, k) for t, k in zip(tails[:-1], kinds)]
        + [
            jax.ShapeDtypeStruct((n_chip, 2, n_dp) + tails[-1], jnp.float32),
            jax.ShapeDtypeStruct((8, 128), jnp.float32),
        ],
        in_specs=[pl.BlockSpec(memory_space=pl.ANY)] * count,
        out_specs=[pl.BlockSpec(memory_space=pltpu.VMEM)] * (count + 1),
        scratch_shapes=scratch,
        compiler_params=pltpu.CompilerParams(
            collective_id=collective_id, has_side_effects=True, vmem_limit_bytes=kernel_vmem
        ),
    )(*arrays)
    shards = [
        join_owned(parts, block.shape[0] // (2 * n_chip), block.shape[1]).astype(jnp.float32)
        for parts, block in zip(results, blocks)
    ]
    critic_total = results[count - 1].reshape(-1, critic_block.shape[1])[:rows]
    return shards, critic_total, results[count][0, 0]


def adam_update(weight, gradient, first_state, second_state):
    first_state = beta_one * first_state + (1.0 - beta_one) * gradient
    second_state = beta_two * second_state + (1.0 - beta_two) * gradient * gradient
    step_size = (
        first_state
        / (1.0 - beta_one**adam_step)
        / (jnp.sqrt(second_state / (1.0 - beta_two**adam_step)) + adam_eps)
    )
    return (weight - learn_rate * (step_size + decay_rate * weight), first_state, second_state)


def per_device(
    mesh,
    patches,
    segments,
    validity,
    image_ids,
    code_ids,
    attn_weights,
    mlp_weights,
    layer_gains,
    edge_weights,
    codebook,
    critic_weights,
    attn_first,
    attn_second,
    mlp_first,
    mlp_second,
    gains_first,
    gains_second,
    edges_first,
    edges_second,
    codebook_first,
    codebook_second,
    critic_first,
    critic_second,
):
    patch_low = patches[0]
    patch_row = patch_low.astype(jnp.float32)
    segment = segments[0]
    valid_row = validity[0]
    valid_mask = valid_row.astype(jnp.float32)
    code_row = code_ids[0]
    image_row = image_ids[0]
    half_layers = LAYERS // 2
    n_chip, n_dp = mesh.shape["fsdp"] // 2, mesh.shape["dp"]
    owned = edge_weights.shape[0]
    gain_count = LAYERS * 9
    edge_shard = jnp.concatenate(
        [
            edge_weights,
            layer_gains.reshape(gain_count, owned).T,
            jnp.zeros((owned, EDGE_WIDE - EDGE - gain_count), jnp.float32),
        ],
        axis=1,
    )
    shards = [edge_shard, codebook.reshape(-1, 128)]
    for layer_idx in range(LAYERS):
        shards += [attn_weights[layer_idx], mlp_weights[layer_idx]]
    edges_all, codes_low, *layer_weights = gather_all(
        [shard.astype(jnp.bfloat16) for shard in shards], n_chip, 1
    )
    codes_low = codes_low.reshape(CODES, LAT)
    gains_all = edges_all[:, EDGE : EDGE + gain_count].T.reshape(LAYERS, 9, D).astype(jnp.float32)
    key_marks = jnp.stack([segment, jnp.where(valid_row > 0, segment, -1)])
    marks = (jnp.pad(key_marks, ((0, 6), (0, 0))), jnp.pad(key_marks.T, ((0, 0), (0, 126))))
    embed_in = edges_all[:, :PIX]
    head_out = edges_all[:, PIX : 2 * PIX]
    down_proj = edges_all[:, 2 * PIX : 2 * PIX + LAT]
    up_proj = edges_all[:, 2 * PIX + LAT : 2 * PIX + 2 * LAT]
    final_gain = edges_all[:, 2 * PIX + 2 * LAT].astype(jnp.float32)
    final_shift = edges_all[:, 2 * PIX + 2 * LAT + 1].astype(jnp.float32)
    critic_mat = critic_weights[:PIX].astype(jnp.bfloat16)
    critic_bias = critic_weights[PIX]
    readout = critic_weights[PIX + 1]
    stream = jnp.einsum("tp,dp->td", patch_low, embed_in, preferred_element_type=jnp.float32)
    kept_weights = []
    saved_all = []
    for layer_idx in range(LAYERS):
        if layer_idx == half_layers:
            encoder_low = stream.astype(jnp.bfloat16)
            latent = jnp.einsum(
                "td,dl->tl", encoder_low, down_proj, preferred_element_type=jnp.float32
            )
            unit_latent, unit_back = jax.vjp(normalize_rows, latent)
            encoded, encoded_back = jax.vjp(normalize_rows, codes_low.astype(jnp.float32))
            chosen = jnp.take(encoded, code_row, axis=0)
            commit_gap = unit_latent - chosen
            commit = jnp.sum(valid_mask * jnp.sum(commit_gap * commit_gap, axis=-1))
            quant_low = (unit_latent + (chosen - unit_latent)).astype(jnp.bfloat16)
            stream = jnp.einsum("tl,dl->td", quant_low, up_proj, preferred_element_type=jnp.float32)
        weights = (layer_weights[2 * layer_idx], layer_weights[2 * layer_idx + 1], gains_all[layer_idx])
        kept_weights.append(weights)
        block_input = stream
        stream, *saved = layer_forward(stream, weights, marks)
        saved_all.append((block_input, *saved))
    final_normed, final_back = jax.vjp(layer_norm, stream, final_gain, final_shift)
    final_low = final_normed.astype(jnp.bfloat16)
    rebuilt = jnp.einsum("td,dp->tp", final_low, head_out, preferred_element_type=jnp.float32)
    feat_table = feature_table()
    feat_diff = jnp.dot(
        rebuilt - patch_row,
        feat_table,
        precision=lax.Precision.HIGHEST,
        preferred_element_type=jnp.float32,
    )
    feature = jnp.sum(valid_mask * jnp.mean(feat_diff * feat_diff, axis=-1))
    rebuilt_low = rebuilt.astype(jnp.bfloat16)
    pre_fake = low_dot(rebuilt_low, critic_mat) + critic_bias
    act_fake, fake_back = jax.vjp(gelu_tanh, pre_fake)
    fake_logits = jnp.sum(act_fake * readout, axis=-1)
    adverse = jnp.sum(valid_mask * jax.nn.softplus(-fake_logits))
    gen_local = feature + adverse_weight * adverse + commit_weight * commit
    pre_real = low_dot(patch_low, critic_mat) + critic_bias
    act_real, real_back = jax.vjp(gelu_tanh, pre_real)
    real_logits = jnp.sum(act_real * readout, axis=-1)
    critic_local = jnp.sum(
        valid_mask * (jax.nn.softplus(-real_logits) + jax.nn.softplus(fake_logits))
    )
    change = jnp.concatenate([jnp.ones((1,), bool), image_row[1:] != image_row[:-1]])
    starts = jnp.sum(jnp.where(change & (valid_row > 0), 1.0, 0.0).astype(jnp.float32))
    grad_feature = jnp.dot(
        valid_mask[:, None] * (2.0 / PIX) * feat_diff,
        feat_table.T,
        precision=lax.Precision.HIGHEST,
        preferred_element_type=jnp.float32,
    )
    grad_logits = -adverse_weight * valid_mask * jax.nn.sigmoid(-fake_logits)
    (grad_pre,) = fake_back(grad_logits[:, None] * readout)
    grad_pre_low = grad_pre.astype(jnp.bfloat16)
    grad_rebuilt = grad_feature + jnp.einsum(
        "th,ph->tp", grad_pre_low, critic_mat, preferred_element_type=jnp.float32
    )
    grad_rebuilt_low = grad_rebuilt.astype(jnp.bfloat16)
    grad_head = jnp.einsum(
        "td,tp->dp", final_low, grad_rebuilt_low, preferred_element_type=jnp.float32
    )
    grad_final = jnp.einsum(
        "tp,dp->td", grad_rebuilt_low, head_out, preferred_element_type=jnp.float32
    )
    grad_stream, grad_final_gain, grad_final_shift = final_back(grad_final)
    layer_parts = [None] * LAYERS
    for layer_idx in reversed(range(LAYERS)):
        grad_stream, *layer_parts[layer_idx] = layer_backward(
            saved_all[layer_idx], kept_weights[layer_idx], grad_stream, marks
        )
        if layer_idx == half_layers:
            grad_quant_low = grad_stream.astype(jnp.bfloat16)
            grad_upw = jnp.einsum(
                "tl,td->dl", quant_low, grad_quant_low, preferred_element_type=jnp.float32
            )
            grad_quant = jnp.einsum(
                "td,dl->tl", grad_quant_low, up_proj, preferred_element_type=jnp.float32
            )
            commit_grad = valid_mask[:, None] * (2.0 * commit_weight) * commit_gap
            (grad_latent,) = unit_back(grad_quant + commit_grad)
            grad_latent_low = grad_latent.astype(jnp.bfloat16)
            grad_downw = jnp.einsum(
                "td,tl->dl", encoder_low, grad_latent_low, preferred_element_type=jnp.float32
            )
            grad_stream = jnp.einsum(
                "tl,dl->td", grad_latent_low, down_proj, preferred_element_type=jnp.float32
            )
            grad_encoded = jax.ops.segment_sum(-commit_grad, code_row, num_segments=CODES)
            (grad_codes,) = encoded_back(grad_encoded)
    grad_embed_low = grad_stream.astype(jnp.bfloat16)
    grad_embed = jnp.einsum(
        "tp,td->dp", patch_low, grad_embed_low, preferred_element_type=jnp.float32
    )
    grad_edges = jnp.concatenate(
        [
            grad_embed,
            grad_head,
            grad_downw,
            grad_upw,
            grad_final_gain[:, None],
            grad_final_shift[:, None],
        ],
        axis=1,
    )
    gpr_low = real_back((-valid_mask * jax.nn.sigmoid(-real_logits))[:, None] * readout)[0].astype(
        jnp.bfloat16
    )
    gpf_low = fake_back((valid_mask * jax.nn.sigmoid(fake_logits))[:, None] * readout)[0].astype(
        jnp.bfloat16
    )
    grad_mat = jnp.einsum(
        "tp,th->ph", patch_low, gpr_low, preferred_element_type=jnp.float32
    ) + jnp.einsum("tp,th->ph", rebuilt_low, gpf_low, preferred_element_type=jnp.float32)
    grad_bias = jnp.sum(gpr_low.astype(jnp.float32), axis=0) + jnp.sum(
        gpf_low.astype(jnp.float32), axis=0
    )
    grad_readout = jnp.sum(
        (-valid_mask * jax.nn.sigmoid(-real_logits))[:, None] * act_real
        + (valid_mask * jax.nn.sigmoid(fake_logits))[:, None] * act_fake,
        axis=0,
    )
    scalars = jnp.pad(jnp.stack([starts, gen_local, critic_local])[None], ((0, 0), (0, D - 3)))
    critic_block = jnp.concatenate([grad_mat, grad_bias[None], grad_readout[None], scalars], axis=0)
    gains_rows = jnp.concatenate([parts[2][:9] for parts in layer_parts], axis=0).T
    edge_block = jnp.concatenate(
        [grad_edges, gains_rows, jnp.zeros((D, EDGE_WIDE - EDGE - gain_count), jnp.float32)], axis=1
    ).astype(jnp.bfloat16)
    blocks = []
    for layer_idx in reversed(range(LAYERS)):
        blocks += [layer_parts[layer_idx][0], layer_parts[layer_idx][1]]
    blocks += [edge_block, grad_codes.astype(jnp.bfloat16).reshape(-1, 128)]
    joined, critic_all, square_sum = reduce_all(blocks, critic_block, n_chip, n_dp, 2)
    images, gen_total, critic_total = (critic_all[PIX + 2, place] for place in range(3))
    edge_total = joined[2 * LAYERS]
    reduced = (
        jnp.stack([joined[2 * (LAYERS - 1 - layer_idx)] for layer_idx in range(LAYERS)]),
        jnp.stack([joined[2 * (LAYERS - 1 - layer_idx) + 1] for layer_idx in range(LAYERS)]),
        edge_total[:, EDGE : EDGE + gain_count].T.reshape(LAYERS, 9, owned),
        edge_total[:, :EDGE],
        joined[2 * LAYERS + 1].reshape(-1, LAT),
    )
    critic_grad = critic_all[: PIX + 2]
    scaled = [gradient / images for gradient in reduced]
    grad_norm = jnp.sqrt(square_sum) / images
    factor = jnp.minimum(1.0, clip_norm / grad_norm)
    new_attn = adam_update(attn_weights, scaled[0] * factor, attn_first, attn_second)
    new_mlp = adam_update(mlp_weights, scaled[1] * factor, mlp_first, mlp_second)
    new_gains = adam_update(layer_gains, scaled[2] * factor, gains_first, gains_second)
    new_edges = adam_update(edge_weights, scaled[3] * factor, edges_first, edges_second)
    new_codes = adam_update(codebook, scaled[4] * factor, codebook_first, codebook_second)
    new_critic = adam_update(critic_weights, critic_grad / images, critic_first, critic_second)
    losses = jnp.stack([gen_total / images, critic_total / images])
    return (
        new_attn[0],
        new_attn[1],
        new_attn[2],
        new_mlp[0],
        new_mlp[1],
        new_mlp[2],
        new_gains[0],
        new_gains[1],
        new_gains[2],
        new_edges[0],
        new_edges[1],
        new_edges[2],
        new_codes[0],
        new_codes[1],
        new_codes[2],
        new_critic[0],
        new_critic[1],
        new_critic[2],
        losses,
        grad_norm,
        new_attn[0].astype(jnp.bfloat16),
        new_mlp[0].astype(jnp.bfloat16),
        new_edges[0].astype(jnp.bfloat16),
        new_codes[0].astype(jnp.bfloat16),
    )


def solution(mesh):
    return jax.shard_map(
        functools.partial(per_device, mesh),
        mesh=mesh,
        in_specs=(
            P(("fsdp", "dp"), None, None),
            P(("fsdp", "dp"), None),
            P(("fsdp", "dp"), None),
            P(("fsdp", "dp"), None),
            P(("fsdp", "dp"), None),
            P(None, "fsdp", None),
            P(None, "fsdp", None),
            P(None, None, "fsdp"),
            P("fsdp", None),
            P("fsdp", None),
            P(),
            P(None, "fsdp", None),
            P(None, "fsdp", None),
            P(None, "fsdp", None),
            P(None, "fsdp", None),
            P(None, None, "fsdp"),
            P(None, None, "fsdp"),
            P("fsdp", None),
            P("fsdp", None),
            P("fsdp", None),
            P("fsdp", None),
            P(),
            P(),
        ),
        out_specs=(
            P(None, "fsdp", None),
            P(None, "fsdp", None),
            P(None, "fsdp", None),
            P(None, "fsdp", None),
            P(None, "fsdp", None),
            P(None, "fsdp", None),
            P(None, None, "fsdp"),
            P(None, None, "fsdp"),
            P(None, None, "fsdp"),
            P("fsdp", None),
            P("fsdp", None),
            P("fsdp", None),
            P("fsdp", None),
            P("fsdp", None),
            P("fsdp", None),
            P(),
            P(),
            P(),
            P(),
            P(),
            P(None, "fsdp", None),
            P(None, "fsdp", None),
            P("fsdp", None),
            P("fsdp", None),
        ),
        check_vma=False,
    )
```

```python
import functools
import math

import jax
import jax.numpy as jnp
from jax import lax
from jax.experimental import pallas as pl
from jax.experimental.pallas import tpu as pltpu
from jax.sharding import PartitionSpec as P

MESH = pl.DeviceIdType.MESH
D = 512
HEADS = 8
HEAD = 64
FF = 2048
LAT = 32
CODES = 8192
PIX = 192
LAYERS = 2
TILE = 256
REACH = 256
PAIRS = HEADS // 2
EDGE = 2 * PIX + 2 * LAT + 2
EDGE_WIDE = 512


beta_one = 0.9
beta_two = 0.95
adam_eps = 1e-08
decay_rate = 0.1
learn_rate = 0.2
clip_norm = 0.5
commit_weight = 0.25
adverse_weight = 0.2
adam_step = 10.0
norm_eps = 1e-05
excluded = -1e30
kernel_vmem = 60 << 20


def layer_norm(values, gain, shift):
    center = values - jnp.mean(values, axis=-1, keepdims=True)
    spread = jnp.mean(center * center, axis=-1, keepdims=True)
    return center * lax.rsqrt(spread + norm_eps) * gain + shift


def dot_nn(left_side, right_side):
    return lax.dot_general(left_side, right_side, (((1,), (0,)), ((), ())), preferred_element_type=jnp.float32)


def dot_nt(left_side, right_side):
    return lax.dot_general(left_side, right_side, (((1,), (1,)), ((), ())), preferred_element_type=jnp.float32)


def dot_tn(left_side, right_side):
    return lax.dot_general(left_side, right_side, (((0,), (0,)), ((), ())), preferred_element_type=jnp.float32)


def center_rows(values):
    center = values - jnp.mean(values, axis=-1, keepdims=True)
    spread = jnp.mean(center * center, axis=-1, keepdims=True)
    scale = lax.rsqrt(spread + norm_eps)
    return center * scale, scale


def norm_rows_back(grad, unit, scale, gain):
    grad_unit = grad * gain
    mean_grad = jnp.mean(grad_unit, axis=-1, keepdims=True)
    mean_along = jnp.mean(grad_unit * unit, axis=-1, keepdims=True)
    return scale * (grad_unit - mean_grad - unit * mean_along)


def gelu_tanh(values):
    cubic_term = values + 0.044715 * values * values * values
    return 0.5 * values * (1.0 + jnp.tanh(0.7978845608028654 * cubic_term))


def gelu_slope(values):
    square = values * values
    bend = jnp.tanh(0.7978845608028654 * values * (1.0 + 0.044715 * square))
    active = 0.5 * values * (1.0 + bend)
    slope = 0.5 * (1.0 + bend) + 0.5 * values * (1.0 - bend * bend) * (
        0.7978845608028654 * (1.0 + 3.0 * 0.044715 * square)
    )
    return active, slope


def key_window(tile_idx, length):
    start = tile_idx * TILE
    return max(0, start - REACH), min(length, start + TILE + REACH)


def rows_at(tile_idx):
    return pl.ds(pl.multiple_of(tile_idx * TILE, TILE), TILE)


def lane_half(array):
    return lax.broadcasted_iota(jnp.int32, array.shape, 1) < HEAD


def split_pair(array):
    low_half = lane_half(array)
    zero = jnp.zeros_like(array)
    return jnp.where(low_half, array, zero), jnp.where(low_half, zero, array)


def forward_kernel(comm, n_chip, n_dp, *refs):
    stream, attn_low, mlp_low, gains, marks_row, marks_col = refs[:6]
    shards, refs = refs[6 : 6 + comm], refs[6 + comm :]
    output, mixed, context, logsum, middle = refs[:5]
    gathered, refs = refs[5 : 5 + comm], refs[5 + comm :]
    bias, active = refs[:2]
    if comm:
        places = Places(n_chip, n_dp)
        places.greet(places.plane_devices())
        gather = Gather(places, shards, gathered, refs[2:])
        for a in range(comm):
            gather.start(a)
    length = stream.shape[0]
    tiles = length // TILE

    def mix_tile(t, carry):
        unit, _ = center_rows(stream[rows_at(t), :])
        hidden = (unit * gains[0:1, :] + gains[1:2, :]).astype(jnp.bfloat16)
        for part in range(3):
            columns = pl.ds(part * D, D)
            mixed[rows_at(t), columns] = dot_nn(hidden, attn_low[:, columns]).astype(jnp.bfloat16)
        return carry

    lax.fori_loop(0, tiles, mix_tile, 0)

    for t in range(tiles):
        if t == 2 and comm:
            gather.forward(0)
        first, last = key_window(t, length)
        span = last - first
        rows = pl.ds(t * TILE, TILE)
        window = pl.ds(first, span)
        row_place = t * TILE + lax.broadcasted_iota(jnp.int32, (TILE, span), 0)
        key_place = first + lax.broadcasted_iota(jnp.int32, (TILE, span), 1)
        allowed = (marks_col[rows, 0:1] == marks_row[1:2, window]) | (row_place == key_place)
        bias[:, 0:span] = jnp.where(allowed, 0.0, excluded)

        def pair_step(pair, sums):
            lanes = pl.ds(pl.multiple_of(pair * 128, 128), 128)
            key_lanes = pl.ds(pl.multiple_of(D + pair * 128, 128), 128)
            value_lanes = pl.ds(pl.multiple_of(2 * D + pair * 128, 128), 128)
            queries = split_pair(mixed[rows, lanes] * jnp.bfloat16(HEAD**-0.5))
            keys = mixed[window, key_lanes]
            values = split_pair(mixed[window, value_lanes])
            total = None
            lane_ids = lax.broadcasted_iota(jnp.int32, (TILE, 128), 1)
            for half in range(2):
                scores = dot_nt(queries[half], keys) + bias[:, 0:span]
                peak = jnp.max(scores, axis=-1, keepdims=True)
                powers = jnp.exp(scores - peak)
                weight = jnp.sum(powers, axis=-1, keepdims=True)
                probs = (powers * (1.0 / weight)).astype(jnp.bfloat16)
                part = dot_nn(probs, values[half])
                total = part if total is None else total + part
                sums = jnp.where(lane_ids == 2 * pair + half, peak + jnp.log(weight), sums)
            context[rows, lanes] = total.astype(jnp.bfloat16)
            return sums

        logsum[rows, :] = lax.fori_loop(0, PAIRS, pair_step, jnp.zeros((TILE, 128), jnp.float32))

    def mlp_tile(t, carry):
        rows = rows_at(t)
        mid = stream[rows, :] + dot_nn(context[rows, :], attn_low[:, 3 * D : 4 * D])
        middle[rows, :] = mid
        unit, _ = center_rows(mid)
        hidden = (unit * gains[2:3, :] + gains[3:4, :]).astype(jnp.bfloat16)
        for part in range(FF // D):
            columns = pl.ds(part * D, D)
            inner = dot_nn(hidden, mlp_low[:, columns]) + gains[5 + part : 6 + part, :]
            active[:, columns] = gelu_tanh(inner).astype(jnp.bfloat16)
        output[rows, :] = mid + dot_nt(active[...], mlp_low[:, FF:]) + gains[4:5, :]
        return carry

    lax.fori_loop(0, tiles, mlp_tile, 0)
    for a in range(1, comm):
        gather.forward(a)
    for a in range(comm):
        gather.finish(a)


def whole_vmem(count):
    return [pl.BlockSpec(memory_space=pltpu.VMEM)] * count


def layer_forward(stream, weights, marks, shards, n_chip, n_dp, collective_id):
    attn_low, mlp_low, gains = weights
    length, comm = stream.shape[0], len(shards)
    anywhere = [pl.BlockSpec(memory_space=pl.ANY)] * comm
    results = pl.pallas_call(
        functools.partial(forward_kernel, comm, n_chip, n_dp),
        out_shape=[
            jax.ShapeDtypeStruct((length, D), jnp.float32),
            jax.ShapeDtypeStruct((length, 3 * D), jnp.bfloat16),
            jax.ShapeDtypeStruct((length, D), jnp.bfloat16),
            jax.ShapeDtypeStruct((length, 128), jnp.float32),
            jax.ShapeDtypeStruct((length, D), jnp.float32),
        ]
        + gathered_shapes(shards, n_chip),
        in_specs=whole_vmem(6) + anywhere,
        out_specs=whole_vmem(5) + anywhere,
        scratch_shapes=[pltpu.VMEM((TILE, TILE + 2 * REACH), jnp.float32), pltpu.VMEM((TILE, FF), jnp.bfloat16)]
        + (Gather.semaphores(comm, n_chip) if comm else []),
        compiler_params=pltpu.CompilerParams(
            vmem_limit_bytes=kernel_vmem, collective_id=collective_id, has_side_effects=comm > 0
        ),
    )(stream, attn_low, mlp_low, gains, *marks, *shards)
    return results[:5], join_gathered(results[5:])


def backward_kernel(comm, n_chip, n_dp, *refs):
    refs = list(refs)
    take = lambda size: [refs.pop(0) for _ in range(size)]
    stream, mixed, context, logsum, middle, attn_low, mlp_low, gains, marks_row, marks_col, grad_stream = take(11)
    later = take(comm)
    grad_input, grad_attn, grad_mlp, grad_gains = take(4)
    parts = take(comm)
    branch, active, grad_inner, hidden_low, grad_out, grad_context, grad_mixed, bias, grad_keys, grad_values = take(10)
    if comm:
        places = Places(n_chip, n_dp)
        places.greet(places.plane_devices())
        planes = PlaneReduce(places, later, take(comm), take(comm), take(comm), refs)
        for a in range(comm):
            planes.start(a)
    length = stream.shape[0]
    tiles = length // TILE
    grad_gains[...] = jnp.zeros_like(grad_gains)

    def add_row(place, rows):
        grad_gains[place : place + 1, :] += jnp.sum(rows, axis=0, keepdims=True)

    def mlp_tile(t, carry):
        rows = rows_at(t)
        upper = grad_stream[rows, :]
        upper_low = upper.astype(jnp.bfloat16)
        branch[rows, :] = upper_low
        add_row(4, upper_low.astype(jnp.float32))
        unit, scale = center_rows(middle[rows, :])
        hidden = (unit * gains[2:3, :] + gains[3:4, :]).astype(jnp.bfloat16)
        hidden_low[rows, :] = hidden
        grad_hidden = jnp.zeros((TILE, D), jnp.float32)
        for part in range(FF // D):
            columns = pl.ds(part * D, D)
            inner = dot_nn(hidden, mlp_low[:, columns]) + gains[5 + part : 6 + part, :]
            act, slope = gelu_slope(inner)
            active[rows, columns] = act.astype(jnp.bfloat16)
            pre_grad = (dot_nn(upper_low, mlp_low[:, pl.ds(FF + part * D, D)]) * slope).astype(jnp.bfloat16)
            grad_inner[rows, columns] = pre_grad
            add_row(5 + part, pre_grad.astype(jnp.float32))
            grad_hidden = grad_hidden + dot_nt(pre_grad, mlp_low[:, columns])
        add_row(2, grad_hidden * unit)
        add_row(3, grad_hidden)
        grad_mid = norm_rows_back(grad_hidden, unit, scale, gains[2:3, :]) + upper
        grad_input[rows, :] = grad_mid
        mid_low = grad_mid.astype(jnp.bfloat16)
        grad_out[rows, :] = mid_low
        grad_context[rows, :] = dot_nt(mid_low, attn_low[:, 3 * D : 4 * D]).astype(jnp.bfloat16)
        return carry

    lax.fori_loop(0, tiles, mlp_tile, 0)

    for a in range(comm):
        planes.add_pair(a)
    for part in range(FF // D):
        columns = pl.ds(part * D, D)
        grad_mlp[:, columns] = dot_tn(hidden_low[...], grad_inner[:, columns]).astype(jnp.bfloat16)
        grad_mlp[:, pl.ds(FF + part * D, D)] = dot_tn(branch[...], active[:, columns]).astype(jnp.bfloat16)
    grad_attn[:, 3 * D : 4 * D] = dot_tn(context[...], grad_out[...]).astype(jnp.bfloat16)

    for t in range(tiles):
        first, last = key_window(t, length)
        span = last - first
        key_place = first + lax.broadcasted_iota(jnp.int32, (span, TILE), 0)
        row_place = t * TILE + lax.broadcasted_iota(jnp.int32, (span, TILE), 1)
        allowed = (marks_col[pl.ds(first, span), 1:2] == marks_row[0:1, pl.ds(t * TILE, TILE)]) | (row_place == key_place)
        bias[t, 0:span, :] = jnp.where(allowed, 0.0, excluded)
    sums_t = [logsum[pl.ds(t * TILE, TILE), :].T[0:8, :] for t in range(tiles)]

    def pair_step(pair, carry):
        lanes = pl.ds(pl.multiple_of(pair * 128, 128), 128)
        key_lanes = pl.ds(pl.multiple_of(D + pair * 128, 128), 128)
        value_lanes = pl.ds(pl.multiple_of(2 * D + pair * 128, 128), 128)
        grad_keys[...] = jnp.zeros_like(grad_keys)
        grad_values[...] = jnp.zeros_like(grad_values)
        for t in range(tiles):
            first, last = key_window(t, length)
            span = last - first
            rows = pl.ds(t * TILE, TILE)
            window = pl.ds(first, span)
            queries = split_pair(mixed[rows, lanes] * jnp.bfloat16(HEAD**-0.5))
            grads = split_pair(grad_context[rows, lanes])
            keys = mixed[window, key_lanes]
            values = mixed[window, value_lanes]
            key_halves = split_pair(keys)
            head_ids = lax.broadcasted_iota(jnp.int32, (8, TILE), 0)
            add_keys, add_values, add_queries = None, None, None
            for half in range(2):
                sums = jnp.sum(jnp.where(head_ids == 2 * pair + half, sums_t[t], 0.0), axis=0, keepdims=True)
                probs = jnp.exp(dot_nt(keys, queries[half]) + bias[t, 0:span, :] - sums)
                grad_probs = dot_nt(values, grads[half])
                weighted = probs * grad_probs
                grad_scores = (weighted - probs * jnp.sum(weighted, axis=0, keepdims=True)).astype(jnp.bfloat16)
                to_keys = dot_nn(grad_scores, queries[half])
                to_values = dot_nn(probs.astype(jnp.bfloat16), grads[half])
                to_queries = dot_tn(grad_scores, key_halves[half])
                if half == 0:
                    add_keys, add_values, add_queries = to_keys, to_values, to_queries
                else:
                    add_keys, add_values, add_queries = add_keys + to_keys, add_values + to_values, add_queries + to_queries
            grad_keys[window, :] += add_keys
            grad_values[window, :] += add_values
            grad_mixed[rows, lanes] = (add_queries * HEAD**-0.5).astype(jnp.bfloat16)
        grad_mixed[:, key_lanes] = grad_keys[...].astype(jnp.bfloat16)
        grad_mixed[:, value_lanes] = grad_values[...].astype(jnp.bfloat16)
        return carry

    lax.fori_loop(0, PAIRS, pair_step, 0)

    def input_tile(t, carry):
        rows = rows_at(t)
        unit, scale = center_rows(stream[rows, :])
        hidden_low[rows, :] = (unit * gains[0:1, :] + gains[1:2, :]).astype(jnp.bfloat16)
        grad_hidden = dot_nt(grad_mixed[rows, :], attn_low[:, 0 : 3 * D])
        add_row(0, grad_hidden * unit)
        add_row(1, grad_hidden)
        grad_input[rows, :] += norm_rows_back(grad_hidden, unit, scale, gains[0:1, :])
        return carry

    lax.fori_loop(0, tiles, input_tile, 0)
    for part in range(3):
        columns = pl.ds(part * D, D)
        grad_attn[:, columns] = dot_tn(hidden_low[...], grad_mixed[:, columns]).astype(jnp.bfloat16)
    for a in range(comm):
        planes.add_chips(a, parts[a])


def layer_backward(saved, weights, grad_stream, marks, later, n_chip, n_dp, collective_id):
    stream, mixed, context, logsum, middle = saved
    attn_low, mlp_low, gains = weights
    length, comm = stream.shape[0], len(later)
    arrays = [split_owners(block, n_chip, n_dp) for block in later]
    plane_scratch, plane_sems = PlaneReduce.scratch(arrays, n_chip, n_dp) if comm else ([], [])
    low = lambda *shape: pltpu.VMEM(shape, jnp.bfloat16)
    results = pl.pallas_call(
        functools.partial(backward_kernel, comm, n_chip, n_dp),
        out_shape=[
            jax.ShapeDtypeStruct((length, D), jnp.float32),
            jax.ShapeDtypeStruct((D, 4 * D), jnp.bfloat16),
            jax.ShapeDtypeStruct((D, 2 * FF), jnp.bfloat16),
            jax.ShapeDtypeStruct((16, D), jnp.float32),
        ]
        + [jax.ShapeDtypeStruct((n_dp,) + a.shape[-2:], a.dtype) for a in arrays],
        in_specs=whole_vmem(11) + [pl.BlockSpec(memory_space=pl.ANY)] * comm,
        out_specs=whole_vmem(4 + comm),
        scratch_shapes=[
            low(length, D), low(length, FF), low(length, FF), low(length, D), low(length, D), low(length, D),
            low(length, 3 * D), pltpu.VMEM((length // TILE, TILE + 2 * REACH, TILE), jnp.float32),
            pltpu.VMEM((length, 128), jnp.float32), pltpu.VMEM((length, 128), jnp.float32),
        ] + plane_scratch + plane_sems,
        compiler_params=pltpu.CompilerParams(
            vmem_limit_bytes=kernel_vmem, collective_id=collective_id, has_side_effects=comm > 0
        ),
    )(stream, mixed, context, logsum, middle, attn_low, mlp_low, gains, *marks, grad_stream, *arrays)
    return results[:4], results[4:]


def normalize_rows(values):
    return values * lax.rsqrt(jnp.sum(values * values, axis=-1, keepdims=True) + 1.0)


def feature_table():
    pixel_idx = jnp.arange(PIX, dtype=jnp.float32)[:, None]
    frequency = jnp.arange(PIX, dtype=jnp.float32)[None, :]
    return jnp.cos(math.pi * (pixel_idx + 0.5) * frequency / PIX) * (
        math.sqrt(2.0 / PIX) / (1.0 + frequency / 16.0)
    )


def low_dot(left_side, right_side):
    return jnp.dot(left_side, right_side, preferred_element_type=jnp.float32)


def add_parts(terms, kind=jnp.bfloat16):
    total = terms[0].astype(jnp.float32)
    for term in terms[1:]:
        total = total + term.astype(jnp.float32)
    return total.astype(kind)


class Places:
    def __init__(self, n_chip, n_dp):
        self.n_chip, self.n_dp = n_chip, n_dp
        self.place = lax.axis_index("fsdp")
        self.plane = lax.axis_index("dp")
        self.core = lax.rem(self.place, 2)
        self.chip = lax.div(self.place, 2)

    def sibling(self):
        return {"fsdp": self.place + 1 - 2 * self.core}

    def chip_at(self, j):
        return lax.rem(self.chip + j, self.n_chip)

    def same_core(self, j):
        return {"fsdp": self.chip_at(j) * 2 + self.core}

    def plane_at(self, t):
        return lax.rem(self.plane + t, self.n_dp)

    def same_place(self, t):
        return {"dp": self.plane_at(t)}

    def greet(self, devices):
        barrier = pltpu.get_barrier_semaphore()
        for device in devices:
            pl.semaphore_signal(barrier, inc=1, device_id=device, device_id_type=MESH)
        pl.semaphore_wait(barrier, len(devices))

    def plane_devices(self):
        return [self.sibling()] + [self.same_core(j) for j in range(1, self.n_chip)]


def remote(source, target, send, recv, device):
    return pltpu.make_async_remote_copy(
        src_ref=source, dst_ref=target, send_sem=send, recv_sem=recv, device_id=device, device_id_type=MESH
    )


class Gather:
    def __init__(self, places, shards, outs, sems):
        self.places, self.shards, self.outs = places, shards, outs
        self.local_sem, self.chip_send, self.chip_recv, self.pair_send, self.pair_recv = sems

    @staticmethod
    def semaphores(count, n_chip):
        dma = pltpu.SemaphoreType.DMA
        return [dma((count,))] + [dma((count, n_chip - 1))] * 2 + [dma((count, n_chip))] * 2

    def local_copy(self, a):
        mine = self.outs[a].at[self.places.chip, self.places.core]
        return pltpu.make_async_copy(self.shards[a], mine, self.local_sem.at[a])

    def chip_copy(self, a, j):
        mine = self.outs[a].at[self.places.chip, self.places.core]
        sems = (self.chip_send.at[a, j - 1], self.chip_recv.at[a, j - 1])
        return remote(self.shards[a], mine, *sems, self.places.same_core(j))

    def pair_copy(self, a, j):
        n_chip = self.places.n_chip
        block = self.outs[a].at[lax.rem(self.places.chip + n_chip - j, n_chip), self.places.core]
        source = self.shards[a] if j == 0 else block
        return remote(source, block, self.pair_send.at[a, j], self.pair_recv.at[a, j], self.places.sibling())

    def start(self, a):
        for j in range(1, self.places.n_chip):
            self.chip_copy(a, j).start()
        self.pair_copy(a, 0).start()
        self.local_copy(a).start()

    def forward(self, a):
        for j in range(1, self.places.n_chip):
            self.chip_copy(a, j).wait_recv()
            self.pair_copy(a, j).start()

    def finish(self, a):
        self.local_copy(a).wait()
        for j in range(self.places.n_chip):
            self.pair_copy(a, j).wait()
            if j > 0:
                self.chip_copy(a, j).wait_send()


def gather_kernel(count, n_chip, n_dp, *refs):
    places = Places(n_chip, n_dp)
    places.greet(places.plane_devices())
    gather = Gather(places, refs[:count], refs[count : 2 * count], refs[2 * count :])
    for a in range(count):
        gather.start(a)
    for a in range(count):
        gather.forward(a)
    for a in range(count):
        gather.finish(a)


def gathered_shapes(shards, n_chip):
    return [jax.ShapeDtypeStruct((n_chip, 2) + s.shape, s.dtype) for s in shards]


def join_gathered(gathered):
    return [g.reshape((-1,) + g.shape[3:]) for g in gathered]


def gather_all(shards, n_chip, n_dp, collective_id):
    count = len(shards)
    gathered = pl.pallas_call(
        functools.partial(gather_kernel, count, n_chip, n_dp),
        out_shape=gathered_shapes(shards, n_chip),
        in_specs=[pl.BlockSpec(memory_space=pl.ANY)] * count,
        out_specs=[pl.BlockSpec(memory_space=pl.ANY)] * count,
        scratch_shapes=Gather.semaphores(count, n_chip),
        compiler_params=pltpu.CompilerParams(collective_id=collective_id, has_side_effects=True),
    )(*shards)
    return join_gathered(gathered)


class PlaneReduce:
    def __init__(self, places, ins, pair_in, sums, chip_in, sems):
        self.places, self.ins, self.pair_in, self.sums, self.chip_in = places, ins, pair_in, sums, chip_in
        self.pair_send, self.pair_recv, self.local_sem, self.chip_send, self.chip_recv = sems

    @staticmethod
    def scratch(arrays, n_chip, n_dp):
        shapes = []
        for outer in (n_chip, n_chip, n_chip - 1):
            shapes += [pltpu.VMEM((outer, n_dp) + a.shape[3:], a.dtype) for a in arrays]
        count, dma = len(arrays), pltpu.SemaphoreType.DMA
        return shapes, [dma((count,))] * 3 + [dma((count, n_chip - 1))] * 2

    def pair_copy(self, a):
        source = self.ins[a].at[:, 1 - self.places.core]
        return remote(source, self.pair_in[a], self.pair_send.at[a], self.pair_recv.at[a], self.places.sibling())

    def local_copy(self, a):
        return pltpu.make_async_copy(self.ins[a].at[:, self.places.core], self.sums[a], self.local_sem.at[a])

    def chip_copy(self, a, j):
        sems = (self.chip_send.at[a, j - 1], self.chip_recv.at[a, j - 1])
        source = self.sums[a].at[self.places.chip_at(j)]
        return remote(source, self.chip_in[a].at[j - 1], *sems, self.places.same_core(j))

    def start(self, a):
        self.pair_copy(a).start()
        self.local_copy(a).start()

    def add_pair(self, a):
        n_chip, n_dp = self.places.n_chip, self.places.n_dp
        self.pair_copy(a).wait()
        self.local_copy(a).wait()

        def body(i, carry):
            c, d = lax.div(i, n_dp), lax.rem(i, n_dp)
            self.sums[a][c, d] = add_parts([self.sums[a][c, d], self.pair_in[a][c, d]], self.ins[a].dtype)
            return carry

        lax.fori_loop(0, n_chip * n_dp, body, 0)
        for j in range(1, n_chip):
            self.chip_copy(a, j).start()

    def add_chips(self, a, part):
        n_chip, n_dp = self.places.n_chip, self.places.n_dp
        for j in range(1, n_chip):
            self.chip_copy(a, j).wait()

        def body(d, carry):
            terms = [self.sums[a][self.places.chip, d]] + [self.chip_in[a][j, d] for j in range(n_chip - 1)]
            part[d] = add_parts(terms, self.ins[a].dtype)
            return carry

        lax.fori_loop(0, n_dp, body, 0)


def reduce_kernel(early, count, n_chip, n_dp, *refs):
    every = early + count
    refs = list(refs)
    take = lambda size: [refs.pop(0) for _ in range(size)]
    ready, ins = take(early), take(count)
    outs, (critic_out, norm_out) = take(every - 1), take(2)
    pair_in, sums, chip_in, part, copy_in = take(count), take(count), take(count), take(count), take(every)
    outs += take(1)
    norm_mine, norm_dp, norm_fsdp = take(3)
    plane_sems = take(5)
    rs_send, rs_recv, ag_send, ag_recv = take(4)
    spread_send, spread_recv, mirror_send, mirror_recv, n1_send, n1_recv, n2_send, n2_recv = refs
    part = ready + part
    places = Places(n_chip, n_dp)
    place, plane, core, chip = places.place, places.plane, places.core, places.chip
    n_place = 2 * n_chip
    last = every - 1
    peers = [{"fsdp": lax.rem(place + j, n_place)} for j in range(1, n_place)]
    copies = [places.same_place(t) for t in range(1, n_dp)]
    places.greet(peers + copies)
    planes = PlaneReduce(places, ins, pair_in, sums, chip_in, plane_sems)

    def rs_copy(a, t):
        sems = (rs_send.at[a, t - 1], rs_recv.at[a, t - 1])
        return remote(part[a].at[places.plane_at(t)], copy_in[a].at[t - 1], *sems, places.same_place(t))

    def ag_copy(a, t):
        sems = (ag_send.at[a, t - 1], ag_recv.at[a, t - 1])
        return remote(outs[a].at[plane], outs[a].at[plane], *sems, places.same_place(t))

    def spread_copy(j):
        sems = (spread_send.at[j - 1], spread_recv.at[j - 1])
        return remote(outs[last], critic_out.at[chip, core], *sems, places.same_core(j))

    def mirror_copy():
        return remote(critic_out.at[:, core], critic_out.at[:, core], mirror_send, mirror_recv, places.sibling())

    def norm_dp_copy(t):
        return remote(norm_mine, norm_dp.at[t - 1], n1_send.at[t - 1], n1_recv.at[t - 1], places.same_place(t))

    def norm_fsdp_copy(j):
        return remote(norm_out, norm_fsdp.at[j - 1], n2_send.at[j - 1], n2_recv.at[j - 1], peers[j - 1])

    def start_dp(a):
        for t in range(1, n_dp):
            rs_copy(a, t).start()

    def stage_pair(a):
        planes.add_pair(a - early)

    def stage_chip(a):
        planes.add_chips(a - early, part[a])
        start_dp(a)

    def stage_dp(a):
        for t in range(1, n_dp):
            rs_copy(a, t).wait()
        total = add_parts([part[a][plane]] + [copy_in[a][t] for t in range(n_dp - 1)], outs[a].dtype)
        outs[a][plane] = total
        for t in range(1, n_dp):
            ag_copy(a, t).start()
        if a != last:
            square = total.astype(jnp.float32) * total.astype(jnp.float32)
            norm_mine[0:1, :] += jnp.sum(jnp.sum(square, axis=0, keepdims=True), axis=1, keepdims=True)

    def stage_end(a):
        for t in range(1, n_dp):
            ag_copy(a, t).wait()
        if a == last:
            critic_out[chip, core] = outs[last][...]
            for j in range(1, n_chip):
                spread_copy(j).start()

    norm_mine[...] = jnp.zeros_like(norm_mine)
    sequence = [last] + list(range(early, last))
    planes.start(sequence[0] - early)
    planes.start(sequence[1] - early)
    for a in range(early):
        start_dp(a)
    for turn in range(count + 2):
        for depth, stage in enumerate((stage_pair, stage_chip, stage_dp)):
            if 0 <= turn - depth < count:
                stage(sequence[turn - depth])
                if depth == 0 and turn + 2 < count:
                    planes.start(sequence[turn + 2] - early)
        if turn < early:
            stage_dp(turn)
        if turn == 3:
            stage_end(last)
    for t in range(1, n_dp):
        norm_dp_copy(t).start()
    for j in range(1, n_chip):
        spread_copy(j).wait()
    mirror_copy().start()
    for t in range(1, n_dp):
        norm_dp_copy(t).wait()
    norm_out[...] = norm_mine[...]
    for t in range(n_dp - 1):
        norm_out[...] += norm_dp[t]
    for j in range(1, n_place):
        norm_fsdp_copy(j).start()
    for a in range(last):
        stage_end(a)
    mirror_copy().wait()
    for j in range(1, n_place):
        norm_fsdp_copy(j).wait()
    total = norm_out[...]
    for j in range(n_place - 1):
        total = total + norm_fsdp[j]
    norm_out[...] = total


def split_owners(gradient, n_chip, n_dp):
    rows, columns = gradient.shape
    owned = rows // (2 * n_chip)
    if owned % (16 * n_dp) == 0:
        return gradient.reshape(n_chip, 2, n_dp, owned // n_dp, columns)
    if columns % (128 * n_dp) == 0:
        parts = gradient.reshape(n_chip, 2, owned, n_dp, columns // n_dp)
        return parts.transpose(0, 1, 3, 2, 4)
    return gradient.reshape(n_chip, 2, n_dp, owned // n_dp, columns)


def join_owned(parts, owned, columns):
    if parts.shape[2] == columns:
        return parts.reshape(owned, columns)
    return parts.transpose(1, 0, 2).reshape(owned, columns)


def reduce_all(ready, blocks, critic_block, n_chip, n_dp, collective_id):
    rows = critic_block.shape[0]
    share = -(-rows // (2 * n_chip * n_dp))
    critic_parts = jnp.pad(critic_block, ((0, share * 2 * n_chip * n_dp - rows), (0, 0)))
    critic_parts = critic_parts.reshape(n_chip, 2, n_dp, share, -1)
    arrays = [split_owners(block, n_chip, n_dp) for block in blocks] + [critic_parts]
    early, count = len(ready), len(arrays)
    parts = [jax.ShapeDtypeStruct((n_dp,) + a.shape[-2:], a.dtype) for a in list(ready) + arrays]
    dma = pltpu.SemaphoreType.DMA
    plane_scratch, plane_sems = PlaneReduce.scratch(arrays, n_chip, n_dp)
    scratch = plane_scratch
    scratch += [pltpu.VMEM(p.shape, p.dtype) for p in parts[early:]]
    scratch += [pltpu.VMEM((n_dp - 1,) + p.shape[1:], p.dtype) for p in parts]
    scratch += [pltpu.VMEM(parts[-1].shape, jnp.float32), pltpu.VMEM((8, 128), jnp.float32)]
    scratch += [pltpu.VMEM((n_dp - 1, 8, 128), jnp.float32), pltpu.VMEM((2 * n_chip - 1, 8, 128), jnp.float32)]
    scratch += plane_sems + [dma((early + count, n_dp - 1))] * 4
    scratch += [dma((n_chip - 1,))] * 2 + [dma(())] * 2 + [dma((n_dp - 1,))] * 2 + [dma((2 * n_chip - 1,))] * 2
    results = pl.pallas_call(
        functools.partial(reduce_kernel, early, count, n_chip, n_dp),
        out_shape=parts[:-1]
        + [
            jax.ShapeDtypeStruct((n_chip, 2) + parts[-1].shape, jnp.float32),
            jax.ShapeDtypeStruct((8, 128), jnp.float32),
        ],
        in_specs=[pl.BlockSpec(memory_space=pltpu.VMEM)] * early + [pl.BlockSpec(memory_space=pl.ANY)] * count,
        out_specs=[pl.BlockSpec(memory_space=pltpu.VMEM)] * (early + count + 1),
        scratch_shapes=scratch,
        compiler_params=pltpu.CompilerParams(
            collective_id=collective_id, has_side_effects=True, vmem_limit_bytes=kernel_vmem
        ),
    )(*ready, *arrays)
    return results[:-2], results[-2].reshape(-1, critic_block.shape[1])[:rows], results[-1][0, 0]


def adam_update(weight, gradient, first_state, second_state):
    first_state = beta_one * first_state + (1.0 - beta_one) * gradient
    second_state = beta_two * second_state + (1.0 - beta_two) * gradient * gradient
    step_size = (
        first_state
        / (1.0 - beta_one**adam_step)
        / (jnp.sqrt(second_state / (1.0 - beta_two**adam_step)) + adam_eps)
    )
    return (weight - learn_rate * (step_size + decay_rate * weight), first_state, second_state)


def per_device(
    mesh,
    patches,
    segments,
    validity,
    image_ids,
    code_ids,
    attn_weights,
    mlp_weights,
    layer_gains,
    edge_weights,
    codebook,
    critic_weights,
    attn_first,
    attn_second,
    mlp_first,
    mlp_second,
    gains_first,
    gains_second,
    edges_first,
    edges_second,
    codebook_first,
    codebook_second,
    critic_first,
    critic_second,
):
    patch_low = patches[0]
    patch_row = patch_low.astype(jnp.float32)
    segment = segments[0]
    valid_row = validity[0]
    valid_mask = valid_row.astype(jnp.float32)
    code_row = code_ids[0]
    image_row = image_ids[0]
    half_layers = LAYERS // 2
    n_chip, n_dp = mesh.shape["fsdp"] // 2, mesh.shape["dp"]
    owned = edge_weights.shape[0]
    gain_count = LAYERS * 9
    edge_shard = jnp.concatenate(
        [
            edge_weights,
            layer_gains.reshape(gain_count, owned).T,
            jnp.zeros((owned, EDGE_WIDE - EDGE - gain_count), jnp.float32),
        ],
        axis=1,
    )
    shards = [edge_shard, codebook.reshape(-1, 128)]
    for layer_idx in range(LAYERS):
        shards += [attn_weights[layer_idx], mlp_weights[layer_idx]]
    shards = [shard.astype(jnp.bfloat16) for shard in shards]
    edges_all, codes_low, *layer_weights = gather_all(shards[:4], n_chip, n_dp, 1)
    codes_low = codes_low.reshape(CODES, LAT)
    gains_all = edges_all[:, EDGE : EDGE + gain_count].T.reshape(LAYERS, 9, D).astype(jnp.float32)
    key_marks = jnp.stack([segment, jnp.where(valid_row > 0, segment, -1)])
    marks = (jnp.pad(key_marks, ((0, 6), (0, 0))), jnp.pad(key_marks.T, ((0, 0), (0, 126))))
    embed_in = edges_all[:, :PIX]
    head_out = edges_all[:, PIX : 2 * PIX]
    down_proj = edges_all[:, 2 * PIX : 2 * PIX + LAT]
    up_proj = edges_all[:, 2 * PIX + LAT : 2 * PIX + 2 * LAT]
    final_gain = edges_all[:, 2 * PIX + 2 * LAT].astype(jnp.float32)
    final_shift = edges_all[:, 2 * PIX + 2 * LAT + 1].astype(jnp.float32)
    critic_mat = critic_weights[:PIX].astype(jnp.bfloat16)
    critic_bias = critic_weights[PIX]
    readout = critic_weights[PIX + 1]
    stream = jnp.einsum("tp,dp->td", patch_low, embed_in, preferred_element_type=jnp.float32)
    kept_weights = []
    saved_all = []
    for layer_idx in range(LAYERS):
        if layer_idx == half_layers:
            encoder_low = stream.astype(jnp.bfloat16)
            latent = jnp.einsum(
                "td,dl->tl", encoder_low, down_proj, preferred_element_type=jnp.float32
            )
            unit_latent, unit_back = jax.vjp(normalize_rows, latent)
            encoded, encoded_back = jax.vjp(normalize_rows, codes_low.astype(jnp.float32))
            chosen = jnp.take(encoded, code_row, axis=0)
            commit_gap = unit_latent - chosen
            commit = jnp.sum(valid_mask * jnp.sum(commit_gap * commit_gap, axis=-1))
            quant_low = (unit_latent + (chosen - unit_latent)).astype(jnp.bfloat16)
            stream = jnp.einsum("tl,dl->td", quant_low, up_proj, preferred_element_type=jnp.float32)
        weights = (layer_weights[2 * layer_idx], layer_weights[2 * layer_idx + 1], gains_all[layer_idx])
        kept_weights.append(weights)
        block_input = stream
        later = shards[4 + 2 * layer_idx : 6 + 2 * layer_idx]
        (stream, *saved), more = layer_forward(stream, weights, marks, later, n_chip, n_dp, 3 if later else None)
        layer_weights += more
        saved_all.append((block_input, *saved))
    final_normed, final_back = jax.vjp(layer_norm, stream, final_gain, final_shift)
    final_low = final_normed.astype(jnp.bfloat16)
    rebuilt = jnp.einsum("td,dp->tp", final_low, head_out, preferred_element_type=jnp.float32)
    feat_table = feature_table()
    feat_diff = jnp.dot(
        rebuilt - patch_row,
        feat_table,
        precision=lax.Precision.HIGHEST,
        preferred_element_type=jnp.float32,
    )
    feature = jnp.sum(valid_mask * jnp.mean(feat_diff * feat_diff, axis=-1))
    rebuilt_low = rebuilt.astype(jnp.bfloat16)
    pre_fake = low_dot(rebuilt_low, critic_mat) + critic_bias
    act_fake, fake_back = jax.vjp(gelu_tanh, pre_fake)
    fake_logits = jnp.sum(act_fake * readout, axis=-1)
    adverse = jnp.sum(valid_mask * jax.nn.softplus(-fake_logits))
    gen_local = feature + adverse_weight * adverse + commit_weight * commit
    pre_real = low_dot(patch_low, critic_mat) + critic_bias
    act_real, real_back = jax.vjp(gelu_tanh, pre_real)
    real_logits = jnp.sum(act_real * readout, axis=-1)
    critic_local = jnp.sum(
        valid_mask * (jax.nn.softplus(-real_logits) + jax.nn.softplus(fake_logits))
    )
    change = jnp.concatenate([jnp.ones((1,), bool), image_row[1:] != image_row[:-1]])
    starts = jnp.sum(jnp.where(change & (valid_row > 0), 1.0, 0.0).astype(jnp.float32))
    grad_feature = jnp.dot(
        valid_mask[:, None] * (2.0 / PIX) * feat_diff,
        feat_table.T,
        precision=lax.Precision.HIGHEST,
        preferred_element_type=jnp.float32,
    )
    grad_logits = -adverse_weight * valid_mask * jax.nn.sigmoid(-fake_logits)
    (grad_pre,) = fake_back(grad_logits[:, None] * readout)
    grad_pre_low = grad_pre.astype(jnp.bfloat16)
    grad_rebuilt = grad_feature + jnp.einsum(
        "th,ph->tp", grad_pre_low, critic_mat, preferred_element_type=jnp.float32
    )
    grad_rebuilt_low = grad_rebuilt.astype(jnp.bfloat16)
    grad_head = jnp.einsum(
        "td,tp->dp", final_low, grad_rebuilt_low, preferred_element_type=jnp.float32
    )
    grad_final = jnp.einsum(
        "tp,dp->td", grad_rebuilt_low, head_out, preferred_element_type=jnp.float32
    )
    grad_stream, grad_final_gain, grad_final_shift = final_back(grad_final)
    layer_parts = [None] * LAYERS
    ready = []
    for layer_idx in reversed(range(LAYERS)):
        later = [] if layer_idx == LAYERS - 1 else layer_parts[layer_idx + 1][:2]
        (grad_stream, *layer_parts[layer_idx]), parts = layer_backward(
            saved_all[layer_idx], kept_weights[layer_idx], grad_stream, marks, later, n_chip, n_dp, 4 if later else None
        )
        ready += parts
        if layer_idx == half_layers:
            grad_quant_low = grad_stream.astype(jnp.bfloat16)
            grad_upw = jnp.einsum(
                "tl,td->dl", quant_low, grad_quant_low, preferred_element_type=jnp.float32
            )
            grad_quant = jnp.einsum(
                "td,dl->tl", grad_quant_low, up_proj, preferred_element_type=jnp.float32
            )
            commit_grad = valid_mask[:, None] * (2.0 * commit_weight) * commit_gap
            (grad_latent,) = unit_back(grad_quant + commit_grad)
            grad_latent_low = grad_latent.astype(jnp.bfloat16)
            grad_downw = jnp.einsum(
                "td,tl->dl", encoder_low, grad_latent_low, preferred_element_type=jnp.float32
            )
            grad_stream = jnp.einsum(
                "tl,dl->td", grad_latent_low, down_proj, preferred_element_type=jnp.float32
            )
            grad_encoded = jax.ops.segment_sum(-commit_grad, code_row, num_segments=CODES)
            (grad_codes,) = encoded_back(grad_encoded)
    grad_embed_low = grad_stream.astype(jnp.bfloat16)
    grad_embed = jnp.einsum(
        "tp,td->dp", patch_low, grad_embed_low, preferred_element_type=jnp.float32
    )
    grad_edges = jnp.concatenate(
        [
            grad_embed,
            grad_head,
            grad_downw,
            grad_upw,
            grad_final_gain[:, None],
            grad_final_shift[:, None],
        ],
        axis=1,
    )
    gpr_low = real_back((-valid_mask * jax.nn.sigmoid(-real_logits))[:, None] * readout)[0].astype(
        jnp.bfloat16
    )
    gpf_low = fake_back((valid_mask * jax.nn.sigmoid(fake_logits))[:, None] * readout)[0].astype(
        jnp.bfloat16
    )
    grad_mat = jnp.einsum(
        "tp,th->ph", patch_low, gpr_low, preferred_element_type=jnp.float32
    ) + jnp.einsum("tp,th->ph", rebuilt_low, gpf_low, preferred_element_type=jnp.float32)
    grad_bias = jnp.sum(gpr_low.astype(jnp.float32), axis=0) + jnp.sum(
        gpf_low.astype(jnp.float32), axis=0
    )
    grad_readout = jnp.sum(
        (-valid_mask * jax.nn.sigmoid(-real_logits))[:, None] * act_real
        + (valid_mask * jax.nn.sigmoid(fake_logits))[:, None] * act_fake,
        axis=0,
    )
    scalars = jnp.pad(jnp.stack([starts, gen_local, critic_local])[None], ((0, 0), (0, D - 3)))
    critic_block = jnp.concatenate([grad_mat, grad_bias[None], grad_readout[None], scalars], axis=0)
    gains_rows = jnp.concatenate([parts[2][:9] for parts in layer_parts], axis=0).T
    edge_block = jnp.concatenate(
        [grad_edges, gains_rows, jnp.zeros((D, EDGE_WIDE - EDGE - gain_count), jnp.float32)], axis=1
    ).astype(jnp.bfloat16)
    blocks = layer_parts[0][:2] + [edge_block, grad_codes.astype(jnp.bfloat16).reshape(-1, 128)]
    totals, critic_all, square_sum = reduce_all(ready, blocks, critic_block, n_chip, n_dp, 2)
    joined = [
        join_owned(parts, block.shape[0] // (2 * n_chip), block.shape[1]).astype(jnp.float32)
        for parts, block in zip(totals, layer_parts[1][:2] + blocks)
    ]
    images, gen_total, critic_total = (critic_all[PIX + 2, place] for place in range(3))
    edge_total = joined[2 * LAYERS]
    reduced = (
        jnp.stack([joined[2 * (LAYERS - 1 - layer_idx)] for layer_idx in range(LAYERS)]),
        jnp.stack([joined[2 * (LAYERS - 1 - layer_idx) + 1] for layer_idx in range(LAYERS)]),
        edge_total[:, EDGE : EDGE + gain_count].T.reshape(LAYERS, 9, owned),
        edge_total[:, :EDGE],
        joined[2 * LAYERS + 1].reshape(-1, LAT),
    )
    critic_grad = critic_all[: PIX + 2]
    scaled = [gradient / images for gradient in reduced]
    grad_norm = jnp.sqrt(square_sum) / images
    factor = jnp.minimum(1.0, clip_norm / grad_norm)
    new_attn = adam_update(attn_weights, scaled[0] * factor, attn_first, attn_second)
    new_mlp = adam_update(mlp_weights, scaled[1] * factor, mlp_first, mlp_second)
    new_gains = adam_update(layer_gains, scaled[2] * factor, gains_first, gains_second)
    new_edges = adam_update(edge_weights, scaled[3] * factor, edges_first, edges_second)
    new_codes = adam_update(codebook, scaled[4] * factor, codebook_first, codebook_second)
    new_critic = adam_update(critic_weights, critic_grad / images, critic_first, critic_second)
    losses = jnp.stack([gen_total / images, critic_total / images])
    return (
        new_attn[0],
        new_attn[1],
        new_attn[2],
        new_mlp[0],
        new_mlp[1],
        new_mlp[2],
        new_gains[0],
        new_gains[1],
        new_gains[2],
        new_edges[0],
        new_edges[1],
        new_edges[2],
        new_codes[0],
        new_codes[1],
        new_codes[2],
        new_critic[0],
        new_critic[1],
        new_critic[2],
        losses,
        grad_norm,
        new_attn[0].astype(jnp.bfloat16),
        new_mlp[0].astype(jnp.bfloat16),
        new_edges[0].astype(jnp.bfloat16),
        new_codes[0].astype(jnp.bfloat16),
    )


def solution(mesh):
    return jax.shard_map(
        functools.partial(per_device, mesh),
        mesh=mesh,
        in_specs=(
            P(("fsdp", "dp"), None, None),
            P(("fsdp", "dp"), None),
            P(("fsdp", "dp"), None),
            P(("fsdp", "dp"), None),
            P(("fsdp", "dp"), None),
            P(None, "fsdp", None),
            P(None, "fsdp", None),
            P(None, None, "fsdp"),
            P("fsdp", None),
            P("fsdp", None),
            P(),
            P(None, "fsdp", None),
            P(None, "fsdp", None),
            P(None, "fsdp", None),
            P(None, "fsdp", None),
            P(None, None, "fsdp"),
            P(None, None, "fsdp"),
            P("fsdp", None),
            P("fsdp", None),
            P("fsdp", None),
            P("fsdp", None),
            P(),
            P(),
        ),
        out_specs=(
            P(None, "fsdp", None),
            P(None, "fsdp", None),
            P(None, "fsdp", None),
            P(None, "fsdp", None),
            P(None, "fsdp", None),
            P(None, "fsdp", None),
            P(None, None, "fsdp"),
            P(None, None, "fsdp"),
            P(None, None, "fsdp"),
            P("fsdp", None),
            P("fsdp", None),
            P("fsdp", None),
            P("fsdp", None),
            P("fsdp", None),
            P("fsdp", None),
            P(),
            P(),
            P(),
            P(),
            P(),
            P(None, "fsdp", None),
            P(None, "fsdp", None),
            P("fsdp", None),
            P("fsdp", None),
        ),
        check_vma=False,
    )
```

```python
import functools
import math

import jax
import jax.numpy as jnp
import numpy as np
from jax import lax
from jax.experimental import pallas as pl
from jax.experimental.pallas import tpu as pltpu
from jax.sharding import PartitionSpec as P

MESH = pl.DeviceIdType.MESH
D = 512
HEADS = 8
HEAD = 64
FF = 2048
LAT = 32
CODES = 8192
PIX = 192
LAYERS = 2
TILE = 256
REACH = 256
PAIRS = HEADS // 2
EDGE = 2 * PIX + 2 * LAT + 2
GAINS = 9
PIX_WIDE = 256
SIDE = 2 * PIX_WIDE
EDGE_WIDE = SIDE + 128
GAIN_ROW = 2 * LAT + 2
CODE_ROWS = CODES * LAT // 128
CRITIC_ROWS = 200


beta_one = 0.9
beta_two = 0.95
adam_eps = 1e-08
decay_rate = 0.1
learn_rate = 0.2
clip_norm = 0.5
commit_weight = 0.25
adverse_weight = 0.2
adam_step = 10.0
norm_eps = 1e-05
excluded = -1e30
kernel_vmem = 61 << 20


def feature_table():
    pixel_idx = np.arange(PIX, dtype=np.float64)[:, None]
    frequency = np.arange(PIX, dtype=np.float64)[None, :]
    table = np.cos(np.pi * (pixel_idx + 0.5) * frequency / PIX) * (math.sqrt(2.0 / PIX) / (1.0 + frequency / 16.0))
    return np.pad(table.astype(np.float32), ((0, PIX_WIDE - PIX), (0, PIX_WIDE - PIX)))


def dot_over(left_side, right_side, left_dim, right_dim, precision=None):
    return lax.dot_general(
        left_side,
        right_side,
        (((left_dim,), (right_dim,)), ((), ())),
        precision=precision,
        preferred_element_type=jnp.float32,
    )


def dot_nn(left_side, right_side):
    return dot_over(left_side, right_side, 1, 0)


def dot_nt(left_side, right_side):
    return dot_over(left_side, right_side, 1, 1)


def dot_tn(left_side, right_side):
    return dot_over(left_side, right_side, 0, 0)


def low(values):
    return values.astype(jnp.bfloat16)


def wide(values):
    return values.astype(jnp.float32)


def center_rows(values):
    center = values - jnp.mean(values, axis=-1, keepdims=True)
    spread = jnp.mean(center * center, axis=-1, keepdims=True)
    scale = lax.rsqrt(spread + norm_eps)
    return center * scale, scale


def norm_rows_back(grad, unit, scale, gain):
    grad_unit = grad * gain
    mean_grad = jnp.mean(grad_unit, axis=-1, keepdims=True)
    mean_along = jnp.mean(grad_unit * unit, axis=-1, keepdims=True)
    return scale * (grad_unit - mean_grad - unit * mean_along)


def unit_scale(values):
    return lax.rsqrt(jnp.sum(values * values, axis=-1, keepdims=True) + 1.0)


def unit_back(grad, values, scale):
    return scale * grad - values * (scale * scale * scale * jnp.sum(values * grad, axis=-1, keepdims=True))


def gelu_tanh(values):
    cubic_term = values + 0.044715 * values * values * values
    return 0.5 * values * (1.0 + jnp.tanh(0.7978845608028654 * cubic_term))


def gelu_slope(values):
    square = values * values
    bend = jnp.tanh(0.7978845608028654 * values * (1.0 + 0.044715 * square))
    half_up = 0.5 + 0.5 * bend
    slope = half_up + 0.5 * values * (1.0 - bend * bend) * (
        0.7978845608028654 + (0.7978845608028654 * 3.0 * 0.044715) * square
    )
    return values * half_up, slope


def softplus(values):
    return jnp.maximum(values, 0.0) + jnp.log(1.0 + jnp.exp(-jnp.abs(values)))


def sigmoid(values):
    return 1.0 / (1.0 + jnp.exp(-values))


def lane_ids(shape):
    return lax.broadcasted_iota(jnp.int32, shape, 1)


def sum_rows(values):
    return jnp.sum(values, axis=0, keepdims=True)


def sum_all(values):
    return jnp.sum(jnp.sum(values, axis=0, keepdims=True), axis=1, keepdims=True)


def key_window(tile_idx, length):
    start = tile_idx * TILE
    return max(0, start - REACH), min(length, start + TILE + REACH)


def rows_at(tile_idx):
    return pl.ds(pl.multiple_of(tile_idx * TILE, TILE), TILE)


def split_pair(array):
    low_half = lane_ids(array.shape) < HEAD
    zero = jnp.zeros_like(array)
    return jnp.where(low_half, array, zero), jnp.where(low_half, zero, array)


def spread_latent(values):
    return values + pltpu.roll(values, 32, 1) + pltpu.roll(values, 64, 1) + pltpu.roll(values, 96, 1)


def weight_columns(ref, first, width):
    return ref[:, :, :, pl.ds(first, width)].reshape(D, width)


def add_parts(terms, kind):
    total = wide(terms[0])
    for term in terms[1:]:
        total = total + wide(term)
    return total.astype(kind)


def no_tick(name):
    pass


class Places:
    def __init__(self, n_chip, n_dp):
        self.n_chip, self.n_dp = n_chip, n_dp
        self.place = lax.axis_index("fsdp")
        self.plane = lax.axis_index("dp")
        self.core = lax.rem(self.place, 2)
        self.chip = lax.div(self.place, 2)

    def sibling(self):
        return {"fsdp": self.place + 1 - 2 * self.core}

    def chip_at(self, j):
        return lax.rem(self.chip + j, self.n_chip)

    def same_core(self, j):
        return {"fsdp": self.chip_at(j) * 2 + self.core}

    def plane_at(self, t):
        return lax.rem(self.plane + t, self.n_dp)

    def same_place(self, t):
        return {"dp": self.plane_at(t)}

    def greet(self, devices):
        barrier = pltpu.get_barrier_semaphore()
        for device in devices:
            pl.semaphore_signal(barrier, inc=1, device_id=device, device_id_type=MESH)
        pl.semaphore_wait(barrier, len(devices))

    def plane_devices(self):
        return [self.sibling()] + [self.same_core(j) for j in range(1, self.n_chip)]


def remote(source, target, send, recv, device):
    return pltpu.make_async_remote_copy(
        src_ref=source, dst_ref=target, send_sem=send, recv_sem=recv, device_id=device, device_id_type=MESH
    )


class Gather:
    def __init__(self, places, shards, outs, sems):
        self.places, self.shards, self.outs = places, shards, outs
        self.local_sem, self.chip_send, self.chip_recv, self.pair_send, self.pair_recv = sems

    @staticmethod
    def semaphores(count, n_chip):
        dma = pltpu.SemaphoreType.DMA
        return [dma((count,))] + [dma((count, n_chip - 1))] * 2 + [dma((count, n_chip))] * 2

    def local_copy(self, a):
        mine = self.outs[a].at[self.places.chip, self.places.core]
        return pltpu.make_async_copy(self.shards[a], mine, self.local_sem.at[a])

    def chip_copy(self, a, j):
        mine = self.outs[a].at[self.places.chip, self.places.core]
        sems = (self.chip_send.at[a, j - 1], self.chip_recv.at[a, j - 1])
        return remote(self.shards[a], mine, *sems, self.places.same_core(j))

    def pair_copy(self, a, j):
        n_chip = self.places.n_chip
        block = self.outs[a].at[lax.rem(self.places.chip + n_chip - j, n_chip), self.places.core]
        source = self.shards[a] if j == 0 else block
        return remote(source, block, self.pair_send.at[a, j], self.pair_recv.at[a, j], self.places.sibling())

    def start(self, a):
        for j in range(1, self.places.n_chip):
            self.chip_copy(a, j).start()
        self.pair_copy(a, 0).start()
        self.local_copy(a).start()

    def forward(self, a):
        for j in range(1, self.places.n_chip):
            self.chip_copy(a, j).wait_recv()
            self.pair_copy(a, j).start()

    def finish(self, a):
        self.local_copy(a).wait()
        for j in range(self.places.n_chip):
            self.pair_copy(a, j).wait()
            if j > 0:
                self.chip_copy(a, j).wait_send()


class PlaneReduce:
    def __init__(self, places, ins, pair_in, sums, chip_in, sems):
        self.places, self.ins, self.pair_in, self.sums, self.chip_in = places, ins, pair_in, sums, chip_in
        self.pair_send, self.pair_recv, self.local_sem, self.chip_send, self.chip_recv = sems

    @staticmethod
    def scratch(arrays, n_chip, n_dp):
        shapes = []
        for outer in (n_chip, n_chip, n_chip - 1):
            shapes += [pltpu.VMEM((outer, n_dp) + a.shape[3:], a.dtype) for a in arrays]
        count, dma = len(arrays), pltpu.SemaphoreType.DMA
        return shapes, [dma((count,))] * 3 + [dma((count, n_chip - 1))] * 2

    def pair_copy(self, a):
        source = self.ins[a].at[:, 1 - self.places.core]
        return remote(source, self.pair_in[a], self.pair_send.at[a], self.pair_recv.at[a], self.places.sibling())

    def local_copy(self, a):
        return pltpu.make_async_copy(self.ins[a].at[:, self.places.core], self.sums[a], self.local_sem.at[a])

    def chip_copy(self, a, j):
        sems = (self.chip_send.at[a, j - 1], self.chip_recv.at[a, j - 1])
        source = self.sums[a].at[self.places.chip_at(j)]
        return remote(source, self.chip_in[a].at[j - 1], *sems, self.places.same_core(j))

    def start(self, a):
        self.pair_copy(a).start()
        self.local_copy(a).start()

    def add_pair(self, a):
        n_chip, n_dp = self.places.n_chip, self.places.n_dp
        self.pair_copy(a).wait()
        self.local_copy(a).wait()

        def body(i, carry):
            c, d = lax.div(i, n_dp), lax.rem(i, n_dp)
            self.sums[a][c, d] = add_parts([self.sums[a][c, d], self.pair_in[a][c, d]], self.ins[a].dtype)
            return carry

        lax.fori_loop(0, n_chip * n_dp, body, 0)
        for j in range(1, n_chip):
            self.chip_copy(a, j).start()

    def add_chips(self, a, part):
        n_chip, n_dp = self.places.n_chip, self.places.n_dp
        for j in range(1, n_chip):
            self.chip_copy(a, j).wait()

        def body(d, carry):
            terms = [self.sums[a][self.places.chip, d]] + [self.chip_in[a][j, d] for j in range(n_chip - 1)]
            part[d] = add_parts(terms, self.ins[a].dtype)
            return carry

        lax.fori_loop(0, n_dp, body, 0)


class PlaceReduce:
    def __init__(self, places, parts, copy_in, outs, sems):
        self.places, self.parts, self.copy_in, self.outs = places, parts, copy_in, outs
        self.rs_send, self.rs_recv, self.ag_send, self.ag_recv = sems

    @staticmethod
    def scratch(parts, n_dp):
        shapes = [pltpu.VMEM((n_dp - 1,) + p.shape[1:], p.dtype) for p in parts]
        return shapes, [pltpu.SemaphoreType.DMA((len(parts), n_dp - 1))] * 4

    def rs_copy(self, a, t):
        sems = (self.rs_send.at[a, t - 1], self.rs_recv.at[a, t - 1])
        source = self.parts[a].at[self.places.plane_at(t)]
        return remote(source, self.copy_in[a].at[t - 1], *sems, self.places.same_place(t))

    def ag_copy(self, a, t):
        sems = (self.ag_send.at[a, t - 1], self.ag_recv.at[a, t - 1])
        mine = self.outs[a].at[self.places.plane]
        return remote(mine, mine, *sems, self.places.same_place(t))

    def start(self, a):
        for t in range(1, self.places.n_dp):
            self.rs_copy(a, t).start()

    def add_copies(self, a):
        n_dp, plane = self.places.n_dp, self.places.plane
        for t in range(1, n_dp):
            self.rs_copy(a, t).wait()
        terms = [self.parts[a][plane]] + [self.copy_in[a][t] for t in range(n_dp - 1)]
        total = add_parts(terms, self.outs[a].dtype)
        self.outs[a][plane] = total
        for t in range(1, n_dp):
            self.ag_copy(a, t).start()
        return sum_all(wide(total) * wide(total))

    def finish(self, a):
        for t in range(1, self.places.n_dp):
            self.ag_copy(a, t).wait()


def part_shapes(arrays, n_dp):
    return [jax.ShapeDtypeStruct((n_dp,) + a.shape[3:], a.dtype) for a in arrays]


class Owners:
    def __init__(self, n_chip, n_dp, rows, columns):
        self.owned = rows // (2 * n_chip)
        self.by_rows = self.owned % (16 * n_dp) == 0 or columns % (128 * n_dp) != 0
        tail = (self.owned // n_dp, columns) if self.by_rows else (self.owned, columns // n_dp)
        self.outer, self.columns, self.tail = (n_chip, 2, n_dp), columns, tail
        self.shape = jax.ShapeDtypeStruct(self.outer + tail, jnp.bfloat16)

    def store(self, ref, first, values):
        n_chip, _, n_dp = self.outer
        width = values.shape[1]
        if self.by_rows:
            ref[:, :, :, :, pl.ds(first, width)] = low(values.reshape(self.outer + (self.tail[0], width)))
            return
        step = min(width, self.tail[1])
        for shift in range(0, width, step):
            part, inside = divmod(first + shift, self.tail[1])
            block = values[:, shift : shift + step].reshape(n_chip, 2, self.owned, step)
            ref[:, :, part, :, pl.ds(inside, step)] = low(block)

    def join(self, parts):
        if self.by_rows:
            return parts.reshape(self.owned, self.columns)
        return parts.transpose(1, 0, 2).reshape(self.owned, self.columns)


def critic_rows(inputs_low, critic_mat, bias, readout):
    active, slope = gelu_slope(dot_nn(inputs_low, critic_mat) + bias)
    return active, slope * readout, jnp.sum(active * readout, axis=-1, keepdims=True)


def load_critic(critic, critic_mat):
    critic_mat[...] = jnp.zeros_like(critic_mat)
    critic_mat[0:PIX, :] = low(critic[0:PIX, :])


def start_kernel(n_chip, n_dp, *refs):
    refs = list(refs)
    take = lambda size: [refs.pop(0) for _ in range(size)]
    edge_low, attn, mlp, patches, critic, info_row, info_col = take(7)
    edge_all, attn_all, attn_low, mlp_low, critic_part = take(5)
    critic_mat, grad_real = take(2)
    places = Places(n_chip, n_dp)
    places.greet(places.plane_devices())
    gather = Gather(places, [edge_low, attn_low.at[0]], [edge_all, attn_all], refs)
    gather.start(0)
    attn_low[0] = low(attn[0])
    gather.start(1)
    for l in range(1, LAYERS):
        attn_low[l] = low(attn[l])
    for l in range(LAYERS):
        mlp_low[l] = low(mlp[l])
    load_critic(critic, critic_mat)
    length = patches.shape[0]

    def real_tile(t, carry):
        loss, bias_sum, read_sum = carry
        rows = rows_at(t)
        active, slope, logit = critic_rows(
            patches[rows, :], critic_mat[...], critic[PIX : PIX + 1, :], critic[PIX + 1 : PIX + 2, :]
        )
        valid = wide(info_col[rows, 2:3])
        weight = -valid * sigmoid(-logit)
        grad = low(weight * slope)
        grad_real[rows, :] = grad
        return (
            loss + sum_all(valid * softplus(-logit)),
            bias_sum + sum_rows(wide(grad)),
            read_sum + sum_rows(weight * active),
        )

    row = jnp.zeros((1, D), jnp.float32)
    loss, bias_sum, read_sum = lax.fori_loop(0, length // TILE, real_tile, (jnp.zeros((1, 1), jnp.float32), row, row))
    gather.forward(0)
    critic_part[0:PIX, :] = dot_tn(patches[...], grad_real[...])[0:PIX, :]
    images = info_row[4:5, :]
    before = pltpu.roll(images, 1, 1)
    first = (images != before) | (lane_ids(images.shape) == 0)
    starts = sum_all(jnp.where(first & (info_row[2:3, :] > 0), 1.0, 0.0))
    lanes = lane_ids((1, D))
    scalars = jnp.where(lanes == 0, starts, jnp.where(lanes == 2, loss, 0.0))
    critic_part[PIX:CRITIC_ROWS, :] = jnp.concatenate(
        [bias_sum, read_sum, scalars, jnp.zeros((CRITIC_ROWS - PIX - 3, D), jnp.float32)], axis=0
    )
    gather.forward(1)
    gather.finish(0)
    gather.finish(1)


def block_forward(
    stream, attn, mlp, gain, info_row, info_col, mixed, context, logsum, middle, bias, active, write, tick
):
    length = stream.shape[0]
    tiles = length // TILE

    def mix_tile(t, carry):
        unit, _ = center_rows(stream[rows_at(t), :])
        hidden = low(unit * gain(0) + gain(1))
        for part in range(3):
            mixed[rows_at(t), pl.ds(part * D, D)] = low(dot_nn(hidden, weight_columns(attn, part * D, D)))
        return carry

    lax.fori_loop(0, tiles, mix_tile, 0)
    tick("mixed")
    for t in range(tiles):
        first, last = key_window(t, length)
        span = last - first
        rows = pl.ds(t * TILE, TILE)
        window = pl.ds(first, span)
        row_place = t * TILE + lax.broadcasted_iota(jnp.int32, (TILE, span), 0)
        key_place = first + lax.broadcasted_iota(jnp.int32, (TILE, span), 1)
        allowed = (info_col[rows, 0:1] == info_row[1:2, window]) | (row_place == key_place)
        bias[:, 0:span] = jnp.where(allowed, 0.0, excluded)

        def pair_step(pair, sums):
            lanes = pl.ds(pl.multiple_of(pair * 128, 128), 128)
            key_lanes = pl.ds(pl.multiple_of(D + pair * 128, 128), 128)
            value_lanes = pl.ds(pl.multiple_of(2 * D + pair * 128, 128), 128)
            queries = split_pair(mixed[rows, lanes] * jnp.bfloat16(HEAD**-0.5))
            keys = mixed[window, key_lanes]
            values = split_pair(mixed[window, value_lanes])
            total = None
            head_lanes = lane_ids((TILE, 128))
            for half in range(2):
                scores = dot_nt(queries[half], keys) + bias[:, 0:span]
                peak = jnp.max(scores, axis=-1, keepdims=True)
                powers = jnp.exp(scores - peak)
                weight = jnp.sum(powers, axis=-1, keepdims=True)
                probs = low(powers * (1.0 / weight))
                part = dot_nn(probs, values[half])
                total = part if total is None else total + part
                sums = jnp.where(head_lanes == 2 * pair + half, peak + jnp.log(weight), sums)
            context[rows, lanes] = low(total)
            return sums

        logsum[rows, :] = lax.fori_loop(0, PAIRS, pair_step, jnp.zeros((TILE, 128), jnp.float32))
    tick("context")

    def mlp_tile(t, carry):
        rows = rows_at(t)
        mid = stream[rows, :] + dot_nn(context[rows, :], weight_columns(attn, 3 * D, D))
        middle[rows, :] = mid
        unit, _ = center_rows(mid)
        hidden = low(unit * gain(2) + gain(3))
        for part in range(FF // D):
            columns = pl.ds(part * D, D)
            inner = dot_nn(hidden, weight_columns(mlp, part * D, D)) + gain(5 + part)
            active[:, columns] = low(gelu_tanh(inner))
        write(rows, mid + dot_nt(active[...], weight_columns(mlp, FF, FF)) + gain(4))
        return carry

    lax.fori_loop(0, tiles, mlp_tile, 0)


def block_backward(
    stream, attn, mlp, gain, info_row, info_col, mixed, context, logsum, middle, grad_stream, grad_input,
    store_attn, store_mlp, small, small_row, scratch, tick,
):
    branch, active, grad_inner, hidden_low, grad_out, grad_context, bias, grad_keys, grad_values = scratch
    grad_mixed = mixed
    length = stream.shape[0]
    tiles = length // TILE

    def add_row(place, values):
        small[small_row + place : small_row + place + 1, :] += sum_rows(values)

    def hidden_tile(t, carry):
        rows = rows_at(t)
        upper_low = low(grad_stream[rows, :])
        branch[rows, :] = upper_low
        add_row(4, wide(upper_low))
        unit, _ = center_rows(middle[rows, :])
        hidden_low[rows, :] = low(unit * gain(2) + gain(3))
        grad_input[rows, :] = jnp.zeros((TILE, D), jnp.float32)
        return carry

    lax.fori_loop(0, tiles, hidden_tile, 0)
    for part in range(FF // D):
        up = weight_columns(mlp, part * D, D)
        down = weight_columns(mlp, FF + part * D, D)

        def inner_tile(t, carry):
            rows = rows_at(t)
            inner = dot_nn(hidden_low[rows, :], up) + gain(5 + part)
            act, slope = gelu_slope(inner)
            active[rows, :] = low(act)
            pre_grad = low(dot_nn(branch[rows, :], down) * slope)
            grad_inner[rows, :] = pre_grad
            add_row(5 + part, wide(pre_grad))
            grad_input[rows, :] += dot_nt(pre_grad, up)
            return carry

        lax.fori_loop(0, tiles, inner_tile, 0)
        store_mlp(part * D, dot_tn(hidden_low[...], grad_inner[...]))
        store_mlp(FF + part * D, dot_tn(branch[...], active[...]))
        tick("mlp%d" % part)

    def middle_tile(t, carry):
        rows = rows_at(t)
        grad_hidden = grad_input[rows, :]
        unit, scale = center_rows(middle[rows, :])
        add_row(2, grad_hidden * unit)
        add_row(3, grad_hidden)
        grad_mid = norm_rows_back(grad_hidden, unit, scale, gain(2)) + grad_stream[rows, :]
        grad_input[rows, :] = grad_mid
        mid_low = low(grad_mid)
        grad_out[rows, :] = mid_low
        grad_context[rows, :] = low(dot_nt(mid_low, weight_columns(attn, 3 * D, D)))
        return carry

    lax.fori_loop(0, tiles, middle_tile, 0)
    store_attn(3 * D, dot_tn(context[...], grad_out[...]))
    for t in range(tiles):
        first, last = key_window(t, length)
        span = last - first
        key_place = first + lax.broadcasted_iota(jnp.int32, (span, TILE), 0)
        row_place = t * TILE + lax.broadcasted_iota(jnp.int32, (span, TILE), 1)
        same = info_col[pl.ds(first, span), 1:2] == info_row[0:1, pl.ds(t * TILE, TILE)]
        bias[t, 0:span, :] = jnp.where(same | (row_place == key_place), 0.0, excluded)
    sums_t = [logsum[pl.ds(t * TILE, TILE), :].T[0:8, :] for t in range(tiles)]
    tick("middle")

    def pair_step(pair, carry):
        lanes = pl.ds(pl.multiple_of(pair * 128, 128), 128)
        key_lanes = pl.ds(pl.multiple_of(D + pair * 128, 128), 128)
        value_lanes = pl.ds(pl.multiple_of(2 * D + pair * 128, 128), 128)
        grad_keys[...] = jnp.zeros_like(grad_keys)
        grad_values[...] = jnp.zeros_like(grad_values)
        for t in range(tiles):
            first, last = key_window(t, length)
            span = last - first
            rows = pl.ds(t * TILE, TILE)
            window = pl.ds(first, span)
            queries = split_pair(mixed[rows, lanes] * jnp.bfloat16(HEAD**-0.5))
            grads = split_pair(grad_context[rows, lanes])
            keys = mixed[window, key_lanes]
            values = mixed[window, value_lanes]
            key_halves = split_pair(keys)
            head_ids = lax.broadcasted_iota(jnp.int32, (8, TILE), 0)
            add_keys, add_values, add_queries = 0.0, 0.0, 0.0
            for half in range(2):
                sums = sum_rows(jnp.where(head_ids == 2 * pair + half, sums_t[t], 0.0))
                probs = jnp.exp(dot_nt(keys, queries[half]) + bias[t, 0:span, :] - sums)
                weighted = probs * dot_nt(values, grads[half])
                grad_scores = low(weighted - probs * sum_rows(weighted))
                add_keys = add_keys + dot_nn(grad_scores, queries[half])
                add_values = add_values + dot_nn(low(probs), grads[half])
                add_queries = add_queries + dot_tn(grad_scores, key_halves[half])
            grad_keys[window, :] += add_keys
            grad_values[window, :] += add_values
            grad_mixed[rows, lanes] = low(add_queries * HEAD**-0.5)
        grad_mixed[:, key_lanes] = low(grad_keys[...])
        grad_mixed[:, value_lanes] = low(grad_values[...])
        return carry

    half_pairs = PAIRS // 2
    lax.fori_loop(0, half_pairs, pair_step, 0)
    tick("pairs")
    lax.fori_loop(half_pairs, PAIRS, pair_step, 0)
    tick("mixed")

    def input_tile(t, carry):
        rows = rows_at(t)
        unit, scale = center_rows(stream[rows, :])
        hidden_low[rows, :] = low(unit * gain(0) + gain(1))
        grad_hidden = dot_nt(grad_mixed[rows, :], weight_columns(attn, 0, 3 * D))
        add_row(0, grad_hidden * unit)
        add_row(1, grad_hidden)
        grad_input[rows, :] += norm_rows_back(grad_hidden, unit, scale, gain(0))
        return carry

    lax.fori_loop(0, tiles, input_tile, 0)
    for part in range(3):
        store_attn(part * D, dot_tn(hidden_low[...], grad_mixed[:, pl.ds(part * D, D)]))


def side_rows(edge, side_t):
    side_t[...] = wide(weight_columns(edge, SIDE, 128)).T
    return lambda layer: lambda row: side_t[GAIN_ROW + GAINS * layer + row : GAIN_ROW + GAINS * layer + row + 1, :]


def encode_kernel(n_chip, n_dp, *refs):
    refs = list(refs)
    take = lambda size: [refs.pop(0) for _ in range(size)]
    edge, attn, patches, info_row, info_col, mlp_low, codes_low, attn_low = take(8)
    stream, mixed, context, logsum, middle, encoder_low, latent, picked, decoder_in, stats = take(10)
    mlp, codes, attn_next = take(3)
    side_t, bias, active = take(3)
    places = Places(n_chip, n_dp)
    places.greet(places.plane_devices())
    shards = [mlp_low.at[0], codes_low] + [attn_low.at[1]]
    gather = Gather(places, shards, [mlp, codes, attn_next], refs)
    gather.start(0)
    gain = side_rows(edge, side_t)(0)
    length = patches.shape[0]
    stats[...] = jnp.zeros_like(stats)

    def embed_tile(t, carry):
        stream[rows_at(t), :] = dot_nt(patches[rows_at(t), :], weight_columns(edge, 0, PIX_WIDE))
        return carry

    lax.fori_loop(0, length // TILE, embed_tile, 0)

    def tick(name):
        if name == "context":
            gather.forward(0)
            gather.start(1)
            gather.start(2)
            gather.finish(0)

    def write(rows, output):
        encoder_low[rows, :] = low(output)

    block_forward(
        stream, attn, mlp, gain, info_row, info_col, mixed, context, logsum, middle, bias, active, write, tick
    )
    gather.forward(1)
    gather.finish(1)
    table = codes[...].reshape(CODE_ROWS, 128)

    def quantize_tile(t, carry):
        rows = rows_at(t)
        side = weight_columns(edge, SIDE, 128)
        lanes = lane_ids((TILE, 128))
        latent_rows = jnp.where(lanes < LAT, dot_nn(encoder_low[rows, :], side), 0.0)
        latent[rows, :] = latent_rows
        code_row, code_lane = info_col[rows, 3:4], info_col[rows, 4:5]
        found = jnp.zeros((TILE, 128), jnp.float32)
        for first in range(0, CODE_ROWS, D):
            hit = lane_ids((TILE, D)) + first == code_row
            found = found + dot_nn(low(jnp.where(hit, 1.0, 0.0)), table[first : first + D, :])
        found = spread_latent(jnp.where(lax.div(lanes, LAT) == code_lane, found, 0.0))
        found = jnp.where(lanes < LAT, found, 0.0)
        picked[rows, :] = found
        unit = latent_rows * unit_scale(latent_rows)
        chosen = found * unit_scale(found)
        gap = unit - chosen
        stats[0:1, :] += sum_all(wide(info_col[rows, 2:3]) * jnp.sum(gap * gap, axis=-1, keepdims=True))
        quantized = unit + (chosen - unit)
        decoder_in[rows, :] = dot_nt(low(pltpu.roll(quantized, LAT, 1)), side)
        return carry

    lax.fori_loop(0, length // TILE, quantize_tile, 0)
    gather.forward(2)
    gather.finish(2)


def decode_kernel(n_chip, n_dp, attn_owners, mlp_owners, *refs):
    refs = list(refs)
    take = lambda size: [refs.pop(0) for _ in range(size)]
    decoder_in, edge, attn, patches, info_row, info_col, critic, critic_part, stats, table, mlp_low = take(11)
    grad_decoder, grad_attn, mlp_part, grad_head, small, critic_block = take(6)
    mlp, side_t, critic_mat, mixed, context, logsum, middle, last_stream, grad_last, grad_mlp = take(10)
    normed_low, rebuilt_low, grad_rebuilt_low, forward_bias, forward_active = take(5)
    scratch = take(9)
    pair_in, sums, chip_in = take(1), take(1), take(1)
    places = Places(n_chip, n_dp)
    places.greet(places.plane_devices())
    gather = Gather(places, [mlp_low.at[1]], [mlp], refs[:5])
    planes = PlaneReduce(places, [grad_mlp], pair_in, sums, chip_in, refs[5:])
    gather.start(0)
    gain = side_rows(edge, side_t)(LAYERS - 1)
    load_critic(critic, critic_mat)
    length = patches.shape[0]

    def forward_tick(name):
        if name == "context":
            gather.forward(0)
            gather.finish(0)

    def write(rows, output):
        last_stream[rows, :] = output

    grad_fake = scratch[0]
    block_forward(
        decoder_in, attn, mlp, gain, info_row, info_col, mixed, context, logsum, middle, forward_bias,
        forward_active, write, forward_tick,
    )
    small[...] = jnp.zeros_like(small)

    def head_tile(t, carry):
        feature, adverse, fake_loss, bias_sum, read_sum = carry
        rows = rows_at(t)
        final_gain, final_shift = side_t[2 * LAT : 2 * LAT + 1, :], side_t[2 * LAT + 1 : 2 * LAT + 2, :]
        unit, scale = center_rows(last_stream[rows, :])
        normed = low(unit * final_gain + final_shift)
        normed_low[rows, :] = normed
        head = weight_columns(edge, PIX_WIDE, PIX_WIDE)
        rebuilt = dot_nn(normed, head)
        valid = wide(info_col[rows, 2:3])
        exact = lax.Precision.HIGHEST
        difference = dot_over(rebuilt - wide(patches[rows, :]), table[...], 1, 0, exact)
        feature = feature + sum_all(valid * jnp.sum(difference * difference, axis=-1, keepdims=True)) * (1.0 / PIX)
        grad_feature = dot_over(valid * (2.0 / PIX) * difference, table[...], 1, 1, exact)
        rebuilt_rows = low(rebuilt)
        rebuilt_low[rows, :] = rebuilt_rows
        act, slope, logit = critic_rows(
            rebuilt_rows, critic_mat[...], critic[PIX : PIX + 1, :], critic[PIX + 1 : PIX + 2, :]
        )
        adverse = adverse + sum_all(valid * softplus(-logit))
        fake_loss = fake_loss + sum_all(valid * softplus(logit))
        weight = valid * sigmoid(logit)
        grad_critic = low(weight * slope)
        grad_fake[rows, :] = grad_critic
        bias_sum = bias_sum + sum_rows(wide(grad_critic))
        read_sum = read_sum + sum_rows(weight * act)
        grad_pre = low((-adverse_weight) * valid * sigmoid(-logit) * slope)
        grad_rebuilt = low(grad_feature + dot_nt(grad_pre, critic_mat[...]))
        grad_rebuilt_low[rows, :] = grad_rebuilt
        grad_normed = dot_nt(grad_rebuilt, head)
        small[2 * LAT : 2 * LAT + 1, :] += sum_rows(grad_normed * unit)
        small[2 * LAT + 1 : 2 * LAT + 2, :] += sum_rows(grad_normed)
        grad_last[rows, :] = norm_rows_back(grad_normed, unit, scale, final_gain)
        return feature, adverse, fake_loss, bias_sum, read_sum

    one, row = jnp.zeros((1, 1), jnp.float32), jnp.zeros((1, D), jnp.float32)
    feature, adverse, fake_loss, bias_sum, read_sum = lax.fori_loop(
        0, length // TILE, head_tile, (one, one, one, row, row)
    )
    grad_head[...] = low(dot_tn(normed_low[...], grad_rebuilt_low[...]))
    critic_block[0:PIX, :] = critic_part[0:PIX, :] + dot_tn(rebuilt_low[...], grad_fake[...])[0:PIX, :]
    lanes = lane_ids((1, D))
    gen_local = feature + adverse_weight * adverse + commit_weight * stats[0:1, 0:1]
    scalars = jnp.where(lanes == 1, gen_local, jnp.where(lanes == 2, fake_loss, 0.0))
    rest = CRITIC_ROWS - PIX - 3
    critic_block[PIX:CRITIC_ROWS, :] = critic_part[PIX:CRITIC_ROWS, :] + jnp.concatenate(
        [bias_sum, read_sum, scalars, jnp.zeros((rest, D), jnp.float32)], axis=0
    )
    if critic_block.shape[0] > CRITIC_ROWS:
        critic_block[CRITIC_ROWS:, :] = jnp.zeros((critic_block.shape[0] - CRITIC_ROWS, D), jnp.float32)

    def tick(name):
        if name == "mlp3":
            planes.start(0)
        if name == "middle":
            planes.add_pair(0)

    block_backward(
        decoder_in, attn, mlp, gain, info_row, info_col, mixed, context, logsum, middle, grad_last, grad_decoder,
        functools.partial(attn_owners.store, grad_attn), functools.partial(mlp_owners.store, grad_mlp),
        small, GAIN_ROW + GAINS * (LAYERS - 1), scratch, tick,
    )
    planes.add_chips(0, mlp_part)


def finish_kernel(n_chip, n_dp, attn_owners, mlp_owners, edge_owners, code_owners, *refs):
    refs = list(refs)
    take = lambda size: [refs.pop(0) for _ in range(size)]
    stream, context, logsum, middle, encoder_low, latent, picked = take(7)
    attn, mlp, edge, patches, info_row, info_col, grad_head, small_in = take(8)
    mlp_part, mixed_in, grad_decoder, attn_later, critic_block = take(5)
    grad_attn, grad_edge, grad_codes, first_part, mlp_total, attn_total, critic_out, norm = take(8)
    side_t, small, grad_mlp, mixed, grad_input, grad_encoder, code_grads = take(7)
    scratch = take(9)
    pair_in, sums, chip_in = take(3), take(3), take(3)
    parts = take(2)
    copy_in = take(3)
    critic_sum = take(1)[0]
    plane_sems, place_sems = take(5), take(4)
    spread_send, spread_recv, mirror_send, mirror_recv, load_sem = refs
    places = Places(n_chip, n_dp)
    places.greet(places.plane_devices() + [places.same_place(t) for t in range(1, n_dp)])
    planes = PlaneReduce(places, [attn_later, critic_block, grad_mlp], pair_in, sums, chip_in, plane_sems)
    copies = PlaceReduce(
        places, [mlp_part] + parts, copy_in, [mlp_total, attn_total, critic_sum], place_sems
    )
    chip, core = places.chip, places.core

    def spread_copy(j):
        sems = (spread_send.at[j - 1], spread_recv.at[j - 1])
        return remote(critic_sum, critic_out.at[chip, core], *sems, places.same_core(j))

    def mirror_copy():
        return remote(critic_out.at[:, core], critic_out.at[:, core], mirror_send, mirror_recv, places.sibling())

    loads = [
        pltpu.make_async_copy(grad_decoder, grad_encoder, load_sem.at[0]),
        pltpu.make_async_copy(mixed_in, mixed, load_sem.at[1]),
    ]
    for load in loads:
        load.start()
    planes.start(0)
    planes.start(1)
    copies.start(0)
    gain = side_rows(edge, side_t)(0)
    small[...] = small_in[...]
    norm[...] = jnp.zeros_like(norm)
    grad_edge[...] = jnp.zeros_like(grad_edge)
    length = patches.shape[0]

    for load in loads:
        load.wait()

    def latent_tile(t, carry):
        grad_up, grad_down = carry
        rows = rows_at(t)
        side = weight_columns(edge, SIDE, 128)
        lanes = lane_ids((TILE, 128))
        latent_rows, found = latent[rows, :], picked[rows, :]
        scale, code_scale = unit_scale(latent_rows), unit_scale(found)
        unit, chosen = latent_rows * scale, found * code_scale
        quantized = low(pltpu.roll(unit + (chosen - unit), LAT, 1))
        grad_low = low(grad_encoder[rows, :])
        grad_up = grad_up + dot_tn(grad_low, quantized)
        grad_unit = jnp.where(lanes < LAT, pltpu.roll(dot_nn(grad_low, side), 128 - LAT, 1), 0.0)
        commit_grad = wide(info_col[rows, 2:3]) * (2.0 * commit_weight) * (unit - chosen)
        grad_latent = low(unit_back(grad_unit + commit_grad, latent_rows, scale))
        grad_down = grad_down + dot_tn(encoder_low[rows, :], grad_latent)
        grad_encoder[rows, :] = dot_nt(grad_latent, side)
        code_grad = spread_latent(unit_back(-commit_grad, found, code_scale))
        code_grad = jnp.where(lax.div(lanes, LAT) == info_col[rows, 4:5], code_grad, 0.0)
        upper = low(code_grad)
        code_grads[rows, 0:128] = upper
        code_grads[rows, 128:256] = low(code_grad - wide(upper))
        return grad_up, grad_down

    empty = jnp.zeros((D, 128), jnp.float32)
    grad_up, grad_down = lax.fori_loop(0, length // TILE, latent_tile, (empty, empty))
    side_grad = grad_up + grad_down
    code_rows = code_owners.owned

    def code_step(place, carry):
        hit = lax.broadcasted_iota(jnp.int32, (code_rows, length), 0) + place * code_rows == info_row[3:4, :]
        sums_two = dot_nn(low(jnp.where(hit, 1.0, 0.0)), code_grads[...])
        total = sums_two[:, 0:128] + sums_two[:, 128:256]
        grad_codes[lax.div(place, 2), lax.rem(place, 2)] = low(total.reshape((n_dp,) + code_owners.tail))
        return carry

    lax.fori_loop(0, 2 * n_chip, code_step, 0)
    planes.add_pair(0)
    planes.add_pair(1)

    def tick(name):
        if name == "mlp0":
            norm[0:1, :] += copies.add_copies(0)
        if name == "mlp3":
            planes.start(2)
            planes.add_chips(0, parts[0])
            copies.start(1)
            planes.add_chips(1, parts[1])
            copies.start(2)
        if name == "middle":
            planes.add_pair(2)
            copies.add_copies(2)
            norm[0:1, :] += copies.add_copies(1)
        if name == "pairs":
            copies.finish(2)
            critic_out[chip, core] = critic_sum[...]
            for j in range(1, n_chip):
                spread_copy(j).start()
        if name == "mixed":
            for j in range(1, n_chip):
                spread_copy(j).wait()
            mirror_copy().start()

    block_backward(
        stream, attn, mlp, gain, info_row, info_col, mixed, context, logsum, middle, grad_encoder, grad_input,
        functools.partial(attn_owners.store, grad_attn), functools.partial(mlp_owners.store, grad_mlp),
        small, GAIN_ROW, scratch, tick,
    )
    branch = scratch[0]

    def low_tile(t, carry):
        branch[rows_at(t), :] = low(grad_input[rows_at(t), :])
        return carry

    lax.fori_loop(0, length // TILE, low_tile, 0)
    edge_owners.store(grad_edge, 0, dot_tn(branch[...], patches[...]))
    edge_owners.store(grad_edge, PIX_WIDE, wide(grad_head[...]))
    edge_owners.store(grad_edge, SIDE, side_grad + small[...].T)
    planes.add_chips(2, first_part)
    copies.finish(0)
    copies.finish(1)
    mirror_copy().wait()


def reduce_kernel(n_chip, n_dp, count, *refs):
    refs = list(refs)
    take = lambda size: [refs.pop(0) for _ in range(size)]
    ready, norm_in = take(2)
    ins = take(count)
    outs, (norm_out,) = take(count + 1), take(1)
    pair_in, sums, chip_in = take(count), take(count), take(count)
    parts, copy_in = [ready] + take(count), take(count + 1)
    norm_mine, norm_dp, norm_fsdp = take(3)
    plane_sems, place_sems = take(5), take(4)
    n1_send, n1_recv, n2_send, n2_recv = refs
    places = Places(n_chip, n_dp)
    n_place = 2 * n_chip
    peers = [{"fsdp": lax.rem(places.place + j, n_place)} for j in range(1, n_place)]
    places.greet(peers + [places.same_place(t) for t in range(1, n_dp)])
    planes = PlaneReduce(places, ins, pair_in, sums, chip_in, plane_sems)
    copies = PlaceReduce(places, parts, copy_in, outs, place_sems)

    def norm_dp_copy(t):
        return remote(norm_mine, norm_dp.at[t - 1], n1_send.at[t - 1], n1_recv.at[t - 1], places.same_place(t))

    def norm_fsdp_copy(j):
        return remote(norm_out, norm_fsdp.at[j - 1], n2_send.at[j - 1], n2_recv.at[j - 1], peers[j - 1])

    for a in range(count):
        planes.start(a)
    copies.start(0)
    norm_mine[...] = norm_in[...]
    for a in range(count):
        planes.add_pair(a)
    norm_mine[0:1, :] += copies.add_copies(0)
    for a in range(count):
        planes.add_chips(a, parts[1 + a])
        copies.start(1 + a)
    for a in range(count):
        norm_mine[0:1, :] += copies.add_copies(1 + a)
    for t in range(1, n_dp):
        norm_dp_copy(t).start()
    for t in range(1, n_dp):
        norm_dp_copy(t).wait()
    norm_out[...] = norm_mine[...]
    for t in range(n_dp - 1):
        norm_out[...] += norm_dp[t]
    for j in range(1, n_place):
        norm_fsdp_copy(j).start()
    for a in range(count + 1):
        copies.finish(a)
    for j in range(1, n_place):
        norm_fsdp_copy(j).wait()
    total = norm_out[...]
    for j in range(n_place - 1):
        total = total + norm_fsdp[j]
    norm_out[...] = total


def adam_update(weight, gradient, first_state, second_state):
    first_state = beta_one * first_state + (1.0 - beta_one) * gradient
    second_state = beta_two * second_state + (1.0 - beta_two) * gradient * gradient
    step_size = (
        first_state
        / (1.0 - beta_one**adam_step)
        / (jnp.sqrt(second_state / (1.0 - beta_two**adam_step)) + adam_eps)
    )
    return (weight - learn_rate * (step_size + decay_rate * weight), first_state, second_state)


def update_kernel(factor, *refs):
    for group in range(2):
        weight, first_state, second_state, total = refs[4 * group : 4 * group + 4]
        outs = refs[8 + 4 * group : 12 + 4 * group]
        updated, first_new, second_new = adam_update(
            weight[0], wide(total[0]) * factor[0, 0], first_state[0], second_state[0]
        )
        outs[0][0], outs[1][0], outs[2][0], outs[3][0] = updated, first_new, second_new, low(updated)


def update_layers(factor, groups, slices):
    in_specs, out_specs, out_shape, operands = [], [], [], []
    for weight, first_state, second_state, total in groups:
        layers, owned, columns = weight.shape
        spec = pl.BlockSpec((1, owned, columns // slices), lambda l, c: (l, 0, c))
        in_specs += [spec] * 4
        out_specs += [spec] * 4
        operands += [weight, first_state, second_state, total]
        out_shape += [jax.ShapeDtypeStruct(weight.shape, jnp.float32)] * 3
        out_shape += [jax.ShapeDtypeStruct(weight.shape, jnp.bfloat16)]
    results = pl.pallas_call(
        update_kernel,
        grid=(LAYERS, slices),
        out_shape=out_shape,
        in_specs=[pl.BlockSpec(memory_space=pltpu.SMEM)] + in_specs,
        out_specs=out_specs,
        compiler_params=pltpu.CompilerParams(vmem_limit_bytes=48 << 20),
    )(factor.reshape(1, 1), *operands)
    return results[:4], results[4:]


def per_device(
    mesh,
    patches,
    segments,
    validity,
    image_ids,
    code_ids,
    attn_weights,
    mlp_weights,
    layer_gains,
    edge_weights,
    codebook,
    critic_weights,
    attn_first,
    attn_second,
    mlp_first,
    mlp_second,
    gains_first,
    gains_second,
    edges_first,
    edges_second,
    codebook_first,
    codebook_second,
    critic_first,
    critic_second,
):
    n_chip, n_dp = mesh.shape["fsdp"] // 2, mesh.shape["dp"]
    length = patches.shape[1]
    owned = edge_weights.shape[0]
    edge_wide = EDGE_WIDE if owned % (16 * n_dp) == 0 else -(-EDGE_WIDE // (128 * n_dp)) * 128 * n_dp
    attn_owners = Owners(n_chip, n_dp, D, 4 * D)
    mlp_owners = Owners(n_chip, n_dp, D, 2 * FF)
    edge_owners = Owners(n_chip, n_dp, D, edge_wide)
    code_owners = Owners(n_chip, n_dp, CODE_ROWS, 128)
    f32, bf16 = jnp.float32, jnp.bfloat16
    shape = jax.ShapeDtypeStruct
    vmem, anywhere = pl.BlockSpec(memory_space=pltpu.VMEM), pl.BlockSpec(memory_space=pl.ANY)
    dma = pltpu.SemaphoreType.DMA

    def scratch(kind, *dims):
        return pltpu.VMEM(dims, kind)

    def params(collective_id):
        return pltpu.CompilerParams(
            collective_id=collective_id, has_side_effects=collective_id is not None, vmem_limit_bytes=kernel_vmem
        )

    def gather_shape(columns, rows=owned):
        return shape((n_chip, 2, rows, columns), bf16)

    blank = functools.partial(jnp.zeros, dtype=f32)
    edge_shard = low(
        jnp.concatenate(
            [
                edge_weights[:, :PIX],
                blank((owned, PIX_WIDE - PIX)),
                edge_weights[:, PIX : 2 * PIX],
                blank((owned, PIX_WIDE - PIX)),
                edge_weights[:, 2 * PIX :],
                layer_gains.reshape(LAYERS * GAINS, owned).T,
                blank((owned, edge_wide - SIDE - GAIN_ROW - LAYERS * GAINS)),
            ],
            axis=1,
        )
    )
    code_shard = low(codebook).reshape(-1, 128)
    segment, valid_row, codes = segments[0], validity[0], code_ids[0]
    per_row = 128 // LAT
    info_row = jnp.stack(
        [segment, jnp.where(valid_row > 0, segment, -1), valid_row, codes // per_row, image_ids[0]]
        + [jnp.zeros_like(segment)] * 3
    )
    info_col = jnp.pad(
        jnp.stack([segment, jnp.where(valid_row > 0, segment, -1), valid_row, codes // per_row, codes % per_row], axis=1),
        ((0, 0), (0, 123)),
    )
    pixels = jnp.pad(patches[0], ((0, 0), (0, PIX_WIDE - PIX)))

    edge_all, attn_zero, attn_low, mlp_low, critic_part = pl.pallas_call(
        functools.partial(start_kernel, n_chip, n_dp),
        out_shape=[
            gather_shape(edge_wide),
            gather_shape(4 * D),
            shape((LAYERS, owned, 4 * D), bf16),
            shape((LAYERS, owned, 2 * FF), bf16),
            shape((CRITIC_ROWS, D), f32),
        ],
        in_specs=[anywhere] + [vmem] * 6,
        out_specs=[anywhere] * 2 + [vmem] * 3,
        scratch_shapes=[scratch(bf16, PIX_WIDE, D), scratch(bf16, length, D)] + Gather.semaphores(2, n_chip),
        compiler_params=params(0),
    )(edge_shard, attn_weights, mlp_weights, pixels, critic_weights, info_row, info_col)

    saved_shapes = [
        shape((length, 3 * D), bf16),
        shape((length, D), bf16),
        shape((length, 128), f32),
        shape((length, D), f32),
    ]
    stream, mixed, context, logsum, middle, encoder_low, latent, picked, decoder_in, stats, mlp_zero, _, attn_one = (
        pl.pallas_call(
            functools.partial(encode_kernel, n_chip, n_dp),
            out_shape=[shape((length, D), f32)]
            + saved_shapes
            + [
                shape((length, D), bf16),
                shape((length, 128), f32),
                shape((length, 128), f32),
                shape((length, D), f32),
                shape((8, 128), f32),
                gather_shape(2 * FF),
                gather_shape(128, code_owners.owned),
                gather_shape(4 * D),
            ],
            in_specs=[vmem] * 5 + [anywhere] * 3,
            out_specs=[vmem] * 12 + [anywhere],
            scratch_shapes=[
                scratch(f32, 128, D),
                scratch(f32, TILE, TILE + 2 * REACH),
                scratch(bf16, TILE, FF),
            ]
            + Gather.semaphores(3, n_chip),
            compiler_params=params(1),
        )(edge_all, attn_zero, pixels, info_row, info_col, mlp_low, code_shard, attn_low)
    )

    places_count = 2 * n_chip * n_dp
    share = -(-CRITIC_ROWS // places_count)
    share = share if share == 1 else -(-share // 8) * 8
    back_scratch = [
        scratch(bf16, length, D),
        scratch(bf16, length, D),
        scratch(bf16, length, D),
        scratch(bf16, length, D),
        scratch(bf16, length, D),
        scratch(bf16, length, D),
        scratch(f32, length // TILE, TILE + 2 * REACH, TILE),
        scratch(f32, length, 128),
        scratch(f32, length, 128),
    ]
    plane_scratch, plane_sems = PlaneReduce.scratch([mlp_owners.shape], n_chip, n_dp)
    mlp_part_shape = part_shapes([mlp_owners.shape], n_dp)[0]
    attn_part_shape = part_shapes([attn_owners.shape], n_dp)[0]
    grad_decoder, grad_attn_one, mlp_one_part, grad_head, small, critic_block = pl.pallas_call(
        functools.partial(decode_kernel, n_chip, n_dp, attn_owners, mlp_owners),
        out_shape=[
            shape((length, D), f32),
            attn_owners.shape,
            mlp_part_shape,
            shape((D, PIX_WIDE), bf16),
            shape((128, D), f32),
            shape((share * places_count, D), f32),
        ],
        in_specs=[vmem] * 10 + [anywhere],
        out_specs=[vmem] * 6,
        scratch_shapes=[
            scratch(bf16, n_chip, 2, owned, 2 * FF),
            scratch(f32, 128, D),
            scratch(bf16, PIX_WIDE, D),
            scratch(bf16, length, 3 * D),
            scratch(bf16, length, D),
            scratch(f32, length, 128),
            scratch(f32, length, D),
            scratch(f32, length, D),
            scratch(f32, length, D),
            scratch(bf16, *mlp_owners.shape.shape),
            scratch(bf16, length, D),
            scratch(bf16, length, PIX_WIDE),
            scratch(bf16, length, PIX_WIDE),
            scratch(f32, TILE, TILE + 2 * REACH),
            scratch(bf16, TILE, FF),
        ]
        + back_scratch
        + plane_scratch
        + Gather.semaphores(1, n_chip)
        + plane_sems,
        compiler_params=params(2),
    )(
        decoder_in,
        edge_all,
        attn_one,
        pixels,
        info_row,
        info_col,
        critic_weights,
        critic_part,
        stats,
        jnp.asarray(feature_table()),
        mlp_low,
    )

    critic_parts = critic_block.reshape(n_chip, 2, n_dp, share, D)
    later = [attn_owners.shape, shape(critic_parts.shape, f32), mlp_owners.shape]
    plane_scratch, plane_sems = PlaneReduce.scratch(later, n_chip, n_dp)
    later_parts = [mlp_part_shape] + part_shapes(later[:2], n_dp)
    place_scratch, place_sems = PlaceReduce.scratch(later_parts, n_dp)
    grad_attn, grad_edge, grad_codes, mlp_zero_part, mlp_one_total, attn_one_total, critic_all, norm_part = (
        pl.pallas_call(
            functools.partial(finish_kernel, n_chip, n_dp, attn_owners, mlp_owners, edge_owners, code_owners),
            out_shape=[
                attn_owners.shape,
                edge_owners.shape,
                code_owners.shape,
                mlp_part_shape,
                mlp_part_shape,
                attn_part_shape,
                shape((n_chip, 2, n_dp, share, D), f32),
                shape((8, 128), f32),
            ],
            in_specs=[vmem] * 16 + [anywhere] * 4,
            out_specs=[vmem] * 8,
            scratch_shapes=[
                scratch(f32, 128, D),
                scratch(f32, 128, D),
                scratch(bf16, *mlp_owners.shape.shape),
                scratch(bf16, length, 3 * D),
                scratch(f32, length, D),
                scratch(f32, length, D),
                scratch(bf16, length, 256),
            ]
            + back_scratch
            + plane_scratch
            + [scratch(p.dtype, *p.shape) for p in later_parts[1:]]
            + place_scratch
            + [scratch(f32, *later_parts[2].shape)]
            + plane_sems
            + place_sems
            + [dma((n_chip - 1,))] * 2
            + [dma(())] * 2
            + [dma((2,))],
            compiler_params=params(3),
        )(
            stream,
            context,
            logsum,
            middle,
            encoder_low,
            latent,
            picked,
            attn_zero,
            mlp_zero,
            edge_all,
            pixels,
            info_row,
            info_col,
            grad_head,
            small,
            mlp_one_part,
            mixed,
            grad_decoder,
            grad_attn_one,
            critic_parts,
        )
    )

    blocks = [grad_attn, grad_edge, grad_codes]
    plane_scratch, plane_sems = PlaneReduce.scratch(blocks, n_chip, n_dp)
    last_parts = [mlp_part_shape] + part_shapes(blocks, n_dp)
    place_scratch, place_sems = PlaceReduce.scratch(last_parts, n_dp)
    mlp_zero_total, attn_zero_total, edge_total, code_total, norm_all = pl.pallas_call(
        functools.partial(reduce_kernel, n_chip, n_dp, len(blocks)),
        out_shape=last_parts + [shape((8, 128), f32)],
        in_specs=[vmem] * 2 + [anywhere] * len(blocks),
        out_specs=[vmem] * (len(blocks) + 2),
        scratch_shapes=plane_scratch
        + [scratch(p.dtype, *p.shape) for p in last_parts[1:]]
        + place_scratch
        + [scratch(f32, 8, 128), scratch(f32, n_dp - 1, 8, 128), scratch(f32, 2 * n_chip - 1, 8, 128)]
        + plane_sems
        + place_sems
        + [dma((n_dp - 1,))] * 2
        + [dma((2 * n_chip - 1,))] * 2,
        compiler_params=params(4),
    )(mlp_zero_part, norm_part, *blocks)

    critic_total = critic_all.reshape(-1, D)
    images, gen_total, critic_sum = (critic_total[PIX + 2, place] for place in range(3))
    grad_norm = jnp.sqrt(norm_all[0, 0]) / images
    factor = jnp.minimum(1.0, clip_norm / grad_norm) / images
    attn_total = jnp.stack([attn_owners.join(attn_zero_total), attn_owners.join(attn_one_total)])
    mlp_total = jnp.stack([mlp_owners.join(mlp_zero_total), mlp_owners.join(mlp_one_total)])
    new_attn, new_mlp = update_layers(
        factor,
        [(attn_weights, attn_first, attn_second, attn_total), (mlp_weights, mlp_first, mlp_second, mlp_total)],
        4,
    )
    edge_total = wide(edge_owners.join(edge_total)) * factor
    edge_grad = jnp.concatenate(
        [edge_total[:, :PIX], edge_total[:, PIX_WIDE : PIX_WIDE + PIX], edge_total[:, SIDE : SIDE + GAIN_ROW]], axis=1
    )
    gain_grad = edge_total[:, SIDE + GAIN_ROW : SIDE + GAIN_ROW + LAYERS * GAINS].T.reshape(LAYERS, GAINS, owned)
    code_grad = wide(code_total.reshape(-1, LAT)) * factor
    new_gains = adam_update(layer_gains, gain_grad, gains_first, gains_second)
    new_edges = adam_update(edge_weights, edge_grad, edges_first, edges_second)
    new_codes = adam_update(codebook, code_grad, codebook_first, codebook_second)
    new_critic = adam_update(critic_weights, critic_total[: PIX + 2] / images, critic_first, critic_second)
    losses = jnp.stack([gen_total / images, critic_sum / images])
    return (
        *new_attn[:3],
        *new_mlp[:3],
        *new_gains,
        *new_edges,
        *new_codes,
        *new_critic,
        losses,
        grad_norm,
        new_attn[3],
        new_mlp[3],
        low(new_edges[0]),
        low(new_codes[0]),
    )


def solution(mesh):
    return jax.shard_map(
        functools.partial(per_device, mesh),
        mesh=mesh,
        in_specs=(
            P(("fsdp", "dp"), None, None),
            P(("fsdp", "dp"), None),
            P(("fsdp", "dp"), None),
            P(("fsdp", "dp"), None),
            P(("fsdp", "dp"), None),
            P(None, "fsdp", None),
            P(None, "fsdp", None),
            P(None, None, "fsdp"),
            P("fsdp", None),
            P("fsdp", None),
            P(),
            P(None, "fsdp", None),
            P(None, "fsdp", None),
            P(None, "fsdp", None),
            P(None, "fsdp", None),
            P(None, None, "fsdp"),
            P(None, None, "fsdp"),
            P("fsdp", None),
            P("fsdp", None),
            P("fsdp", None),
            P("fsdp", None),
            P(),
            P(),
        ),
        out_specs=(
            P(None, "fsdp", None),
            P(None, "fsdp", None),
            P(None, "fsdp", None),
            P(None, "fsdp", None),
            P(None, "fsdp", None),
            P(None, "fsdp", None),
            P(None, None, "fsdp"),
            P(None, None, "fsdp"),
            P(None, None, "fsdp"),
            P("fsdp", None),
            P("fsdp", None),
            P("fsdp", None),
            P("fsdp", None),
            P("fsdp", None),
            P("fsdp", None),
            P(),
            P(),
            P(),
            P(),
            P(),
            P(None, "fsdp", None),
            P(None, "fsdp", None),
            P("fsdp", None),
            P("fsdp", None),
        ),
        check_vma=False,
    )
```

```python
import functools
import math

import jax
import jax.numpy as jnp
import numpy as np
from jax import lax
from jax.experimental import pallas as pl
from jax.experimental.pallas import tpu as pltpu
from jax.sharding import PartitionSpec as P

MESH = pl.DeviceIdType.MESH
D = 512
HEADS = 8
HEAD = 64
FF = 2048
LAT = 32
CODES = 8192
PIX = 192
LAYERS = 2
TILE = 256
REACH = 256
PAIRS = HEADS // 2
EDGE = 2 * PIX + 2 * LAT + 2
GAINS = 9
PIX_WIDE = 256
SIDE = 2 * PIX_WIDE
EDGE_WIDE = SIDE + 128
GAIN_ROW = 2 * LAT + 2
CODE_ROWS = CODES * LAT // 128
CRITIC_ROWS = 200


beta_one = 0.9
beta_two = 0.95
adam_eps = 1e-08
decay_rate = 0.1
learn_rate = 0.2
clip_norm = 0.5
commit_weight = 0.25
adverse_weight = 0.2
adam_step = 10.0
norm_eps = 1e-05
excluded = -1e30
kernel_vmem = 62 << 20


def feature_table():
    pixel_idx = np.arange(PIX, dtype=np.float64)[:, None]
    frequency = np.arange(PIX, dtype=np.float64)[None, :]
    table = np.cos(np.pi * (pixel_idx + 0.5) * frequency / PIX) * (math.sqrt(2.0 / PIX) / (1.0 + frequency / 16.0))
    return np.pad(table.astype(np.float32), ((0, PIX_WIDE - PIX), (0, PIX_WIDE - PIX)))


def dot_over(left_side, right_side, left_dim, right_dim, precision=None):
    return lax.dot_general(
        left_side,
        right_side,
        (((left_dim,), (right_dim,)), ((), ())),
        precision=precision,
        preferred_element_type=jnp.float32,
    )


def dot_nn(left_side, right_side):
    return dot_over(left_side, right_side, 1, 0)


def dot_nt(left_side, right_side):
    return dot_over(left_side, right_side, 1, 1)


def dot_tn(left_side, right_side):
    return dot_over(left_side, right_side, 0, 0)


def low(values):
    return values.astype(jnp.bfloat16)


def wide(values):
    return values.astype(jnp.float32)


def center_rows(values):
    center = values - jnp.mean(values, axis=-1, keepdims=True)
    spread = jnp.mean(center * center, axis=-1, keepdims=True)
    scale = lax.rsqrt(spread + norm_eps)
    return center * scale, scale


def norm_rows_back(grad, unit, scale, gain):
    grad_unit = grad * gain
    mean_grad = jnp.mean(grad_unit, axis=-1, keepdims=True)
    mean_along = jnp.mean(grad_unit * unit, axis=-1, keepdims=True)
    return scale * (grad_unit - mean_grad - unit * mean_along)


def unit_scale(values):
    return lax.rsqrt(jnp.sum(values * values, axis=-1, keepdims=True) + 1.0)


def unit_back(grad, values, scale):
    return scale * grad - values * (scale * scale * scale * jnp.sum(values * grad, axis=-1, keepdims=True))


def gelu_tanh(values):
    cubic_term = values + 0.044715 * values * values * values
    return 0.5 * values * (1.0 + jnp.tanh(0.7978845608028654 * cubic_term))


def gelu_slope(values):
    square = values * values
    bend = jnp.tanh(0.7978845608028654 * values * (1.0 + 0.044715 * square))
    half_up = 0.5 + 0.5 * bend
    slope = half_up + 0.5 * values * (1.0 - bend * bend) * (
        0.7978845608028654 + (0.7978845608028654 * 3.0 * 0.044715) * square
    )
    return values * half_up, slope


def softplus(values):
    return jnp.maximum(values, 0.0) + jnp.log(1.0 + jnp.exp(-jnp.abs(values)))


def sigmoid(values):
    return 1.0 / (1.0 + jnp.exp(-values))


def lane_ids(shape):
    return lax.broadcasted_iota(jnp.int32, shape, 1)


def sum_rows(values):
    return jnp.sum(values, axis=0, keepdims=True)


def sum_all(values):
    return jnp.sum(jnp.sum(values, axis=0, keepdims=True), axis=1, keepdims=True)


def key_window(tile_idx, length):
    start = tile_idx * TILE
    return max(0, start - REACH), min(length, start + TILE + REACH)


def rows_at(tile_idx):
    return pl.ds(tile_idx * TILE, TILE)


def unrolled(count, body, carry=0):
    for idx in range(count):
        carry = body(idx, carry)
    return carry


def split_pair(array):
    low_half = lane_ids(array.shape) < HEAD
    zero = jnp.zeros_like(array)
    return jnp.where(low_half, array, zero), jnp.where(low_half, zero, array)


def pair_lanes(pair):
    return (pl.ds(start + pair * 128, 128) for start in (0, D, 2 * D))


def ones_lanes(rows, count):
    return low(jnp.where(lane_ids((rows, 128)) < count, 1.0, 0.0))


def minus_lanes(column):
    upper = low(column)
    rest = column - wide(upper)
    middle = low(rest)
    lower = low(rest - wide(middle))
    lanes = lane_ids((column.shape[0], 128))
    parts = jnp.where(lanes == 0, wide(upper), jnp.where(lanes == 1, wide(middle), wide(lower)))
    return low(jnp.where(lanes < 3, -parts, 0.0))


def spread_latent(values):
    return values + pltpu.roll(values, 32, 1) + pltpu.roll(values, 64, 1) + pltpu.roll(values, 96, 1)


def weight_columns(ref, first, width):
    return ref[:, :, :, pl.ds(first, width)].reshape(D, width)


def add_parts(terms, kind):
    total = wide(terms[0])
    for term in terms[1:]:
        total = total + wide(term)
    return total.astype(kind)


def no_tick(name):
    pass


class Places:
    def __init__(self, n_chip, n_dp):
        self.n_chip, self.n_dp = n_chip, n_dp
        self.place = lax.axis_index("fsdp")
        self.plane = lax.axis_index("dp")
        self.core = lax.rem(self.place, 2)
        self.chip = lax.div(self.place, 2)

    def sibling(self):
        return {"fsdp": self.place + 1 - 2 * self.core}

    def chip_at(self, j):
        return lax.rem(self.chip + j, self.n_chip)

    def same_core(self, j):
        return {"fsdp": self.chip_at(j) * 2 + self.core}

    def device(self, chip):
        return {"fsdp": chip * 2 + self.core}

    def chip_flip(self, bits):
        low_bit, high_bit = lax.rem(self.chip, 2), lax.div(self.chip, 2)
        low_bit = 1 - low_bit if bits % 2 else low_bit
        high_bit = 1 - high_bit if bits >= 2 else high_bit
        return high_bit * 2 + low_bit

    def first_near(self):
        return self.chip_flip(1) * (1 - self.core) + self.chip_flip(2) * self.core

    def second_near(self):
        return self.chip_flip(2) * (1 - self.core) + self.chip_flip(1) * self.core

    def plane_at(self, t):
        return lax.rem(self.plane + t, self.n_dp)

    def same_place(self, t):
        return {"dp": self.plane_at(t)}

    def greet(self, devices):
        barrier = pltpu.get_barrier_semaphore()
        for device in devices:
            pl.semaphore_signal(barrier, inc=1, device_id=device, device_id_type=MESH)
        pl.semaphore_wait(barrier, len(devices))

    def plane_devices(self):
        return [self.sibling()] + [self.same_core(j) for j in range(1, self.n_chip)]


def remote(source, target, send, recv, device):
    return pltpu.make_async_remote_copy(
        src_ref=source, dst_ref=target, send_sem=send, recv_sem=recv, device_id=device, device_id_type=MESH
    )


class Gather:
    def __init__(self, places, shards, outs, sems, lookahead):
        self.places, self.shards, self.outs = places, shards, outs
        self.local_sem, self.chip_send, self.chip_recv, self.pair_send, self.pair_recv = sems
        self.square = places.n_chip == 4
        count = len(shards)
        self.steps = []
        for a in range(min(lookahead, count)):
            self.start(a)
        for a in range(count):
            self.steps.append((self.middle, a))
            if a + lookahead < count:
                self.steps.append((self.start, a + lookahead))
            if a > 0:
                self.steps.append((self.end, a - 1))
        self.steps.append((self.end, count - 1))

    @staticmethod
    def semaphores(count, n_chip):
        dma = pltpu.SemaphoreType.DMA
        return [dma((count,))] + [dma((count, n_chip - 1))] * 2 + [dma((count, n_chip))] * 2

    def chip_from(self, j):
        places = self.places
        if self.square:
            return places.chip_flip(j)
        return lax.rem(places.chip + places.n_chip - j, places.n_chip)

    def chip_to(self, j):
        return self.places.chip_flip(j) if self.square else self.places.chip_at(j)

    def block(self, a, chip):
        return self.outs[a](chip, self.places.core)

    def local_copy(self, a):
        return pltpu.make_async_copy(self.shards[a], self.block(a, self.places.chip), self.local_sem.at[a])

    def chip_copy(self, a, j):
        sems = (self.chip_send.at[a, j - 1], self.chip_recv.at[a, j - 1])
        places = self.places
        if self.square and j == 3:
            source, target = self.block(a, places.first_near()), places.second_near()
            return remote(source, source, *sems, places.device(target))
        return remote(self.shards[a], self.block(a, places.chip), *sems, places.device(self.chip_to(j)))

    def pair_copy(self, a, j):
        block = self.block(a, self.chip_from(j) if j else self.places.chip)
        source = block if j else self.shards[a]
        return remote(source, block, self.pair_send.at[a, j], self.pair_recv.at[a, j], self.places.sibling())

    def start(self, a):
        for j in range(1, self.places.n_chip):
            if not (self.square and j == 3):
                self.chip_copy(a, j).start()
        self.pair_copy(a, 0).start()
        self.local_copy(a).start()

    def middle(self, a):
        near = 3 if self.square else self.places.n_chip
        for j in range(1, near):
            self.chip_copy(a, j).wait_recv()
        if self.square:
            self.chip_copy(a, 3).start()
        for j in range(1, near):
            self.pair_copy(a, j).start()

    def end(self, a):
        if self.square:
            self.chip_copy(a, 3).wait_recv()
            self.pair_copy(a, 3).start()

    def pump(self, count):
        for _ in range(min(count, len(self.steps))):
            step, a = self.steps.pop(0)
            step(a)

    def use(self, a):
        while (self.end, a) in self.steps:
            self.pump(1)
        self.local_copy(a).wait()
        for j in range(self.places.n_chip):
            self.pair_copy(a, j).wait()
            if j > 0:
                self.chip_copy(a, j).wait_send()


class PlaneReduce:
    def __init__(self, places, ins, pair_in, sums, chip_in, sems):
        self.places, self.ins, self.pair_in, self.sums, self.chip_in = places, ins, pair_in, sums, chip_in
        self.pair_send, self.pair_recv, self.local_sem, self.chip_send, self.chip_recv = sems
        self.square = places.n_chip == 4

    @staticmethod
    def scratch(arrays, n_chip, n_dp):
        shapes = []
        for outer in (n_chip, n_chip, n_chip - 1):
            shapes += [pltpu.VMEM((outer, n_dp) + a.shape[3:], a.dtype) for a in arrays]
        count, dma = len(arrays), pltpu.SemaphoreType.DMA
        return shapes, [dma((count,))] * 3 + [dma((count, n_chip - 1))] * 2

    def pair_copy(self, a):
        source = self.ins[a].at[:, 1 - self.places.core]
        return remote(source, self.pair_in[a], self.pair_send.at[a], self.pair_recv.at[a], self.places.sibling())

    def local_copy(self, a):
        return pltpu.make_async_copy(self.ins[a].at[:, self.places.core], self.sums[a], self.local_sem.at[a])

    def chip_copy(self, a, j):
        places = self.places
        sems = (self.chip_send.at[a, j - 1], self.chip_recv.at[a, j - 1])
        if not self.square:
            source, target = places.chip_at(j), places.chip_at(j)
        elif j < 3:
            source, target = (places.first_near(), places.chip_flip(3))[j - 1], places.first_near()
        else:
            source, target = places.second_near(), places.second_near()
        return remote(self.sums[a].at[source], self.chip_in[a].at[j - 1], *sems, places.device(target))

    def start(self, a):
        self.pair_copy(a).start()
        self.local_copy(a).start()

    def add_pair(self, a):
        n_chip, n_dp = self.places.n_chip, self.places.n_dp
        self.pair_copy(a).wait()
        self.local_copy(a).wait()

        def body(i, carry):
            c, d = lax.div(i, n_dp), lax.rem(i, n_dp)
            self.sums[a][c, d] = add_parts([self.sums[a][c, d], self.pair_in[a][c, d]], self.sums[a].dtype)
            return carry

        lax.fori_loop(0, n_chip * n_dp, body, 0)
        for j in range(1, 3 if self.square else n_chip):
            self.chip_copy(a, j).start()

    def relay(self, a):
        if not self.square:
            return
        for j in (1, 2):
            self.chip_copy(a, j).wait()
        near = self.places.second_near()

        def body(d, carry):
            self.sums[a][near, d] = add_parts([self.sums[a][near, d], self.chip_in[a][1, d]], self.sums[a].dtype)
            return carry

        lax.fori_loop(0, self.places.n_dp, body, 0)
        self.chip_copy(a, 3).start()

    def add_chips(self, a, part):
        n_chip, n_dp = self.places.n_chip, self.places.n_dp
        for j in (3,) if self.square else range(1, n_chip):
            self.chip_copy(a, j).wait()
        slots = (0, 2) if self.square else range(n_chip - 1)

        def body(d, carry):
            terms = [self.sums[a][self.places.chip, d]] + [self.chip_in[a][j, d] for j in slots]
            part[d] = add_parts(terms, self.sums[a].dtype)
            return carry

        lax.fori_loop(0, n_dp, body, 0)


class PlaceReduce:
    def __init__(self, places, parts, copy_in, outs, sems):
        self.places, self.parts, self.copy_in, self.outs = places, parts, copy_in, outs
        self.rs_send, self.rs_recv, self.ag_send, self.ag_recv = sems

    @staticmethod
    def scratch(parts, n_dp):
        shapes = [pltpu.VMEM((n_dp - 1,) + p.shape[1:], p.dtype) for p in parts]
        return shapes, [pltpu.SemaphoreType.DMA((len(parts), n_dp - 1))] * 4

    def rs_copy(self, a, t):
        sems = (self.rs_send.at[a, t - 1], self.rs_recv.at[a, t - 1])
        source = self.parts[a].at[self.places.plane_at(t)]
        return remote(source, self.copy_in[a].at[t - 1], *sems, self.places.same_place(t))

    def ag_copy(self, a, t):
        sems = (self.ag_send.at[a, t - 1], self.ag_recv.at[a, t - 1])
        mine = self.outs[a].at[self.places.plane]
        return remote(mine, mine, *sems, self.places.same_place(t))

    def start(self, a):
        for t in range(1, self.places.n_dp):
            self.rs_copy(a, t).start()

    def add_copies(self, a):
        n_dp, plane = self.places.n_dp, self.places.plane
        for t in range(1, n_dp):
            self.rs_copy(a, t).wait()
        terms = [self.parts[a][plane]] + [self.copy_in[a][t] for t in range(n_dp - 1)]
        total = add_parts(terms, self.outs[a].dtype)
        self.outs[a][plane] = total
        for t in range(1, n_dp):
            self.ag_copy(a, t).start()
        return sum_all(wide(total) * wide(total))

    def finish(self, a):
        for t in range(1, self.places.n_dp):
            self.ag_copy(a, t).wait()


def part_shapes(arrays, n_dp):
    return [jax.ShapeDtypeStruct((n_dp,) + a.shape[3:], a.dtype) for a in arrays]


class Owners:
    def __init__(self, n_chip, n_dp, rows, columns):
        self.owned = rows // (2 * n_chip)
        self.by_rows = self.owned % (16 * n_dp) == 0 or columns % (128 * n_dp) != 0
        tail = (self.owned // n_dp, columns) if self.by_rows else (self.owned, columns // n_dp)
        self.outer, self.columns, self.tail = (n_chip, 2, n_dp), columns, tail
        self.shape = jax.ShapeDtypeStruct(self.outer + tail, jnp.bfloat16)

    def store(self, ref, first, values):
        n_chip, _, n_dp = self.outer
        width = values.shape[1]
        if self.by_rows:
            ref[:, :, :, :, pl.ds(first, width)] = low(values.reshape(self.outer + (self.tail[0], width)))
            return
        step = min(width, self.tail[1])
        for shift in range(0, width, step):
            part, inside = divmod(first + shift, self.tail[1])
            block = values[:, shift : shift + step].reshape(n_chip, 2, self.owned, step)
            ref[:, :, part, :, pl.ds(inside, step)] = low(block)

    def join(self, parts):
        if self.by_rows:
            return parts.reshape(self.owned, self.columns)
        return parts.transpose(1, 0, 2).reshape(self.owned, self.columns)


def critic_rows(inputs_low, critic_mat, bias, readout):
    active, slope = gelu_slope(dot_nn(inputs_low, critic_mat) + bias)
    return active, slope * readout, jnp.sum(active * readout, axis=-1, keepdims=True)


def block_forward(
    stream, attn, mlp, gain, info_row, info_col, mixed, context, logsum, middle, bias, active, write, tick
):
    length = stream.shape[0]
    tiles = length // TILE

    def mix_tile(t, carry):
        unit, _ = center_rows(stream[rows_at(t), :])
        hidden = low(unit * gain(0) + gain(1))
        for part in range(3):
            mixed[rows_at(t), pl.ds(part * D, D)] = low(dot_nn(hidden, weight_columns(attn, part * D, D)))
        return carry

    unrolled(tiles, mix_tile)
    tick("mixed")
    for t in range(tiles):
        tick("tile%d" % t)
        first, last = key_window(t, length)
        span = last - first
        rows = pl.ds(t * TILE, TILE)
        window = pl.ds(first, span)
        row_place = t * TILE + lax.broadcasted_iota(jnp.int32, (TILE, span), 0)
        key_place = first + lax.broadcasted_iota(jnp.int32, (TILE, span), 1)
        allowed = (info_col[rows, 0:1] == info_row[1:2, window]) | (row_place == key_place)
        masked = jnp.where(allowed, 0.0, excluded)
        for part in range(span // TILE):
            bias[0, rows_at(part), :] = masked[:, part * TILE : (part + 1) * TILE]

        def pair_step(pair, sums):
            lanes, key_lanes, value_lanes = pair_lanes(pair)
            queries = split_pair(mixed[rows, lanes] * jnp.bfloat16(HEAD**-0.5))
            keys = mixed[window, key_lanes]
            counted = ones_lanes(span, 128)
            results = []
            for half, values in enumerate(split_pair(mixed[window, value_lanes])):
                masked = jnp.concatenate([bias[0, rows_at(part), :] for part in range(span // TILE)], axis=1)
                scores = dot_nt(queries[half], keys) + masked
                peak = jnp.max(scores, axis=-1, keepdims=True)
                powers = low(jnp.exp(scores - peak))
                total = dot_nn(powers, jnp.concatenate([values, counted], axis=1))
                weight = total[:, 128:256]
                results.append(total[:, 0:128] * (1.0 / weight))
                sums = jnp.where(lane_ids((TILE, 128)) == 2 * pair + half, peak + jnp.log(weight), sums)
            context[rows, lanes] = low(results[0] + results[1])
            return sums

        sums = jnp.zeros((TILE, 128), jnp.float32)
        for pair in range(PAIRS):
            sums = pair_step(pair, sums)
        logsum[rows, :] = sums
    tick("context")

    def mlp_tile(t, carry):
        rows = rows_at(t)
        mid = stream[rows, :] + dot_nn(context[rows, :], weight_columns(attn, 3 * D, D))
        middle[rows, :] = mid
        unit, _ = center_rows(mid)
        hidden = low(unit * gain(2) + gain(3))
        for part in range(FF // D):
            inner = dot_nn(hidden, weight_columns(mlp, part * D, D)) + gain(5 + part)
            active[rows_at(part), :] = low(gelu_tanh(inner))
        total = mid + gain(4)
        for part in range(FF // D):
            total = total + dot_nt(active[rows_at(part), :], weight_columns(mlp, FF + part * D, D))
        write(rows, total)
        return carry

    unrolled(tiles, mlp_tile)


def block_backward(
    stream, attn, mlp, gain, info_row, info_col, mixed, context, logsum, middle, grad_stream, grad_input,
    store_attn, store_mlp, small, small_row, scratch, tick,
):
    branch, active, grad_inner, hidden_low, grad_out, grad_context, bias, grad_keys, grad_values = scratch
    grad_mixed = mixed
    length = stream.shape[0]
    tiles = length // TILE

    def add_row(place, values):
        small[small_row + place : small_row + place + 1, :] += sum_rows(values)

    def hidden_tile(t, carry):
        rows = rows_at(t)
        upper_low = low(grad_stream[rows, :])
        branch[rows, :] = upper_low
        add_row(4, wide(upper_low))
        unit, _ = center_rows(middle[rows, :])
        hidden_low[rows, :] = low(unit * gain(2) + gain(3))
        grad_input[rows, :] = jnp.zeros((TILE, D), jnp.float32)
        return carry

    unrolled(tiles, hidden_tile)
    for part in range(FF // D):
        up = weight_columns(mlp, part * D, D)
        down = weight_columns(mlp, FF + part * D, D)

        def inner_tile(t, carry):
            rows = rows_at(t)
            inner = dot_nn(hidden_low[rows, :], up) + gain(5 + part)
            act, slope = gelu_slope(inner)
            active[rows, :] = low(act)
            pre_grad = low(dot_nn(branch[rows, :], down) * slope)
            grad_inner[rows, :] = pre_grad
            add_row(5 + part, wide(pre_grad))
            grad_input[rows, :] += dot_nt(pre_grad, up)
            return carry

        unrolled(tiles, inner_tile)
        store_mlp(part * D, dot_tn(hidden_low[...], grad_inner[...]))
        store_mlp(FF + part * D, dot_tn(branch[...], active[...]))
        tick("mlp%d" % part)

    def middle_tile(t, carry):
        rows = rows_at(t)
        grad_hidden = grad_input[rows, :]
        unit, scale = center_rows(middle[rows, :])
        add_row(2, grad_hidden * unit)
        add_row(3, grad_hidden)
        grad_mid = norm_rows_back(grad_hidden, unit, scale, gain(2)) + grad_stream[rows, :]
        grad_input[rows, :] = grad_mid
        mid_low = low(grad_mid)
        grad_out[rows, :] = mid_low
        grad_context[rows, :] = low(dot_nt(mid_low, weight_columns(attn, 3 * D, D)))
        return carry

    unrolled(tiles, middle_tile)
    store_attn(3 * D, dot_tn(context[...], grad_out[...]))
    for t in range(tiles):
        first, last = key_window(t, length)
        span = last - first
        key_place = first + lax.broadcasted_iota(jnp.int32, (span, TILE), 0)
        row_place = t * TILE + lax.broadcasted_iota(jnp.int32, (span, TILE), 1)
        same = info_col[pl.ds(first, span), 1:2] == info_row[0:1, pl.ds(t * TILE, TILE)]
        bias[t, 0:span, :] = jnp.where(same | (row_place == key_place), 0.0, excluded)
    tick("middle")

    def pair_step(pair, carry):
        lanes, key_lanes, value_lanes = pair_lanes(pair)
        grad_keys[...] = jnp.zeros_like(grad_keys)
        grad_values[...] = jnp.zeros_like(grad_values)
        for t in range(tiles):
            first, last = key_window(t, length)
            span = last - first
            rows = pl.ds(t * TILE, TILE)
            window = pl.ds(first, span)
            queries = split_pair(mixed[rows, lanes] * jnp.bfloat16(HEAD**-0.5))
            grads = split_pair(grad_context[rows, lanes])
            along = wide(grad_context[rows, lanes]) * wide(context[rows, lanes])
            keys = mixed[window, key_lanes]
            key_halves = split_pair(keys)
            ones = ones_lanes(span, 3)
            keys_wide = jnp.concatenate([keys, ones], axis=1)
            values_wide = jnp.concatenate([mixed[window, value_lanes], ones], axis=1)
            low_half = lane_ids((TILE, 128)) < HEAD
            add_keys, add_values, add_queries = 0.0, 0.0, 0.0
            for half in range(2):
                head = 2 * pair + half
                sums = logsum[rows, head : head + 1]
                kept = jnp.where(low_half == (half == 0), along, 0.0)
                shift = jnp.sum(kept, axis=-1, keepdims=True)
                queries_wide = jnp.concatenate([queries[half], minus_lanes(sums)], axis=1)
                grads_wide = jnp.concatenate([grads[half], minus_lanes(shift)], axis=1)
                probs = jnp.exp(dot_nt(keys_wide, queries_wide) + bias[t, 0:span, :])
                grad_scores = low(probs * dot_nt(values_wide, grads_wide))
                add_keys = add_keys + dot_nn(grad_scores, queries[half])
                add_values = add_values + dot_nn(low(probs), grads[half])
                add_queries = add_queries + dot_tn(grad_scores, key_halves[half])
            grad_keys[window, :] += add_keys
            grad_values[window, :] += add_values
            grad_mixed[rows, lanes] = low(add_queries * HEAD**-0.5)
        grad_mixed[:, key_lanes] = low(grad_keys[...])
        grad_mixed[:, value_lanes] = low(grad_values[...])
        return carry

    for pair in range(PAIRS):
        pair_step(pair, 0)
        tick("pair%d" % pair)

    def lead_tile(t, carry):
        unit, _ = center_rows(stream[rows_at(t), :])
        hidden_low[rows_at(t), :] = low(unit * gain(0) + gain(1))
        return carry

    unrolled(tiles, lead_tile)
    for part in range(3):
        store_attn(part * D, dot_tn(hidden_low[...], grad_mixed[:, pl.ds(part * D, D)]))
    tick("attn")

    def input_tile(t, carry):
        rows = rows_at(t)
        unit, scale = center_rows(stream[rows, :])
        grad_hidden = 0.0
        for part in range(3):
            columns = pl.ds(part * D, D)
            grad_hidden = grad_hidden + dot_nt(grad_mixed[rows, columns], weight_columns(attn, part * D, D))
        add_row(0, grad_hidden * unit)
        add_row(1, grad_hidden)
        grad_input[rows, :] += norm_rows_back(grad_hidden, unit, scale, gain(0))
        return carry

    unrolled(tiles, input_tile)


def side_rows(edge, side_t):
    side_t[...] = wide(weight_columns(edge, SIDE, 128)).T
    return lambda layer: lambda row: side_t[GAIN_ROW + GAINS * layer + row : GAIN_ROW + GAINS * layer + row + 1, :]


class Spill:
    def __init__(self, pairs, sems):
        self.copies = [pltpu.make_async_copy(source, target, sems.at[i]) for i, (source, target) in enumerate(pairs)]

    def start(self, *picks):
        for i in picks:
            self.copies[i].start()

    def wait(self, *picks):
        for i in picks:
            self.copies[i].wait()


def gather_target(ref, first=None, width=None):
    if first is None:
        return lambda chip, core: ref.at[chip, core]
    return lambda chip, core: ref.at[chip, core, :, pl.ds(first, width)]


def front_kernel(n_chip, n_dp, attn_owners, mlp_owners, *refs):
    refs = list(refs)
    take = lambda size: [refs.pop(0) for _ in range(size)]
    patches, info_row, info_col, critic, table = take(5)
    edge_low, codes_low, attn_low, mlp_low = take(4)
    spilled = take(11)
    grad_decoder, grad_attn, mlp_part, grad_head, small, critic_block = take(6)
    edge, attn_zero, mlp_zero, codes, attn_one, mlp_one = take(6)
    side_t, critic_mat, mixed, context, logsum, middle, stream, last_stream = take(8)
    grad_mlp = take(1)[0]
    scratch = take(9)
    encoder_low, latent, picked, forward_bias = scratch[0], scratch[7], scratch[8], scratch[6]
    normed_low, wide_pair = scratch[3], scratch[1]
    rebuilt_low, grad_rebuilt_low = (wide_pair.at[:, pl.ds(part * PIX_WIDE, PIX_WIDE)] for part in range(2))
    pair_in, sums, chip_in = take(1), take(1), take(1)
    places = Places(n_chip, n_dp)
    places.greet(places.plane_devices())
    half = FF
    shards = [edge_low, attn_low.at[0], mlp_low.at[0, :, pl.ds(0, half)], mlp_low.at[0, :, pl.ds(half, half)]]
    shards += [codes_low, attn_low.at[1], mlp_low.at[1, :, pl.ds(0, half)], mlp_low.at[1, :, pl.ds(half, half)]]
    targets = [gather_target(edge), gather_target(attn_zero)]
    targets += [gather_target(mlp_zero, 0, half), gather_target(mlp_zero, half, half)]
    targets += [gather_target(codes), gather_target(attn_one)]
    targets += [gather_target(mlp_one, 0, half), gather_target(mlp_one, half, half)]
    gather = Gather(places, shards, targets, refs[:5], 2)
    planes = PlaneReduce(places, [grad_mlp], pair_in, sums, chip_in, refs[5:10])
    kept = [edge, attn_zero, mlp_zero, last_stream, mixed, context, logsum, middle, encoder_low, latent, picked]
    spill = Spill(list(zip(kept, spilled)), refs[10])
    length = patches.shape[0]
    tiles = length // TILE
    one, row = jnp.zeros((1, 1), jnp.float32), jnp.zeros((1, D), jnp.float32)
    lanes = lane_ids((1, D))
    padding = jnp.zeros((CRITIC_ROWS - PIX - 3, D), jnp.float32)

    critic_mat[...] = jnp.zeros_like(critic_mat)
    critic_mat[0:PIX, :] = low(critic[0:PIX, :])
    critic_block[...] = jnp.zeros_like(critic_block)
    critic_grad = scratch[0]

    def critic_tile(rows, inputs_low):
        return critic_rows(inputs_low, critic_mat[...], critic[PIX : PIX + 1, :], critic[PIX + 1 : PIX + 2, :])

    def real_tile(t, carry):
        loss, bias_sum, read_sum = carry
        rows = rows_at(t)
        active, slope, logit = critic_tile(rows, patches[rows, :])
        valid = wide(info_col[rows, 2:3])
        weight = -valid * sigmoid(-logit)
        grad = low(weight * slope)
        critic_grad[rows, :] = grad
        if t == tiles - 1:
            gather.pump(2)
        loss = loss + sum_all(valid * softplus(-logit))
        return loss, bias_sum + sum_rows(wide(grad)), read_sum + sum_rows(weight * active)

    loss, bias_sum, read_sum = unrolled(tiles, real_tile, (one, row, row))
    critic_block[0:PIX, :] = dot_tn(patches[...], critic_grad[...])[0:PIX, :]
    images = info_row[4:5, :]
    first = (images != pltpu.roll(images, 1, 1)) | (lane_ids(images.shape) == 0)
    starts = sum_all(jnp.where(first & (info_row[2:3, :] > 0), 1.0, 0.0))
    scalars = jnp.where(lanes == 0, starts, jnp.where(lanes == 2, loss, 0.0))
    critic_block[PIX:CRITIC_ROWS, :] = jnp.concatenate([bias_sum, read_sum, scalars, padding], axis=0)

    gather.use(0)
    gains = side_rows(edge, side_t)

    def embed_tile(t, carry):
        last_stream[rows_at(t), :] = dot_nt(patches[rows_at(t), :], weight_columns(edge, 0, PIX_WIDE))
        return carry

    unrolled(tiles, embed_tile)
    gather.use(1)

    def zero_tick(name):
        if name == "tile2":
            gather.pump(3)
        if name == "context":
            gather.use(2)
            gather.use(3)
            spill.start(0, 1, 2, 3, 4, 5, 6)

    def write_encoder(rows, output):
        encoder_low[rows, :] = low(output)

    block_forward(
        last_stream, attn_zero, mlp_zero, gains(0), info_row, info_col, mixed, context, logsum, middle, forward_bias,
        scratch[2], write_encoder, zero_tick,
    )
    gather.use(4)
    spill.start(7, 8)

    def quantize_tile(t, commit):
        rows = rows_at(t)
        side = weight_columns(edge, SIDE, 128)
        narrow = lane_ids((TILE, 128))
        latent_rows = jnp.where(narrow < LAT, dot_nn(encoder_low[rows, :], side), 0.0)
        latent[rows, :] = latent_rows
        code_row, code_lane = info_col[rows, 3:4], info_col[rows, 4:5]
        found = jnp.zeros((TILE, 128), jnp.float32)
        for begin in range(0, CODE_ROWS, D):
            hit = lane_ids((TILE, D)) + begin == code_row
            piece = codes[...].reshape(CODE_ROWS, 128)[begin : begin + D, :]
            found = found + dot_nn(low(jnp.where(hit, 1.0, 0.0)), piece)
        found = spread_latent(jnp.where(lax.div(narrow, LAT) == code_lane, found, 0.0))
        found = jnp.where(narrow < LAT, found, 0.0)
        picked[rows, :] = found
        unit = latent_rows * unit_scale(latent_rows)
        chosen = found * unit_scale(found)
        gap = unit - chosen
        stream[rows, :] = dot_nt(low(pltpu.roll(unit + (chosen - unit), LAT, 1)), side)
        return commit + sum_all(wide(info_col[rows, 2:3]) * jnp.sum(gap * gap, axis=-1, keepdims=True))

    commit = unrolled(tiles, quantize_tile, one)
    spill.start(9, 10)
    gather.use(5)
    spill.wait(0, 1, 2, 3, 4, 5, 6)

    def one_tick(name):
        if name == "context":
            gather.use(6)
            gather.use(7)
            spill.wait(7, 8, 9, 10)

    def write_last(rows, output):
        last_stream[rows, :] = output

    block_forward(
        stream, attn_one, mlp_one, gains(1), info_row, info_col, mixed, context, logsum, middle, forward_bias,
        scratch[2], write_last, one_tick,
    )
    small[...] = jnp.zeros_like(small)

    def head_tile(t, carry):
        feature, adverse, fake_loss, bias_sum, read_sum = carry
        rows = rows_at(t)
        final_gain, final_shift = side_t[2 * LAT : 2 * LAT + 1, :], side_t[2 * LAT + 1 : 2 * LAT + 2, :]
        unit, scale = center_rows(last_stream[rows, :])
        normed = low(unit * final_gain + final_shift)
        normed_low[rows, :] = normed
        head = weight_columns(edge, PIX_WIDE, PIX_WIDE)
        rebuilt = dot_nn(normed, head)
        valid = wide(info_col[rows, 2:3])
        exact = lax.Precision.HIGHEST
        difference = dot_over(rebuilt - wide(patches[rows, :]), table[...], 1, 0, exact)
        feature = feature + sum_all(valid * jnp.sum(difference * difference, axis=-1, keepdims=True)) * (1.0 / PIX)
        grad_feature = dot_over(valid * (2.0 / PIX) * difference, table[...], 1, 1, exact)
        rebuilt_rows = low(rebuilt)
        rebuilt_low[rows, :] = rebuilt_rows
        act, slope, logit = critic_tile(rows, rebuilt_rows)
        adverse = adverse + sum_all(valid * softplus(-logit))
        fake_loss = fake_loss + sum_all(valid * softplus(logit))
        weight = valid * sigmoid(logit)
        grad_critic = low(weight * slope)
        critic_grad[rows, :] = grad_critic
        bias_sum = bias_sum + sum_rows(wide(grad_critic))
        read_sum = read_sum + sum_rows(weight * act)
        grad_pre = low((-adverse_weight) * valid * sigmoid(-logit) * slope)
        grad_rebuilt = low(grad_feature + dot_nt(grad_pre, critic_mat[...]))
        grad_rebuilt_low[rows, :] = grad_rebuilt
        grad_normed = dot_nt(grad_rebuilt, head)
        small[2 * LAT : 2 * LAT + 1, :] += sum_rows(grad_normed * unit)
        small[2 * LAT + 1 : 2 * LAT + 2, :] += sum_rows(grad_normed)
        last_stream[rows, :] = norm_rows_back(grad_normed, unit, scale, final_gain)
        return feature, adverse, fake_loss, bias_sum, read_sum

    feature, adverse, fake_loss, bias_sum, read_sum = unrolled(tiles, head_tile, (one, one, one, row, row))
    grad_head[...] = low(dot_tn(normed_low[...], grad_rebuilt_low[...]))
    critic_block[0:PIX, :] += dot_tn(rebuilt_low[...], critic_grad[...])[0:PIX, :]
    gen_local = feature + adverse_weight * adverse + commit_weight * commit
    scalars = jnp.where(lanes == 1, gen_local, jnp.where(lanes == 2, fake_loss, 0.0))
    critic_block[PIX:CRITIC_ROWS, :] += jnp.concatenate([bias_sum, read_sum, scalars, padding], axis=0)

    def tick(name):
        if name == "mlp3":
            planes.start(0)
        if name == "middle":
            planes.add_pair(0)
        if name == "pair2":
            planes.relay(0)

    block_backward(
        stream, attn_one, mlp_one, gains(1), info_row, info_col, mixed, context, logsum, middle, last_stream,
        grad_decoder, functools.partial(attn_owners.store, grad_attn), functools.partial(mlp_owners.store, grad_mlp),
        small, GAIN_ROW + GAINS, scratch, tick,
    )
    planes.add_chips(0, mlp_part)


def back_kernel(n_chip, n_dp, attn_owners, mlp_owners, edge_owners, code_owners, *refs):
    refs = list(refs)
    take = lambda size: [refs.pop(0) for _ in range(size)]
    patches, info_row, info_col, grad_head, small_in, mlp_part = take(6)
    saved = take(12)
    attn_later, critic_block = take(2)
    attn_total, mlp_total, attn_later_total, mlp_later_total, edge_total, code_total, critic_out, norm_out = take(8)
    edge, attn, mlp, mixed, context, logsum, middle, grad_encoder = take(8)
    side_t, small, grad_mlp, grad_attn, grad_edge, grad_codes, grad_input, code_grads = take(8)
    scratch = take(9)
    stream, encoder_low, latent, picked = grad_encoder, scratch[0], scratch[7], scratch[8]
    loaded = [edge, attn, mlp, stream, mixed, context, logsum, middle, encoder_low, latent, picked, grad_encoder]
    pair_in, sums, chip_in = take(5), take(5), take(5)
    parts, copy_in = take(6), take(7)
    critic_sum, norm_mine, norm_dp, norm_fsdp = take(4)
    plane_sems, late_sems, place_sems = take(5), take(5), take(4)
    spread_send, spread_recv, mirror_send, mirror_recv, n1_send, n1_recv, n2_send, n2_recv, load_sem = refs
    places = Places(n_chip, n_dp)
    n_place = 2 * n_chip
    peers = [{"fsdp": lax.rem(places.place + j, n_place)} for j in range(1, n_place)]
    chip, core = places.chip, places.core
    loads = Spill(list(zip(saved, loaded)), load_sem)
    loads.start(11, 9, 10, 8, 0, 2, 7, 1, 5, 4, 6)
    places.greet(peers + [places.same_place(t) for t in range(1, n_dp)])
    first = lambda items: list(items[0:3])
    planes = PlaneReduce(
        places, [attn_later, critic_block, grad_mlp], first(pair_in), first(sums), first(chip_in), plane_sems
    )
    again = lambda items: [items[0], items[3], items[4]]
    late = PlaneReduce(
        places, [grad_attn, grad_codes, grad_edge], again(pair_in), again(sums), again(chip_in), late_sems
    )
    totals = [mlp_later_total, attn_later_total, critic_sum, code_total, mlp_total, attn_total, edge_total]
    copies = PlaceReduce(places, [mlp_part] + parts, copy_in, totals, place_sems)

    def spread_copy(j):
        there = places.chip_at(j)
        sems = (spread_send.at[j - 1], spread_recv.at[j - 1])
        return remote(critic_sum, critic_out.at[chip, core], *sems, places.device(there))

    def mirror_copy():
        return remote(critic_out.at[:, core], critic_out.at[:, core], mirror_send, mirror_recv, places.sibling())

    def norm_dp_copy(t):
        return remote(norm_mine, norm_dp.at[t - 1], n1_send.at[t - 1], n1_recv.at[t - 1], places.same_place(t))

    def norm_fsdp_copy(j):
        return remote(norm_out, norm_fsdp.at[j - 1], n2_send.at[j - 1], n2_recv.at[j - 1], peers[j - 1])

    def add_square(a):
        norm_mine[0:1, :] += copies.add_copies(a)

    def pass_on(group, a, b):
        group.add_chips(a, parts[b - 1])
        copies.start(b)

    planes.start(0)
    planes.start(1)
    copies.start(0)
    small[...] = small_in[...]
    norm_mine[...] = jnp.zeros_like(norm_mine)
    grad_edge[...] = jnp.zeros_like(grad_edge)
    length = patches.shape[0]
    tiles = length // TILE
    loads.wait(11, 9, 10, 8, 0)
    gain = side_rows(edge, side_t)(0)

    def latent_tile(t, carry):
        grad_up, grad_down = carry
        rows = rows_at(t)
        side = weight_columns(edge, SIDE, 128)
        lanes = lane_ids((TILE, 128))
        latent_rows, found = latent[rows, :], picked[rows, :]
        scale, code_scale = unit_scale(latent_rows), unit_scale(found)
        unit, chosen = latent_rows * scale, found * code_scale
        quantized = low(pltpu.roll(unit + (chosen - unit), LAT, 1))
        grad_low = low(grad_encoder[rows, :])
        grad_up = grad_up + dot_tn(grad_low, quantized)
        grad_unit = jnp.where(lanes < LAT, pltpu.roll(dot_nn(grad_low, side), 128 - LAT, 1), 0.0)
        commit_grad = wide(info_col[rows, 2:3]) * (2.0 * commit_weight) * (unit - chosen)
        grad_latent = low(unit_back(grad_unit + commit_grad, latent_rows, scale))
        grad_down = grad_down + dot_tn(encoder_low[rows, :], grad_latent)
        grad_encoder[rows, :] = dot_nt(grad_latent, side)
        code_grad = spread_latent(unit_back(-commit_grad, found, code_scale))
        code_grad = jnp.where(lax.div(lanes, LAT) == info_col[rows, 4:5], code_grad, 0.0)
        upper = low(code_grad)
        code_grads[rows, 0:128] = upper
        code_grads[rows, 128:256] = low(code_grad - wide(upper))
        return grad_up, grad_down

    empty = jnp.zeros((D, 128), jnp.float32)
    grad_up, grad_down = unrolled(tiles, latent_tile, (empty, empty))
    small[...] += (grad_up + grad_down).T
    planes.add_pair(0)
    planes.add_pair(1)
    code_rows = code_owners.owned

    def code_step(place, carry):
        hit = lax.broadcasted_iota(jnp.int32, (code_rows, length), 0) + place * code_rows == info_row[3:4, :]
        sums_two = dot_nn(low(jnp.where(hit, 1.0, 0.0)), code_grads[...])
        total = sums_two[:, 0:128] + sums_two[:, 128:256]
        grad_codes[lax.div(place, 2), lax.rem(place, 2)] = low(total.reshape((n_dp,) + code_owners.tail))
        return carry

    lax.fori_loop(0, 2 * n_chip, code_step, 0)
    late.start(1)
    loads.wait(2, 7)

    def tick(name):
        if name == "mlp0":
            planes.relay(0)
            planes.relay(1)
            late.add_pair(1)
        if name == "mlp1":
            add_square(0)
            pass_on(planes, 0, 1)
            pass_on(planes, 1, 2)
            late.relay(1)
        if name == "mlp3":
            planes.start(2)
            pass_on(late, 1, 3)
            loads.wait(1, 5)
        if name == "middle":
            planes.add_pair(2)
            copies.add_copies(2)
            loads.start(3)
            loads.wait(4, 6)
        if name == "pair0":
            add_square(1)
            add_square(3)
        if name == "pair1":
            planes.relay(2)
            copies.finish(2)
            critic_out[chip, core] = critic_sum[...]
            for j in range(1, n_chip):
                spread_copy(j).start()
        if name == "pair2":
            pass_on(planes, 2, 4)
            copies.finish(0)
        if name == "pair3":
            for j in range(1, n_chip):
                spread_copy(j).wait()
            mirror_copy().start()
            loads.wait(3)
        if name == "attn":
            late.start(0)

    block_backward(
        stream, attn, mlp, gain, info_row, info_col, mixed, context, logsum, middle, grad_encoder, grad_input,
        functools.partial(attn_owners.store, grad_attn), functools.partial(mlp_owners.store, grad_mlp),
        small, GAIN_ROW, scratch, tick,
    )
    late.add_pair(0)
    branch = scratch[0]
    for t in range(tiles):
        branch[rows_at(t), :] = low(grad_input[rows_at(t), :])
    edge_owners.store(grad_edge, 0, dot_tn(branch[...], patches[...]))
    edge_owners.store(grad_edge, PIX_WIDE, wide(grad_head[...]))
    edge_owners.store(grad_edge, SIDE, small[...].T)
    late.start(2)
    add_square(4)
    late.relay(0)
    late.add_pair(2)
    pass_on(late, 0, 5)
    late.relay(2)
    pass_on(late, 2, 6)
    add_square(5)
    add_square(6)
    for t in range(1, n_dp):
        norm_dp_copy(t).start()
    copies.finish(1)
    copies.finish(3)
    copies.finish(4)
    mirror_copy().wait()
    for t in range(1, n_dp):
        norm_dp_copy(t).wait()
    norm_out[...] = norm_mine[...]
    for t in range(n_dp - 1):
        norm_out[...] += norm_dp[t]
    for j in range(1, n_place):
        norm_fsdp_copy(j).start()
    copies.finish(5)
    copies.finish(6)
    for j in range(1, n_place):
        norm_fsdp_copy(j).wait()
    total = norm_out[...]
    for j in range(n_place - 1):
        total = total + norm_fsdp[j]
    norm_out[...] = total


def adam_update(weight, gradient, first_state, second_state):
    first_state = beta_one * first_state + (1.0 - beta_one) * gradient
    second_state = beta_two * second_state + (1.0 - beta_two) * gradient * gradient
    step_size = (
        first_state
        / (1.0 - beta_one**adam_step)
        / (jnp.sqrt(second_state / (1.0 - beta_two**adam_step)) + adam_eps)
    )
    return (weight - learn_rate * (step_size + decay_rate * weight), first_state, second_state)


def update_kernel(factor, *refs):
    for group in range(2):
        weight, first_state, second_state, total = refs[4 * group : 4 * group + 4]
        outs = refs[8 + 4 * group : 12 + 4 * group]
        updated, first_new, second_new = adam_update(
            weight[0], wide(total[0]) * factor[0, 0], first_state[0], second_state[0]
        )
        outs[0][0], outs[1][0], outs[2][0], outs[3][0] = updated, first_new, second_new, low(updated)


def update_layers(factor, groups, slices):
    in_specs, out_specs, out_shape, operands = [], [], [], []
    for weight, first_state, second_state, total in groups:
        layers, owned, columns = weight.shape
        spec = pl.BlockSpec((1, owned, columns // slices), lambda l, c: (l, 0, c))
        in_specs += [spec] * 4
        out_specs += [spec] * 4
        operands += [weight, first_state, second_state, total]
        out_shape += [jax.ShapeDtypeStruct(weight.shape, jnp.float32)] * 3
        out_shape += [jax.ShapeDtypeStruct(weight.shape, jnp.bfloat16)]
    results = pl.pallas_call(
        update_kernel,
        grid=(LAYERS, slices),
        out_shape=out_shape,
        in_specs=[pl.BlockSpec(memory_space=pltpu.SMEM)] + in_specs,
        out_specs=out_specs,
        compiler_params=pltpu.CompilerParams(vmem_limit_bytes=48 << 20),
    )(factor.reshape(1, 1), *operands)
    return results[:4], results[4:]


def per_device(
    mesh,
    patches,
    segments,
    validity,
    image_ids,
    code_ids,
    attn_weights,
    mlp_weights,
    layer_gains,
    edge_weights,
    codebook,
    critic_weights,
    attn_first,
    attn_second,
    mlp_first,
    mlp_second,
    gains_first,
    gains_second,
    edges_first,
    edges_second,
    codebook_first,
    codebook_second,
    critic_first,
    critic_second,
):
    n_chip, n_dp = mesh.shape["fsdp"] // 2, mesh.shape["dp"]
    length = patches.shape[1]
    owned = edge_weights.shape[0]
    edge_wide = EDGE_WIDE if owned % (16 * n_dp) == 0 else -(-EDGE_WIDE // (128 * n_dp)) * 128 * n_dp
    attn_owners = Owners(n_chip, n_dp, D, 4 * D)
    mlp_owners = Owners(n_chip, n_dp, D, 2 * FF)
    edge_owners = Owners(n_chip, n_dp, D, edge_wide)
    code_owners = Owners(n_chip, n_dp, CODE_ROWS, 128)
    f32, bf16 = jnp.float32, jnp.bfloat16
    shape = jax.ShapeDtypeStruct
    vmem, anywhere = pl.BlockSpec(memory_space=pltpu.VMEM), pl.BlockSpec(memory_space=pl.ANY)
    dma = pltpu.SemaphoreType.DMA

    def scratch(kind, *dims):
        return pltpu.VMEM(dims, kind)

    def params(collective_id):
        return pltpu.CompilerParams(
            collective_id=collective_id, has_side_effects=collective_id is not None, vmem_limit_bytes=kernel_vmem
        )

    def gather_shape(columns, rows=owned):
        return shape((n_chip, 2, rows, columns), bf16)

    blank = functools.partial(jnp.zeros, dtype=f32)
    edge_shard = low(
        jnp.concatenate(
            [
                edge_weights[:, :PIX],
                blank((owned, PIX_WIDE - PIX)),
                edge_weights[:, PIX : 2 * PIX],
                blank((owned, PIX_WIDE - PIX)),
                edge_weights[:, 2 * PIX :],
                layer_gains.reshape(LAYERS * GAINS, owned).T,
                blank((owned, edge_wide - SIDE - GAIN_ROW - LAYERS * GAINS)),
            ],
            axis=1,
        )
    )
    code_shard = low(codebook).reshape(-1, 128)
    segment, valid_row, codes = segments[0], validity[0], code_ids[0]
    per_row = 128 // LAT
    info_row = jnp.stack(
        [segment, jnp.where(valid_row > 0, segment, -1), valid_row, codes // per_row, image_ids[0]]
        + [jnp.zeros_like(segment)] * 3
    )
    info_col = jnp.pad(
        jnp.stack([segment, jnp.where(valid_row > 0, segment, -1), valid_row, codes // per_row, codes % per_row], axis=1),
        ((0, 0), (0, 123)),
    )
    pixels = jnp.pad(patches[0], ((0, 0), (0, PIX_WIDE - PIX)))

    attn_low, mlp_low = low(attn_weights), low(mlp_weights)
    places_count = 2 * n_chip * n_dp
    share = -(-CRITIC_ROWS // places_count)
    share = share if share == 1 else -(-share // 8) * 8
    back_scratch = [
        scratch(bf16, length, D),
        scratch(bf16, length, D),
        scratch(bf16, length, D),
        scratch(bf16, length, D),
        scratch(bf16, length, D),
        scratch(bf16, length, D),
        scratch(f32, length // TILE, TILE + 2 * REACH, TILE),
        scratch(f32, length, 128),
        scratch(f32, length, 128),
    ]
    plane_scratch, plane_sems = PlaneReduce.scratch([mlp_owners.shape], n_chip, n_dp)
    mlp_part_shape = part_shapes([mlp_owners.shape], n_dp)[0]
    attn_part_shape = part_shapes([attn_owners.shape], n_dp)[0]
    kept = [
        gather_shape(edge_wide),
        gather_shape(4 * D),
        gather_shape(2 * FF),
        shape((length, D), f32),
        shape((length, 3 * D), bf16),
        shape((length, D), bf16),
        shape((length, 128), f32),
        shape((length, D), f32),
        shape((length, D), bf16),
        shape((length, 128), f32),
        shape((length, 128), f32),
    ]
    front_scratch = kept[:3] + [gather_shape(128, code_owners.owned), gather_shape(4 * D), gather_shape(2 * FF)]
    front_scratch += [shape((128, D), f32), shape((PIX_WIDE, D), bf16)] + kept[4:8] + [kept[3]] * 2
    front_scratch += [mlp_owners.shape]
    results = pl.pallas_call(
        functools.partial(front_kernel, n_chip, n_dp, attn_owners, mlp_owners),
        out_shape=kept
        + [
            shape((length, D), f32),
            attn_owners.shape,
            mlp_part_shape,
            shape((D, PIX_WIDE), bf16),
            shape((128, D), f32),
            shape((share * places_count, D), f32),
        ],
        in_specs=[vmem] * 5 + [anywhere] * 4,
        out_specs=[anywhere] * 11 + [vmem] * 6,
        scratch_shapes=[scratch(s.dtype, *s.shape) for s in front_scratch]
        + back_scratch
        + plane_scratch
        + Gather.semaphores(8, n_chip)
        + plane_sems
        + [dma((11,))],
        compiler_params=params(0),
    )(
        pixels,
        info_row,
        info_col,
        critic_weights,
        jnp.asarray(feature_table()),
        edge_shard,
        code_shard,
        attn_low,
        mlp_low,
    )
    edge_all, attn_zero, mlp_zero, stream, mixed, context, logsum, middle, encoder_low, latent, picked = results[:11]
    grad_decoder, grad_attn_one, mlp_one_part, grad_head, small, critic_block = results[11:]

    critic_parts = critic_block.reshape(n_chip, 2, n_dp, share, D)
    critic_shape = shape(critic_parts.shape, f32)
    reduced = [attn_owners.shape, critic_shape, mlp_owners.shape, code_owners.shape, edge_owners.shape]
    plane_scratch, _ = PlaneReduce.scratch(reduced, n_chip, n_dp)
    _, plane_sems = PlaneReduce.scratch(reduced[:3], n_chip, n_dp)
    attn_part, critic_part, mlp_part, code_part, edge_part = part_shapes(reduced, n_dp)
    last_parts = [mlp_part, attn_part, critic_part, code_part, mlp_part, attn_part, edge_part]
    place_scratch, place_sems = PlaceReduce.scratch(last_parts, n_dp)
    back_inputs = [edge_all, attn_zero, mlp_zero, stream, mixed, context, logsum, middle, encoder_low, latent, picked]
    back_inputs.append(grad_decoder)
    local = [shape((128, D), f32)] * 2 + [mlp_owners.shape, attn_owners.shape, edge_owners.shape, code_owners.shape]
    local += [shape((length, D), f32), shape((length, 256), bf16)]
    results = pl.pallas_call(
        functools.partial(back_kernel, n_chip, n_dp, attn_owners, mlp_owners, edge_owners, code_owners),
        out_shape=[attn_part, mlp_part, attn_part, mlp_part, edge_part, code_part, critic_shape, shape((8, 128), f32)],
        in_specs=[vmem] * 6 + [anywhere] * 14,
        out_specs=[vmem] * 8,
        scratch_shapes=[scratch(a.dtype, *a.shape) for a in back_inputs[:3] + back_inputs[4:8] + back_inputs[11:] + local]
        + back_scratch
        + plane_scratch
        + [scratch(p.dtype, *p.shape) for p in last_parts[1:]]
        + place_scratch
        + [scratch(f32, *critic_part.shape), scratch(f32, 8, 128)]
        + [scratch(f32, n_dp - 1, 8, 128), scratch(f32, 2 * n_chip - 1, 8, 128)]
        + plane_sems * 2
        + place_sems
        + [dma((n_chip - 1,))] * 2
        + [dma(())] * 2
        + [dma((n_dp - 1,))] * 2
        + [dma((2 * n_chip - 1,))] * 2
        + [dma((len(back_inputs),))],
        compiler_params=params(1),
    )(pixels, info_row, info_col, grad_head, small, mlp_one_part, *back_inputs, grad_attn_one, critic_parts)
    attn_zero_total, mlp_zero_total, attn_one_total, mlp_one_total, edge_total, code_total, critic_all, norm_all = results

    critic_total = critic_all.reshape(-1, D)
    images, gen_total, critic_sum = (critic_total[PIX + 2, place] for place in range(3))
    grad_norm = jnp.sqrt(norm_all[0, 0]) / images
    factor = jnp.minimum(1.0, clip_norm / grad_norm) / images
    attn_total = jnp.stack([attn_owners.join(attn_zero_total), attn_owners.join(attn_one_total)])
    mlp_total = jnp.stack([mlp_owners.join(mlp_zero_total), mlp_owners.join(mlp_one_total)])
    new_attn, new_mlp = update_layers(
        factor,
        [(attn_weights, attn_first, attn_second, attn_total), (mlp_weights, mlp_first, mlp_second, mlp_total)],
        4,
    )
    edge_total = wide(edge_owners.join(edge_total)) * factor
    edge_grad = jnp.concatenate(
        [edge_total[:, :PIX], edge_total[:, PIX_WIDE : PIX_WIDE + PIX], edge_total[:, SIDE : SIDE + GAIN_ROW]], axis=1
    )
    gain_grad = edge_total[:, SIDE + GAIN_ROW : SIDE + GAIN_ROW + LAYERS * GAINS].T.reshape(LAYERS, GAINS, owned)
    code_grad = wide(code_total.reshape(-1, LAT)) * factor
    new_gains = adam_update(layer_gains, gain_grad, gains_first, gains_second)
    new_edges = adam_update(edge_weights, edge_grad, edges_first, edges_second)
    new_codes = adam_update(codebook, code_grad, codebook_first, codebook_second)
    new_critic = adam_update(critic_weights, critic_total[: PIX + 2] / images, critic_first, critic_second)
    losses = jnp.stack([gen_total / images, critic_sum / images])
    return (
        *new_attn[:3],
        *new_mlp[:3],
        *new_gains,
        *new_edges,
        *new_codes,
        *new_critic,
        losses,
        grad_norm,
        new_attn[3],
        new_mlp[3],
        low(new_edges[0]),
        low(new_codes[0]),
    )


def solution(mesh):
    return jax.shard_map(
        functools.partial(per_device, mesh),
        mesh=mesh,
        in_specs=(
            P(("fsdp", "dp"), None, None),
            P(("fsdp", "dp"), None),
            P(("fsdp", "dp"), None),
            P(("fsdp", "dp"), None),
            P(("fsdp", "dp"), None),
            P(None, "fsdp", None),
            P(None, "fsdp", None),
            P(None, None, "fsdp"),
            P("fsdp", None),
            P("fsdp", None),
            P(),
            P(None, "fsdp", None),
            P(None, "fsdp", None),
            P(None, "fsdp", None),
            P(None, "fsdp", None),
            P(None, None, "fsdp"),
            P(None, None, "fsdp"),
            P("fsdp", None),
            P("fsdp", None),
            P("fsdp", None),
            P("fsdp", None),
            P(),
            P(),
        ),
        out_specs=(
            P(None, "fsdp", None),
            P(None, "fsdp", None),
            P(None, "fsdp", None),
            P(None, "fsdp", None),
            P(None, "fsdp", None),
            P(None, "fsdp", None),
            P(None, None, "fsdp"),
            P(None, None, "fsdp"),
            P(None, None, "fsdp"),
            P("fsdp", None),
            P("fsdp", None),
            P("fsdp", None),
            P("fsdp", None),
            P("fsdp", None),
            P("fsdp", None),
            P(),
            P(),
            P(),
            P(),
            P(),
            P(None, "fsdp", None),
            P(None, "fsdp", None),
            P("fsdp", None),
            P("fsdp", None),
        ),
        check_vma=False,
    )
```

```python
import functools
import math

import jax
import jax.numpy as jnp
import numpy as np
from jax import lax
from jax.experimental import pallas as pl
from jax.experimental.pallas import tpu as pltpu
from jax.sharding import PartitionSpec as P

MESH = pl.DeviceIdType.MESH
D = 512
HEADS = 8
HEAD = 64
FF = 2048
LAT = 32
CODES = 8192
PIX = 192
LAYERS = 2
TILE = 256
REACH = 256
PAIRS = HEADS // 2
EDGE = 2 * PIX + 2 * LAT + 2
GAINS = 9
PIX_WIDE = 256
SIDE = 2 * PIX_WIDE
EDGE_WIDE = SIDE + 128
GAIN_ROW = 2 * LAT + 2
CODE_ROWS = CODES * LAT // 128
CRITIC_ROWS = 200


beta_one = 0.9
beta_two = 0.95
adam_eps = 1e-08
decay_rate = 0.1
learn_rate = 0.2
clip_norm = 0.5
commit_weight = 0.25
adverse_weight = 0.2
adam_step = 10.0
norm_eps = 1e-05
excluded = -1e30
kernel_vmem = 62 << 20


def feature_table():
    pixel_idx = np.arange(PIX, dtype=np.float64)[:, None]
    frequency = np.arange(PIX, dtype=np.float64)[None, :]
    table = np.cos(np.pi * (pixel_idx + 0.5) * frequency / PIX) * (math.sqrt(2.0 / PIX) / (1.0 + frequency / 16.0))
    return np.pad(table.astype(np.float32), ((0, PIX_WIDE - PIX), (0, PIX_WIDE - PIX)))


def dot_over(left_side, right_side, left_dim, right_dim, precision=None):
    return lax.dot_general(
        left_side,
        right_side,
        (((left_dim,), (right_dim,)), ((), ())),
        precision=precision,
        preferred_element_type=jnp.float32,
    )


def dot_nn(left_side, right_side):
    return dot_over(left_side, right_side, 1, 0)


def dot_nt(left_side, right_side):
    return dot_over(left_side, right_side, 1, 1)


def dot_tn(left_side, right_side):
    return dot_over(left_side, right_side, 0, 0)


def low(values):
    return values.astype(jnp.bfloat16)


def wide(values):
    return values.astype(jnp.float32)


def center_rows(values):
    center = values - jnp.mean(values, axis=-1, keepdims=True)
    spread = jnp.mean(center * center, axis=-1, keepdims=True)
    scale = lax.rsqrt(spread + norm_eps)
    return center * scale, scale


def norm_rows_back(grad, unit, scale, gain):
    grad_unit = grad * gain
    mean_grad = jnp.mean(grad_unit, axis=-1, keepdims=True)
    mean_along = jnp.mean(grad_unit * unit, axis=-1, keepdims=True)
    return scale * (grad_unit - mean_grad - unit * mean_along)


def unit_scale(values):
    return lax.rsqrt(jnp.sum(values * values, axis=-1, keepdims=True) + 1.0)


def unit_back(grad, values, scale):
    return scale * grad - values * (scale * scale * scale * jnp.sum(values * grad, axis=-1, keepdims=True))


def gelu_tanh(values):
    cubic_term = values + 0.044715 * values * values * values
    return 0.5 * values * (1.0 + jnp.tanh(0.7978845608028654 * cubic_term))


def gelu_slope(values):
    square = values * values
    bend = jnp.tanh(0.7978845608028654 * values * (1.0 + 0.044715 * square))
    half_up = 0.5 + 0.5 * bend
    slope = half_up + 0.5 * values * (1.0 - bend * bend) * (
        0.7978845608028654 + (0.7978845608028654 * 3.0 * 0.044715) * square
    )
    return values * half_up, slope


def softplus(values):
    return jnp.maximum(values, 0.0) + jnp.log(1.0 + jnp.exp(-jnp.abs(values)))


def sigmoid(values):
    return 1.0 / (1.0 + jnp.exp(-values))


def lane_ids(shape):
    return lax.broadcasted_iota(jnp.int32, shape, 1)


def sum_rows(values):
    return jnp.sum(values, axis=0, keepdims=True)


def sum_all(values):
    return jnp.sum(jnp.sum(values, axis=0, keepdims=True), axis=1, keepdims=True)


def key_window(tile_idx, length):
    start = tile_idx * TILE
    return max(0, start - REACH), min(length, start + TILE + REACH)


def bias_rows(tile_idx, length):
    spans = [last - first for first, last in (key_window(t, length) for t in range(tile_idx + 1))]
    return pl.ds(sum(spans[:-1]), spans[-1])


def fill_columns(info_row, info_col):
    rows = wide(info_row[...])
    rows = jnp.concatenate([rows, jnp.zeros((120, rows.shape[1]), jnp.float32)], axis=0)
    info_col[...] = rows.T.astype(jnp.int32)


def rows_at(tile_idx):
    return pl.ds(tile_idx * TILE, TILE)


def unrolled(count, body, carry=0):
    for idx in range(count):
        carry = body(idx, carry)
    return carry


def split_pair(array):
    low_half = lane_ids(array.shape) < HEAD
    zero = jnp.zeros_like(array)
    return jnp.where(low_half, array, zero), jnp.where(low_half, zero, array)


def pair_lanes(pair):
    return (pl.ds(start + pair * 128, 128) for start in (0, D, 2 * D))


def ones_lanes(rows, count):
    return low(jnp.where(lane_ids((rows, 128)) < count, 1.0, 0.0))


def minus_lanes(column):
    upper = low(column)
    rest = column - wide(upper)
    middle = low(rest)
    lower = low(rest - wide(middle))
    lanes = lane_ids((column.shape[0], 128))
    parts = jnp.where(lanes == 0, wide(upper), jnp.where(lanes == 1, wide(middle), wide(lower)))
    return low(jnp.where(lanes < 3, -parts, 0.0))


def spread_latent(values):
    return values + pltpu.roll(values, 32, 1) + pltpu.roll(values, 64, 1) + pltpu.roll(values, 96, 1)


def weight_columns(ref, first, width):
    return ref[:, :, :, pl.ds(first, width)].reshape(D, width)


def add_parts(terms, kind):
    total = wide(terms[0])
    for term in terms[1:]:
        total = total + wide(term)
    return total.astype(kind)


def no_tick(name):
    pass


class Places:
    def __init__(self, n_chip, n_dp):
        self.n_chip, self.n_dp = n_chip, n_dp
        self.place = lax.axis_index("fsdp")
        self.plane = lax.axis_index("dp")
        self.core = lax.rem(self.place, 2)
        self.chip = lax.div(self.place, 2)

    def sibling(self):
        return {"fsdp": self.place + 1 - 2 * self.core}

    def chip_at(self, j):
        return lax.rem(self.chip + j, self.n_chip)

    def same_core(self, j):
        return {"fsdp": self.chip_at(j) * 2 + self.core}

    def device(self, chip):
        return {"fsdp": chip * 2 + self.core}

    def chip_flip(self, bits):
        low_bit, high_bit = lax.rem(self.chip, 2), lax.div(self.chip, 2)
        low_bit = 1 - low_bit if bits % 2 else low_bit
        high_bit = 1 - high_bit if bits >= 2 else high_bit
        return high_bit * 2 + low_bit

    def first_near(self):
        return self.chip_flip(1) * (1 - self.core) + self.chip_flip(2) * self.core

    def second_near(self):
        return self.chip_flip(2) * (1 - self.core) + self.chip_flip(1) * self.core

    def plane_at(self, t):
        return lax.rem(self.plane + t, self.n_dp)

    def same_place(self, t):
        return {"dp": self.plane_at(t)}

    def greet(self, devices):
        barrier = pltpu.get_barrier_semaphore()
        for device in devices:
            pl.semaphore_signal(barrier, inc=1, device_id=device, device_id_type=MESH)
        pl.semaphore_wait(barrier, len(devices))

    def plane_devices(self):
        return [self.sibling()] + [self.same_core(j) for j in range(1, self.n_chip)]


def remote(source, target, send, recv, device):
    return pltpu.make_async_remote_copy(
        src_ref=source, dst_ref=target, send_sem=send, recv_sem=recv, device_id=device, device_id_type=MESH
    )


class Gather:
    def __init__(self, places, shards, outs, sems, lookahead):
        self.places, self.shards, self.outs = places, shards, outs
        self.local_sem, self.chip_send, self.chip_recv, self.pair_send, self.pair_recv = sems
        self.square = places.n_chip == 4
        count = len(shards)
        self.steps = []
        for a in range(min(lookahead, count)):
            self.start(a)
        for a in range(count):
            self.steps.append((self.middle, a))
            if a + lookahead < count:
                self.steps.append((self.start, a + lookahead))
            if a > 0:
                self.steps.append((self.end, a - 1))
        self.steps.append((self.end, count - 1))

    @staticmethod
    def semaphores(count, n_chip):
        dma = pltpu.SemaphoreType.DMA
        return [dma((count,))] + [dma((count, n_chip - 1))] * 2 + [dma((count, n_chip))] * 2

    def chip_from(self, j):
        places = self.places
        if self.square:
            return places.chip_flip(j)
        return lax.rem(places.chip + places.n_chip - j, places.n_chip)

    def chip_to(self, j):
        return self.places.chip_flip(j) if self.square else self.places.chip_at(j)

    def block(self, a, chip):
        return self.outs[a](chip, self.places.core)

    def local_copy(self, a):
        return pltpu.make_async_copy(self.shards[a], self.block(a, self.places.chip), self.local_sem.at[a])

    def chip_copy(self, a, j):
        sems = (self.chip_send.at[a, j - 1], self.chip_recv.at[a, j - 1])
        places = self.places
        if self.square and j == 3:
            source, target = self.block(a, places.first_near()), places.second_near()
            return remote(source, source, *sems, places.device(target))
        return remote(self.shards[a], self.block(a, places.chip), *sems, places.device(self.chip_to(j)))

    def pair_copy(self, a, j):
        block = self.block(a, self.chip_from(j) if j else self.places.chip)
        source = block if j else self.shards[a]
        return remote(source, block, self.pair_send.at[a, j], self.pair_recv.at[a, j], self.places.sibling())

    def start(self, a):
        for j in range(1, self.places.n_chip):
            if not (self.square and j == 3):
                self.chip_copy(a, j).start()
        self.pair_copy(a, 0).start()
        self.local_copy(a).start()

    def middle(self, a):
        near = 3 if self.square else self.places.n_chip
        for j in range(1, near):
            self.chip_copy(a, j).wait_recv()
        if self.square:
            self.chip_copy(a, 3).start()
        for j in range(1, near):
            self.pair_copy(a, j).start()

    def end(self, a):
        if self.square:
            self.chip_copy(a, 3).wait_recv()
            self.pair_copy(a, 3).start()

    def pump(self, count):
        for _ in range(min(count, len(self.steps))):
            step, a = self.steps.pop(0)
            step(a)

    def use(self, a):
        while (self.end, a) in self.steps:
            self.pump(1)
        self.local_copy(a).wait()
        for j in range(self.places.n_chip):
            self.pair_copy(a, j).wait()
            if j > 0:
                self.chip_copy(a, j).wait_send()


class PlaneReduce:
    def __init__(self, places, ins, pair_in, sums, chip_in, sems):
        self.places, self.ins, self.pair_in, self.sums, self.chip_in = places, ins, pair_in, sums, chip_in
        self.pair_send, self.pair_recv, self.local_sem, self.chip_send, self.chip_recv = sems
        self.square = places.n_chip == 4

    @staticmethod
    def scratch(arrays, n_chip, n_dp):
        shapes = []
        for outer in (n_chip, n_chip, n_chip - 1):
            shapes += [pltpu.VMEM((outer, n_dp) + a.shape[3:], a.dtype) for a in arrays]
        count, dma = len(arrays), pltpu.SemaphoreType.DMA
        return shapes, [dma((count,))] * 3 + [dma((count, n_chip - 1))] * 2

    def pair_copy(self, a):
        source = self.ins[a].at[:, 1 - self.places.core]
        return remote(source, self.pair_in[a], self.pair_send.at[a], self.pair_recv.at[a], self.places.sibling())

    def local_copy(self, a):
        return pltpu.make_async_copy(self.ins[a].at[:, self.places.core], self.sums[a], self.local_sem.at[a])

    def chip_copy(self, a, j):
        places = self.places
        sems = (self.chip_send.at[a, j - 1], self.chip_recv.at[a, j - 1])
        if not self.square:
            source, target = places.chip_at(j), places.chip_at(j)
        elif j < 3:
            source, target = (places.first_near(), places.chip_flip(3))[j - 1], places.first_near()
        else:
            source, target = places.second_near(), places.second_near()
        return remote(self.sums[a].at[source], self.chip_in[a].at[j - 1], *sems, places.device(target))

    def start(self, a):
        self.pair_copy(a).start()
        self.local_copy(a).start()

    def add_pair(self, a):
        n_chip, n_dp = self.places.n_chip, self.places.n_dp
        self.pair_copy(a).wait()
        self.local_copy(a).wait()

        def body(i, carry):
            c, d = lax.div(i, n_dp), lax.rem(i, n_dp)
            self.sums[a][c, d] = add_parts([self.sums[a][c, d], self.pair_in[a][c, d]], self.sums[a].dtype)
            return carry

        lax.fori_loop(0, n_chip * n_dp, body, 0)
        for j in range(1, 3 if self.square else n_chip):
            self.chip_copy(a, j).start()

    def relay(self, a):
        if not self.square:
            return
        for j in (1, 2):
            self.chip_copy(a, j).wait()
        near = self.places.second_near()

        def body(d, carry):
            self.sums[a][near, d] = add_parts([self.sums[a][near, d], self.chip_in[a][1, d]], self.sums[a].dtype)
            return carry

        lax.fori_loop(0, self.places.n_dp, body, 0)
        self.chip_copy(a, 3).start()

    def add_chips(self, a, part):
        n_chip, n_dp = self.places.n_chip, self.places.n_dp
        for j in (3,) if self.square else range(1, n_chip):
            self.chip_copy(a, j).wait()
        slots = (0, 2) if self.square else range(n_chip - 1)

        def body(d, carry):
            terms = [self.sums[a][self.places.chip, d]] + [self.chip_in[a][j, d] for j in slots]
            part[d] = add_parts(terms, self.sums[a].dtype)
            return carry

        lax.fori_loop(0, n_dp, body, 0)


class PlaceReduce:
    def __init__(self, places, parts, copy_in, outs, sems):
        self.places, self.parts, self.copy_in, self.outs = places, parts, copy_in, outs
        self.rs_send, self.rs_recv, self.ag_send, self.ag_recv = sems

    @staticmethod
    def scratch(parts, n_dp):
        shapes = [pltpu.VMEM((n_dp - 1,) + p.shape[1:], p.dtype) for p in parts]
        return shapes, [pltpu.SemaphoreType.DMA((len(parts), n_dp - 1))] * 4

    def rs_copy(self, a, t):
        sems = (self.rs_send.at[a, t - 1], self.rs_recv.at[a, t - 1])
        source = self.parts[a].at[self.places.plane_at(t)]
        return remote(source, self.copy_in[a].at[t - 1], *sems, self.places.same_place(t))

    def ag_copy(self, a, t):
        sems = (self.ag_send.at[a, t - 1], self.ag_recv.at[a, t - 1])
        mine = self.outs[a].at[self.places.plane]
        return remote(mine, mine, *sems, self.places.same_place(t))

    def start(self, a):
        for t in range(1, self.places.n_dp):
            self.rs_copy(a, t).start()

    def sum_copies(self, a, kind):
        n_dp, plane = self.places.n_dp, self.places.plane
        for t in range(1, n_dp):
            self.rs_copy(a, t).wait()
        return add_parts([self.parts[a][plane]] + [self.copy_in[a][t] for t in range(n_dp - 1)], kind)

    def publish(self, a, total):
        self.outs[a][self.places.plane] = total
        for t in range(1, self.places.n_dp):
            self.ag_copy(a, t).start()
        return sum_all(wide(total) * wide(total))

    def add_copies(self, a):
        return self.publish(a, self.sum_copies(a, self.outs[a].dtype))

    def finish(self, a):
        for t in range(1, self.places.n_dp):
            self.ag_copy(a, t).wait()


def part_shapes(arrays, n_dp):
    return [jax.ShapeDtypeStruct((n_dp,) + a.shape[3:], a.dtype) for a in arrays]


class Owners:
    def __init__(self, n_chip, n_dp, rows, columns):
        self.owned = rows // (2 * n_chip)
        self.by_rows = self.owned % (16 * n_dp) == 0 or columns % (128 * n_dp) != 0
        tail = (self.owned // n_dp, columns) if self.by_rows else (self.owned, columns // n_dp)
        self.outer, self.columns, self.tail = (n_chip, 2, n_dp), columns, tail
        self.shape = jax.ShapeDtypeStruct(self.outer + tail, jnp.bfloat16)

    def store(self, ref, first, values):
        n_chip, _, n_dp = self.outer
        width = values.shape[1]
        if self.by_rows:
            ref[:, :, :, :, pl.ds(first, width)] = low(values.reshape(self.outer + (self.tail[0], width)))
            return
        step = min(width, self.tail[1])
        for shift in range(0, width, step):
            part, inside = divmod(first + shift, self.tail[1])
            block = values[:, shift : shift + step].reshape(n_chip, 2, self.owned, step)
            ref[:, :, part, :, pl.ds(inside, step)] = low(block)

    def join(self, parts):
        outer = parts.shape[:-3]
        if not self.by_rows:
            parts = jnp.moveaxis(parts, -3, -2)
        return parts.reshape(outer + (self.owned, self.columns))


def critic_rows(inputs_low, critic_mat, bias, readout):
    active, slope = gelu_slope(dot_nn(inputs_low, critic_mat) + bias)
    return active, slope * readout, jnp.sum(active * readout, axis=-1, keepdims=True)


def block_forward(
    stream, attn, mlp, gain, info_row, info_col, mixed, context, logsum, middle, bias, active, write, tick
):
    length = stream.shape[0]
    tiles = length // TILE

    def mix_tile(t, carry):
        unit, _ = center_rows(stream[rows_at(t), :])
        hidden = low(unit * gain(0) + gain(1))
        for part in range(3):
            mixed[rows_at(t), pl.ds(part * D, D)] = low(dot_nn(hidden, weight_columns(attn, part * D, D)))
        return carry

    unrolled(tiles, mix_tile)
    tick("mixed")
    for t in range(tiles):
        tick("tile%d" % t)
        first, last = key_window(t, length)
        span = last - first
        rows = pl.ds(t * TILE, TILE)
        window = pl.ds(first, span)
        row_place = t * TILE + lax.broadcasted_iota(jnp.int32, (TILE, span), 0)
        key_place = first + lax.broadcasted_iota(jnp.int32, (TILE, span), 1)
        allowed = (info_col[rows, 0:1] == info_row[1:2, window]) | (row_place == key_place)
        masked = jnp.where(allowed, 0.0, excluded)
        for part in range(span // TILE):
            bias[rows_at(part), :] = low(masked[:, part * TILE : (part + 1) * TILE])

        def pair_step(pair, sums):
            lanes, key_lanes, value_lanes = pair_lanes(pair)
            queries = split_pair(mixed[rows, lanes] * jnp.bfloat16(HEAD**-0.5))
            keys = mixed[window, key_lanes]
            counted = ones_lanes(span, 128)
            results = []
            for half, values in enumerate(split_pair(mixed[window, value_lanes])):
                masked = jnp.concatenate([bias[rows_at(part), :] for part in range(span // TILE)], axis=1)
                scores = dot_nt(queries[half], keys) + wide(masked)
                peak = jnp.max(scores, axis=-1, keepdims=True)
                powers = low(jnp.exp(scores - peak))
                total = dot_nn(powers, jnp.concatenate([values, counted], axis=1))
                weight = total[:, 128:256]
                results.append(total[:, 0:128] * (1.0 / weight))
                sums = jnp.where(lane_ids((TILE, 128)) == 2 * pair + half, peak + jnp.log(weight), sums)
            context[rows, lanes] = low(results[0] + results[1])
            return sums

        sums = jnp.zeros((TILE, 128), jnp.float32)
        for pair in range(PAIRS):
            sums = pair_step(pair, sums)
        logsum[rows, :] = sums
    tick("context")

    def mlp_tile(t, carry):
        rows = rows_at(t)
        mid = stream[rows, :] + dot_nn(context[rows, :], weight_columns(attn, 3 * D, D))
        middle[rows, :] = mid
        unit, _ = center_rows(mid)
        hidden = low(unit * gain(2) + gain(3))
        for part in range(FF // D):
            inner = dot_nn(hidden, weight_columns(mlp, part * D, D)) + gain(5 + part)
            active[rows_at(part), :] = low(gelu_tanh(inner))
        total = mid + gain(4)
        for part in range(FF // D):
            total = total + dot_nt(active[rows_at(part), :], weight_columns(mlp, FF + part * D, D))
        write(rows, total)
        tick("row%d" % t)
        return carry

    unrolled(tiles, mlp_tile)


def block_backward(
    stream, attn, mlp, gain, info_row, info_col, mixed, context, logsum, middle, grad_stream, grad_input,
    store_attn, store_mlp, small, small_row, scratch, tick,
):
    branch, active, grad_inner, hidden_low, grad_out, grad_context, bias, grad_keys, grad_values = scratch
    grad_mixed = mixed
    length = stream.shape[0]
    tiles = length // TILE

    def add_row(place, values):
        small[small_row + place : small_row + place + 1, :] += sum_rows(values)

    def hidden_tile(t, carry):
        rows = rows_at(t)
        upper_low = low(grad_stream[rows, :])
        branch[rows, :] = upper_low
        add_row(4, wide(upper_low))
        unit, _ = center_rows(middle[rows, :])
        hidden_low[rows, :] = low(unit * gain(2) + gain(3))
        grad_input[rows, :] = jnp.zeros((TILE, D), jnp.float32)
        return carry

    unrolled(tiles, hidden_tile)
    for part in range(FF // D):
        up = weight_columns(mlp, part * D, D)
        down = weight_columns(mlp, FF + part * D, D)

        def inner_tile(t, carry):
            rows = rows_at(t)
            inner = dot_nn(hidden_low[rows, :], up) + gain(5 + part)
            act, slope = gelu_slope(inner)
            active[rows, :] = low(act)
            pre_grad = low(dot_nn(branch[rows, :], down) * slope)
            grad_inner[rows, :] = pre_grad
            add_row(5 + part, wide(pre_grad))
            grad_input[rows, :] += dot_nt(pre_grad, up)
            return carry

        unrolled(tiles, inner_tile)
        store_mlp(part, 0, dot_tn(hidden_low[...], grad_inner[...]))
        store_mlp(part, 1, dot_tn(branch[...], active[...]))
        tick("mlp%d" % part)

    def middle_tile(t, carry):
        rows = rows_at(t)
        grad_hidden = grad_input[rows, :]
        unit, scale = center_rows(middle[rows, :])
        add_row(2, grad_hidden * unit)
        add_row(3, grad_hidden)
        grad_mid = norm_rows_back(grad_hidden, unit, scale, gain(2)) + grad_stream[rows, :]
        grad_input[rows, :] = grad_mid
        mid_low = low(grad_mid)
        grad_out[rows, :] = mid_low
        grad_context[rows, :] = low(dot_nt(mid_low, weight_columns(attn, 3 * D, D)))
        return carry

    unrolled(tiles, middle_tile)
    store_attn(3 * D, dot_tn(context[...], grad_out[...]))
    for t in range(tiles):
        first, last = key_window(t, length)
        span = last - first
        key_place = first + lax.broadcasted_iota(jnp.int32, (span, TILE), 0)
        row_place = t * TILE + lax.broadcasted_iota(jnp.int32, (span, TILE), 1)
        same = info_col[pl.ds(first, span), 1:2] == info_row[0:1, pl.ds(t * TILE, TILE)]
        bias[bias_rows(t, length), :] = low(jnp.where(same | (row_place == key_place), 0.0, excluded))
    tick("middle")

    def pair_step(pair, carry):
        lanes, key_lanes, value_lanes = pair_lanes(pair)
        grad_keys[...] = jnp.zeros_like(grad_keys)
        grad_values[...] = jnp.zeros_like(grad_values)
        for t in range(tiles):
            first, last = key_window(t, length)
            span = last - first
            rows = pl.ds(t * TILE, TILE)
            window = pl.ds(first, span)
            queries = split_pair(mixed[rows, lanes] * jnp.bfloat16(HEAD**-0.5))
            grads = split_pair(grad_context[rows, lanes])
            along = wide(grad_context[rows, lanes]) * wide(context[rows, lanes])
            keys = mixed[window, key_lanes]
            key_halves = split_pair(keys)
            ones = ones_lanes(span, 3)
            keys_wide = jnp.concatenate([keys, ones], axis=1)
            values_wide = jnp.concatenate([mixed[window, value_lanes], ones], axis=1)
            low_half = lane_ids((TILE, 128)) < HEAD
            add_keys, add_values, add_queries = 0.0, 0.0, 0.0
            for half in range(2):
                head = 2 * pair + half
                sums = logsum[rows, head : head + 1]
                kept = jnp.where(low_half == (half == 0), along, 0.0)
                shift = jnp.sum(kept, axis=-1, keepdims=True)
                queries_wide = jnp.concatenate([queries[half], minus_lanes(sums)], axis=1)
                grads_wide = jnp.concatenate([grads[half], minus_lanes(shift)], axis=1)
                probs = jnp.exp(dot_nt(keys_wide, queries_wide) + wide(bias[bias_rows(t, length), :]))
                grad_scores = low(probs * dot_nt(values_wide, grads_wide))
                add_keys = add_keys + dot_nn(grad_scores, queries[half])
                add_values = add_values + dot_nn(low(probs), grads[half])
                add_queries = add_queries + dot_tn(grad_scores, key_halves[half])
            grad_keys[window, :] += add_keys
            grad_values[window, :] += add_values
            grad_mixed[rows, lanes] = low(add_queries * HEAD**-0.5)
        grad_mixed[:, key_lanes] = low(grad_keys[...])
        grad_mixed[:, value_lanes] = low(grad_values[...])
        return carry

    for pair in range(PAIRS):
        pair_step(pair, 0)
        tick("pair%d" % pair)

    def lead_tile(t, carry):
        unit, _ = center_rows(stream[rows_at(t), :])
        hidden_low[rows_at(t), :] = low(unit * gain(0) + gain(1))
        return carry

    unrolled(tiles, lead_tile)
    for part in range(3):
        store_attn(part * D, dot_tn(hidden_low[...], grad_mixed[:, pl.ds(part * D, D)]))
    tick("attn")

    def input_tile(t, carry):
        rows = rows_at(t)
        unit, scale = center_rows(stream[rows, :])
        grad_hidden = 0.0
        for part in range(3):
            columns = pl.ds(part * D, D)
            grad_hidden = grad_hidden + dot_nt(grad_mixed[rows, columns], weight_columns(attn, part * D, D))
        add_row(0, grad_hidden * unit)
        add_row(1, grad_hidden)
        grad_input[rows, :] += norm_rows_back(grad_hidden, unit, scale, gain(0))
        return carry

    unrolled(tiles, input_tile)


def side_rows(edge, side_t):
    side_t[...] = wide(weight_columns(edge, SIDE, 128)).T
    return lambda layer: lambda row: side_t[GAIN_ROW + GAINS * layer + row : GAIN_ROW + GAINS * layer + row + 1, :]


class Spill:
    def __init__(self, pairs, sems):
        self.copies = [pltpu.make_async_copy(source, target, sems.at[i]) for i, (source, target) in enumerate(pairs)]

    def start(self, *picks):
        for i in picks:
            self.copies[i].start()

    def wait(self, *picks):
        for i in picks:
            self.copies[i].wait()


def gather_target(ref, first=None, width=None):
    if first is None:
        return lambda chip, core: ref.at[chip, core]
    return lambda chip, core: ref.at[chip, core, :, pl.ds(first, width)]


def edge_places(shape, gain_layer=None):
    rows, columns = (lax.broadcasted_iota(jnp.int32, shape, dim) for dim in range(2))
    if gain_layer is not None:
        return low(jnp.where(columns == rows + SIDE + GAIN_ROW + GAINS * gain_layer, 1.0, 0.0))
    pad = PIX_WIDE - PIX
    moved = rows + jnp.where(rows >= PIX, pad, 0) + jnp.where(rows >= 2 * PIX, pad, 0)
    return low(jnp.where(columns == moved, 1.0, 0.0))


def code_places(part):
    rows, columns = (lax.broadcasted_iota(jnp.int32, (LAT, 128), dim) for dim in range(2))
    return low(jnp.where(columns == rows + part * LAT, 1.0, 0.0))


def build_edges(edge_weights, layer_gains, edge_low):
    columns = edge_low.shape[1]
    total = dot_nn(low(edge_weights[...]), edge_places((EDGE, columns)))
    for l in range(LAYERS):
        total = total + dot_tn(low(layer_gains[l]), edge_places((GAINS, columns), l))
    edge_low[...] = low(total)


def build_codes(codebook, codes_low):
    rows = codes_low.shape[0]
    total = 0.0
    for part in range(128 // LAT):
        total = total + dot_nn(low(codebook[part * rows : (part + 1) * rows, :]), code_places(part))
    codes_low[...] = low(total)


def fill_pixels(patches_in, patches):
    patches[...] = jnp.zeros_like(patches)
    patches[:, 0:PIX] = patches_in[...]


def store_halves(owners, halves, part, which, values):
    parts_each = FF // D // 2
    owners.store(halves[part // parts_each], (part % parts_each * 2 + which) * D, values)


def front_kernel(n_chip, n_dp, attn_owners, mlp_owners, *refs):
    refs = list(refs)
    take = lambda size: [refs.pop(0) for _ in range(size)]
    patches_in, info_row, critic, table, edge_weights, layer_gains, codebook = take(7)
    attn_low, mlp_low = take(2)
    spilled = take(11)
    grad_decoder, grad_attn, first_part, second_part, grad_head, small, critic_block = take(7)
    edge, attn_zero, mlp_zero, codes, attn_one, mlp_one = take(6)
    side_t, critic_mat, mixed, context, logsum, middle, stream, last_stream = take(8)
    grad_mlp, (info_col, patches, edge_low, codes_low) = take(2), take(4)
    scratch = take(9)
    encoder_low, latent, picked, forward_bias = scratch[0], scratch[7], scratch[8], scratch[6]
    normed_low, wide_pair = scratch[3], scratch[1]
    rebuilt_low, grad_rebuilt_low = (wide_pair.at[:, pl.ds(part * PIX_WIDE, PIX_WIDE)] for part in range(2))
    pair_in, sums, chip_in = take(2), take(2), take(2)
    places = Places(n_chip, n_dp)
    places.greet(places.plane_devices())
    half = FF
    build_edges(edge_weights, layer_gains, edge_low)
    shards = [edge_low, attn_low.at[0], mlp_low.at[0, :, pl.ds(0, half)], mlp_low.at[0, :, pl.ds(half, half)]]
    shards += [codes_low, attn_low.at[1], mlp_low.at[1, :, pl.ds(0, half)], mlp_low.at[1, :, pl.ds(half, half)]]
    targets = [gather_target(edge), gather_target(attn_zero)]
    targets += [gather_target(mlp_zero, 0, half), gather_target(mlp_zero, half, half)]
    targets += [gather_target(codes), gather_target(attn_one)]
    targets += [gather_target(mlp_one, 0, half), gather_target(mlp_one, half, half)]
    gather = Gather(places, shards, targets, refs[:5], 2)
    build_codes(codebook, codes_low)
    planes = PlaneReduce(places, grad_mlp, pair_in, sums, chip_in, refs[5:10])
    kept = [edge, attn_zero, mlp_zero, last_stream, mixed, context, logsum, middle, encoder_low, latent, picked]
    spill = Spill(list(zip(kept, spilled)), refs[10])
    fill_columns(info_row, info_col)
    fill_pixels(patches_in, patches)
    length = patches.shape[0]
    tiles = length // TILE
    one, row = jnp.zeros((1, 1), jnp.float32), jnp.zeros((1, D), jnp.float32)
    lanes = lane_ids((1, D))
    padding = jnp.zeros((CRITIC_ROWS - PIX - 3, D), jnp.float32)

    critic_mat[...] = jnp.zeros_like(critic_mat)
    critic_mat[0:PIX, :] = low(critic[0:PIX, :])
    critic_block[...] = jnp.zeros_like(critic_block)
    critic_grad = scratch[0]

    def critic_tile(rows, inputs_low):
        return critic_rows(inputs_low, critic_mat[...], critic[PIX : PIX + 1, :], critic[PIX + 1 : PIX + 2, :])

    def real_tile(t, carry):
        loss, bias_sum, read_sum = carry
        rows = rows_at(t)
        active, slope, logit = critic_tile(rows, patches[rows, :])
        valid = wide(info_col[rows, 2:3])
        weight = -valid * sigmoid(-logit)
        grad = low(weight * slope)
        critic_grad[rows, :] = grad
        if t == tiles - 1:
            gather.pump(2)
        loss = loss + sum_all(valid * softplus(-logit))
        return loss, bias_sum + sum_rows(wide(grad)), read_sum + sum_rows(weight * active)

    loss, bias_sum, read_sum = unrolled(tiles, real_tile, (one, row, row))
    critic_block[0:PIX, :] = dot_tn(patches[...], critic_grad[...])[0:PIX, :]
    images = info_row[5:6, :]
    first = (images != pltpu.roll(images, 1, 1)) | (lane_ids(images.shape) == 0)
    starts = sum_all(jnp.where(first & (info_row[2:3, :] > 0), 1.0, 0.0))
    scalars = jnp.where(lanes == 0, starts, jnp.where(lanes == 2, loss, 0.0))
    critic_block[PIX:CRITIC_ROWS, :] = jnp.concatenate([bias_sum, read_sum, scalars, padding], axis=0)

    gather.use(0)
    gains = side_rows(edge, side_t)

    def embed_tile(t, carry):
        last_stream[rows_at(t), :] = dot_nt(patches[rows_at(t), :], weight_columns(edge, 0, PIX_WIDE))
        return carry

    unrolled(tiles, embed_tile)
    gather.use(1)

    def zero_tick(name):
        if name == "tile2":
            gather.pump(3)
        if name == "context":
            gather.use(2)
            gather.use(3)
            spill.start(0, 1, 2, 3, 4, 5, 6)

    def write_encoder(rows, output):
        encoder_low[rows, :] = low(output)

    block_forward(
        last_stream, attn_zero, mlp_zero, gains(0), info_row, info_col, mixed, context, logsum, middle, forward_bias,
        scratch[2], write_encoder, zero_tick,
    )
    gather.use(4)
    spill.start(7, 8)

    def quantize_tile(t, commit):
        rows = rows_at(t)
        side = weight_columns(edge, SIDE, 128)
        narrow = lane_ids((TILE, 128))
        latent_rows = jnp.where(narrow < LAT, dot_nn(encoder_low[rows, :], side), 0.0)
        latent[rows, :] = latent_rows
        code_row, code_lane = info_col[rows, 3:4], info_col[rows, 4:5]
        found = jnp.zeros((TILE, 128), jnp.float32)
        for begin in range(0, CODE_ROWS, D):
            hit = lane_ids((TILE, D)) + begin == code_row
            piece = codes[...].reshape(CODE_ROWS, 128)[begin : begin + D, :]
            found = found + dot_nn(low(jnp.where(hit, 1.0, 0.0)), piece)
        found = spread_latent(jnp.where(lax.div(narrow, LAT) == code_lane, found, 0.0))
        found = jnp.where(narrow < LAT, found, 0.0)
        picked[rows, :] = found
        unit = latent_rows * unit_scale(latent_rows)
        chosen = found * unit_scale(found)
        gap = unit - chosen
        stream[rows, :] = dot_nt(low(pltpu.roll(unit + (chosen - unit), LAT, 1)), side)
        return commit + sum_all(wide(info_col[rows, 2:3]) * jnp.sum(gap * gap, axis=-1, keepdims=True))

    commit = unrolled(tiles, quantize_tile, one)
    spill.start(9, 10)
    gather.use(5)
    spill.wait(0, 1, 2, 3, 4, 5, 6)

    def one_tick(name):
        if name == "tile2":
            gather.pump(2)
        if name == "context":
            gather.use(6)
            gather.use(7)
            spill.wait(7, 8, 9, 10)

    def write_last(rows, output):
        last_stream[rows, :] = output

    block_forward(
        stream, attn_one, mlp_one, gains(1), info_row, info_col, mixed, context, logsum, middle, forward_bias,
        scratch[2], write_last, one_tick,
    )
    small[...] = jnp.zeros_like(small)

    def head_tile(t, carry):
        feature, adverse, fake_loss, bias_sum, read_sum = carry
        rows = rows_at(t)
        final_gain, final_shift = side_t[2 * LAT : 2 * LAT + 1, :], side_t[2 * LAT + 1 : 2 * LAT + 2, :]
        unit, scale = center_rows(last_stream[rows, :])
        normed = low(unit * final_gain + final_shift)
        normed_low[rows, :] = normed
        head = weight_columns(edge, PIX_WIDE, PIX_WIDE)
        rebuilt = dot_nn(normed, head)
        valid = wide(info_col[rows, 2:3])
        exact = lax.Precision.HIGHEST
        difference = dot_over(rebuilt - wide(patches[rows, :]), table[...], 1, 0, exact)
        feature = feature + sum_all(valid * jnp.sum(difference * difference, axis=-1, keepdims=True)) * (1.0 / PIX)
        grad_feature = dot_over(valid * (2.0 / PIX) * difference, table[...], 1, 1, exact)
        rebuilt_rows = low(rebuilt)
        rebuilt_low[rows, :] = rebuilt_rows
        act, slope, logit = critic_tile(rows, rebuilt_rows)
        adverse = adverse + sum_all(valid * softplus(-logit))
        fake_loss = fake_loss + sum_all(valid * softplus(logit))
        weight = valid * sigmoid(logit)
        grad_critic = low(weight * slope)
        critic_grad[rows, :] = grad_critic
        bias_sum = bias_sum + sum_rows(wide(grad_critic))
        read_sum = read_sum + sum_rows(weight * act)
        grad_pre = low((-adverse_weight) * valid * sigmoid(-logit) * slope)
        grad_rebuilt = low(grad_feature + dot_nt(grad_pre, critic_mat[...]))
        grad_rebuilt_low[rows, :] = grad_rebuilt
        grad_normed = dot_nt(grad_rebuilt, head)
        small[2 * LAT : 2 * LAT + 1, :] += sum_rows(grad_normed * unit)
        small[2 * LAT + 1 : 2 * LAT + 2, :] += sum_rows(grad_normed)
        last_stream[rows, :] = norm_rows_back(grad_normed, unit, scale, final_gain)
        return feature, adverse, fake_loss, bias_sum, read_sum

    feature, adverse, fake_loss, bias_sum, read_sum = unrolled(tiles, head_tile, (one, one, one, row, row))
    grad_head[...] = low(dot_tn(normed_low[...], grad_rebuilt_low[...]))
    critic_block[0:PIX, :] += dot_tn(rebuilt_low[...], critic_grad[...])[0:PIX, :]
    gen_local = feature + adverse_weight * adverse + commit_weight * commit
    scalars = jnp.where(lanes == 1, gen_local, jnp.where(lanes == 2, fake_loss, 0.0))
    critic_block[PIX:CRITIC_ROWS, :] += jnp.concatenate([bias_sum, read_sum, scalars, padding], axis=0)

    def tick(name):
        if name == "mlp1":
            planes.start(0)
        if name == "mlp3":
            planes.start(1)
        if name == "middle":
            planes.add_pair(0)
            planes.add_pair(1)
        if name == "pair2":
            planes.relay(0)
            planes.relay(1)

    block_backward(
        stream, attn_one, mlp_one, gains(1), info_row, info_col, mixed, context, logsum, middle, last_stream,
        grad_decoder, functools.partial(attn_owners.store, grad_attn), functools.partial(store_halves, mlp_owners, grad_mlp),
        small, GAIN_ROW + GAINS, scratch, tick,
    )
    planes.add_chips(0, first_part)
    planes.add_chips(1, second_part)


def back_kernel(n_chip, n_dp, attn_owners, mlp_owners, edge_owners, code_owners, *refs):
    refs = list(refs)
    take = lambda size: [refs.pop(0) for _ in range(size)]
    patches_in, info_row, grad_head, small_in, first_part, second_part = take(6)
    saved = take(12)
    attn_later, critic_block = take(2)
    attn_totals, mlp_totals, edge_total, code_total, critic_out, report = take(6)
    edge, attn, mlp, mixed, context, logsum, middle, grad_encoder = take(8)
    side_t, small, grad_attn, grad_edge, grad_codes, grad_input, code_grads, info_col, patches = take(9)
    grad_mlp = take(2)
    scratch = take(9)
    stream, encoder_low, latent, picked = grad_encoder, scratch[0], scratch[7], scratch[8]
    loaded = [edge, attn, mlp, stream, mixed, context, logsum, middle, encoder_low, latent, picked, grad_encoder]
    pair_in, sums, chip_in = take(6), take(6), take(6)
    parts, copy_in = take(7), take(9)
    critic_sum, norm_mine, norm_dp, norm_fsdp, norm_out, critic_rows_all = take(6)
    plane_sems, late_sems, place_sems = take(5), take(5), take(4)
    spread_send, spread_recv, mirror_send, mirror_recv, n1_send, n1_recv, n2_send, n2_recv, load_sem = refs
    places = Places(n_chip, n_dp)
    n_place = 2 * n_chip
    peers = [{"fsdp": lax.rem(places.place + j, n_place)} for j in range(1, n_place)]
    chip, core = places.chip, places.core
    loads = Spill(list(zip(saved, loaded)), load_sem)
    loads.start(11, 9, 10, 8, 0, 2, 7, 1, 5, 4, 6)
    places.greet(peers + [places.same_place(t) for t in range(1, n_dp)])
    planes = PlaneReduce(
        places, [attn_later, critic_block] + grad_mlp, pair_in[0:4], sums[0:4], chip_in[0:4], plane_sems
    )
    again = lambda items: [items[0], items[4], items[5]]
    late = PlaneReduce(
        places, [grad_attn, grad_codes, grad_edge], again(pair_in), again(sums), again(chip_in), late_sems
    )
    mlp_views = [mlp_totals.at[l, half] for l in range(LAYERS) for half in range(2)]
    totals = mlp_views[2:] + [attn_totals.at[1], critic_sum, code_total]
    totals += mlp_views[:2] + [attn_totals.at[0], edge_total]
    copies = PlaceReduce(places, [first_part, second_part] + parts, copy_in, totals, place_sems)

    def spread_copy(j):
        there = places.chip_at(j)
        sems = (spread_send.at[j - 1], spread_recv.at[j - 1])
        return remote(critic_sum, critic_out.at[chip, core], *sems, places.device(there))

    def mirror_copy():
        return remote(critic_out.at[:, core], critic_out.at[:, core], mirror_send, mirror_recv, places.sibling())

    def norm_dp_copy(t):
        return remote(norm_mine, norm_dp.at[t - 1], n1_send.at[t - 1], n1_recv.at[t - 1], places.same_place(t))

    def norm_fsdp_copy(j):
        return remote(norm_out, norm_fsdp.at[j - 1], n2_send.at[j - 1], n2_recv.at[j - 1], peers[j - 1])

    def add_square(a):
        norm_mine[0:1, :] += copies.add_copies(a)

    def pass_on(group, a, b):
        group.add_chips(a, parts[b - 2])
        copies.start(b)

    planes.start(0)
    planes.start(1)
    small[...] = small_in[...]
    norm_mine[...] = jnp.zeros_like(norm_mine)
    copies.start(0)
    copies.start(1)
    fill_columns(info_row, info_col)
    fill_pixels(patches_in, patches)
    grad_edge[...] = jnp.zeros_like(grad_edge)
    length = patches.shape[0]
    tiles = length // TILE
    loads.wait(11, 9, 10, 8, 0)
    gain = side_rows(edge, side_t)(0)

    def latent_tile(t, carry):
        grad_up, grad_down = carry
        rows = rows_at(t)
        side = weight_columns(edge, SIDE, 128)
        lanes = lane_ids((TILE, 128))
        latent_rows, found = latent[rows, :], picked[rows, :]
        scale, code_scale = unit_scale(latent_rows), unit_scale(found)
        unit, chosen = latent_rows * scale, found * code_scale
        quantized = low(pltpu.roll(unit + (chosen - unit), LAT, 1))
        grad_low = low(grad_encoder[rows, :])
        grad_up = grad_up + dot_tn(grad_low, quantized)
        grad_unit = jnp.where(lanes < LAT, pltpu.roll(dot_nn(grad_low, side), 128 - LAT, 1), 0.0)
        commit_grad = wide(info_col[rows, 2:3]) * (2.0 * commit_weight) * (unit - chosen)
        grad_latent = low(unit_back(grad_unit + commit_grad, latent_rows, scale))
        grad_down = grad_down + dot_tn(encoder_low[rows, :], grad_latent)
        grad_encoder[rows, :] = dot_nt(grad_latent, side)
        code_grad = spread_latent(unit_back(-commit_grad, found, code_scale))
        code_grad = jnp.where(lax.div(lanes, LAT) == info_col[rows, 4:5], code_grad, 0.0)
        upper = low(code_grad)
        code_grads[rows, 0:128] = upper
        code_grads[rows, 128:256] = low(code_grad - wide(upper))
        return grad_up, grad_down

    empty = jnp.zeros((D, 128), jnp.float32)
    grad_up, grad_down = unrolled(tiles, latent_tile, (empty, empty))
    small[...] += (grad_up + grad_down).T
    planes.add_pair(0)
    planes.add_pair(1)
    code_rows = code_owners.owned

    def code_step(place, carry):
        hit = lax.broadcasted_iota(jnp.int32, (code_rows, length), 0) + place * code_rows == info_row[3:4, :]
        sums_two = dot_nn(low(jnp.where(hit, 1.0, 0.0)), code_grads[...])
        total = sums_two[:, 0:128] + sums_two[:, 128:256]
        grad_codes[lax.div(place, 2), lax.rem(place, 2)] = low(total.reshape((n_dp,) + code_owners.tail))
        return carry

    lax.fori_loop(0, 2 * n_chip, code_step, 0)
    late.start(1)
    loads.wait(2, 7)

    def tick(name):
        if name == "mlp0":
            planes.relay(0)
            planes.relay(1)
            late.add_pair(1)
            add_square(0)
        if name == "mlp1":
            planes.start(2)
            add_square(1)
            pass_on(planes, 0, 2)
            pass_on(planes, 1, 3)
            late.relay(1)
        if name == "mlp2":
            planes.add_pair(2)
        if name == "mlp3":
            planes.start(3)
            pass_on(late, 1, 4)
            add_square(2)
            copies.add_copies(3)
            loads.wait(1, 5)
        if name == "middle":
            planes.relay(2)
            planes.add_pair(3)
            loads.start(3)
            loads.wait(4, 6)
        if name == "pair0":
            pass_on(planes, 2, 5)
            add_square(4)
            copies.finish(3)
            critic_out[chip, core] = critic_sum[...]
            for j in range(1, n_chip):
                spread_copy(j).start()
        if name == "pair1":
            planes.relay(3)
        if name == "pair2":
            add_square(5)
            for j in range(1, n_chip):
                spread_copy(j).wait()
            mirror_copy().start()
        if name == "pair3":
            pass_on(planes, 3, 6)
            loads.wait(3)
        if name == "attn":
            late.start(0)

    block_backward(
        stream, attn, mlp, gain, info_row, info_col, mixed, context, logsum, middle, grad_encoder, grad_input,
        functools.partial(attn_owners.store, grad_attn), functools.partial(store_halves, mlp_owners, grad_mlp),
        small, GAIN_ROW, scratch, tick,
    )
    late.add_pair(0)
    branch = scratch[0]
    for t in range(tiles):
        branch[rows_at(t), :] = low(grad_input[rows_at(t), :])
    edge_owners.store(grad_edge, 0, dot_tn(branch[...], patches[...]))
    edge_owners.store(grad_edge, PIX_WIDE, wide(grad_head[...]))
    edge_owners.store(grad_edge, SIDE, small[...].T)
    late.start(2)
    late.relay(0)
    late.add_pair(2)
    add_square(6)
    pass_on(late, 0, 7)
    late.relay(2)
    pass_on(late, 2, 8)
    add_square(7)
    add_square(8)
    for t in range(1, n_dp):
        norm_dp_copy(t).start()
    for a in (0, 1, 2, 4, 5, 6):
        copies.finish(a)
    mirror_copy().wait()
    for t in range(1, n_dp):
        norm_dp_copy(t).wait()
    norm_out[...] = norm_mine[...]
    for t in range(n_dp - 1):
        norm_out[...] += norm_dp[t]
    for j in range(1, n_place):
        norm_fsdp_copy(j).start()
    copies.finish(7)
    copies.finish(8)
    for j in range(1, n_place):
        norm_fsdp_copy(j).wait()
    total = norm_out[...]
    for j in range(n_place - 1):
        total = total + norm_fsdp[j]
    critic_rows_all[...] = critic_out[...].reshape(critic_rows_all.shape)
    scalars = critic_rows_all[PIX + 2 : PIX + 3, 0:128]
    images = scalars[:, 0:1]
    grad_norm = jnp.sqrt(total[0:1, 0:1]) / images
    scale = jnp.minimum(1.0, clip_norm / grad_norm) / images
    lanes = lane_ids(report.shape)
    rest = jnp.where(lanes == 3, scale, jnp.where(lanes == 4, 1.0 / images, 0.0))
    report[...] = jnp.where(lanes == 0, grad_norm, jnp.where(lanes < 3, scalars / images, rest))


def adam_update(weight, gradient, first_state, second_state):
    first_state = beta_one * first_state + (1.0 - beta_one) * gradient
    second_state = beta_two * second_state + (1.0 - beta_two) * gradient * gradient
    step_size = (
        first_state
        / (1.0 - beta_one**adam_step)
        / (jnp.sqrt(second_state / (1.0 - beta_two**adam_step)) + adam_eps)
    )
    return (weight - learn_rate * (step_size + decay_rate * weight), first_state, second_state)


def update_kernel(factor, *refs):
    scale = factor[0, 0]
    states, totals, outs = (refs[0:3], refs[3:6]), refs[6:9], (refs[9:13], refs[13:17])
    gradients = (totals[0][0], jnp.concatenate([totals[1][0, 0], totals[2][0, 0]], axis=1))
    for state, gradient, out in zip(states, gradients, outs):
        weight, first_state, second_state = (ref[0] for ref in state)
        updated, first_new, second_new = adam_update(weight, wide(gradient) * scale, first_state, second_state)
        out[0][0], out[1][0], out[2][0], out[3][0] = updated, first_new, second_new, low(updated)


def update_layers(factor, attn, mlp, attn_total, mlp_total):
    owned = attn[0].shape[1]
    slices = FF // D
    each = slices // 2

    def stored(block):
        place = block % slices * 2 + block // slices
        return place // slices, place % slices

    def mlp_spec(shift):
        return pl.BlockSpec((1, 1, owned, D), lambda l, c: (l, stored(2 * c + shift)[0], 0, stored(2 * c + shift)[1]))

    state_specs, out_shape = [], []
    for weight in (attn[0], mlp[0]):
        state_specs.append(pl.BlockSpec((1, owned, weight.shape[2] // slices), lambda l, c: (l, 0, c)))
        out_shape += [jax.ShapeDtypeStruct(weight.shape, jnp.float32)] * 3
        out_shape += [jax.ShapeDtypeStruct(weight.shape, jnp.bfloat16)]
    attn_spec, mlp_states = state_specs
    results = pl.pallas_call(
        update_kernel,
        grid=(LAYERS, slices),
        out_shape=out_shape,
        in_specs=[pl.BlockSpec(memory_space=pltpu.SMEM)]
        + [attn_spec] * 3
        + [mlp_states] * 3
        + [attn_spec, mlp_spec(0), mlp_spec(1)],
        out_specs=[attn_spec] * 4 + [mlp_states] * 4,
        compiler_params=pltpu.CompilerParams(vmem_limit_bytes=48 << 20),
    )(factor.reshape(1, 1), *attn, *mlp, attn_total, mlp_total, mlp_total)
    return results[:4], results[4:]


def per_device(
    mesh,
    patches,
    segments,
    validity,
    image_ids,
    code_ids,
    attn_weights,
    mlp_weights,
    layer_gains,
    edge_weights,
    codebook,
    critic_weights,
    attn_first,
    attn_second,
    mlp_first,
    mlp_second,
    gains_first,
    gains_second,
    edges_first,
    edges_second,
    codebook_first,
    codebook_second,
    critic_first,
    critic_second,
):
    n_chip, n_dp = mesh.shape["fsdp"] // 2, mesh.shape["dp"]
    length = patches.shape[1]
    owned = edge_weights.shape[0]
    edge_wide = EDGE_WIDE if owned % (16 * n_dp) == 0 else -(-EDGE_WIDE // (128 * n_dp)) * 128 * n_dp
    attn_owners = Owners(n_chip, n_dp, D, 4 * D)
    mlp_owners = Owners(n_chip, n_dp, D, FF)
    edge_owners = Owners(n_chip, n_dp, D, edge_wide)
    code_owners = Owners(n_chip, n_dp, CODE_ROWS, 128)
    f32, bf16 = jnp.float32, jnp.bfloat16
    shape = jax.ShapeDtypeStruct
    vmem, anywhere = pl.BlockSpec(memory_space=pltpu.VMEM), pl.BlockSpec(memory_space=pl.ANY)
    dma = pltpu.SemaphoreType.DMA

    def scratch(kind, *dims):
        return pltpu.VMEM(dims, kind)

    def params(collective_id):
        return pltpu.CompilerParams(
            collective_id=collective_id, has_side_effects=collective_id is not None, vmem_limit_bytes=kernel_vmem
        )

    def gather_shape(columns, rows=owned):
        return shape((n_chip, 2, rows, columns), bf16)

    local_bits = (CODES // (2 * n_chip)).bit_length() - 1
    part_bits = local_bits - (128 // LAT).bit_length() + 1
    local = code_ids & ((1 << local_bits) - 1)
    code_row = ((code_ids >> local_bits) << part_bits) + (local & ((1 << part_bits) - 1))
    info_row = jnp.concatenate(
        [segments, jnp.where(validity > 0, segments, -1), validity, code_row, local >> part_bits] + [image_ids] * 3
    )
    pixels = patches.reshape(length, PIX)

    attn_low, mlp_low = low(attn_weights), low(mlp_weights)
    places_count = 2 * n_chip * n_dp
    share = -(-CRITIC_ROWS // places_count)
    share = share if share == 1 else -(-share // 8) * 8
    back_scratch = [
        scratch(bf16, length, D),
        scratch(bf16, length, D),
        scratch(bf16, length, D),
        scratch(bf16, length, D),
        scratch(bf16, length, D),
        scratch(bf16, length, D),
        scratch(bf16, sum(last - first for first, last in (key_window(t, length) for t in range(length // TILE))), TILE),
        scratch(f32, length, 128),
        scratch(f32, length, 128),
    ]
    plane_scratch, plane_sems = PlaneReduce.scratch([mlp_owners.shape] * 2, n_chip, n_dp)
    half_part = part_shapes([mlp_owners.shape], n_dp)[0]
    kept = [
        gather_shape(edge_wide),
        gather_shape(4 * D),
        gather_shape(2 * FF),
        shape((length, D), f32),
        shape((length, 3 * D), bf16),
        shape((length, D), bf16),
        shape((length, 128), f32),
        shape((length, D), f32),
        shape((length, D), bf16),
        shape((length, 128), f32),
        shape((length, 128), f32),
    ]
    front_scratch = kept[:3] + [gather_shape(128, code_owners.owned), gather_shape(4 * D), gather_shape(2 * FF)]
    front_scratch += [shape((128, D), f32), shape((PIX_WIDE, D), bf16)] + kept[4:8] + [kept[3]] * 2
    front_scratch += [mlp_owners.shape] * 2 + [shape((length, 128), jnp.int32), shape((length, PIX_WIDE), bf16)]
    front_scratch += [shape((owned, edge_wide), bf16), shape((code_owners.owned, 128), bf16)]
    results = pl.pallas_call(
        functools.partial(front_kernel, n_chip, n_dp, attn_owners, mlp_owners),
        out_shape=kept
        + [
            shape((length, D), f32),
            attn_owners.shape,
            half_part,
            half_part,
            shape((D, PIX_WIDE), bf16),
            shape((128, D), f32),
            shape((share * places_count, D), f32),
        ],
        in_specs=[vmem] * 7 + [anywhere] * 2,
        out_specs=[anywhere] * 11 + [vmem] * 7,
        scratch_shapes=[scratch(s.dtype, *s.shape) for s in front_scratch]
        + back_scratch
        + plane_scratch
        + Gather.semaphores(8, n_chip)
        + plane_sems
        + [dma((11,))],
        compiler_params=params(0),
    )(
        pixels,
        info_row,
        critic_weights,
        jnp.asarray(feature_table()),
        edge_weights,
        layer_gains,
        codebook,
        attn_low,
        mlp_low,
    )
    edge_all, attn_zero, mlp_zero, stream, mixed, context, logsum, middle, encoder_low, latent, picked = results[:11]
    grad_decoder, grad_attn_one, first_part, second_part, grad_head, small, critic_block = results[11:]

    critic_parts = critic_block.reshape(n_chip, 2, n_dp, share, D)
    critic_shape = shape(critic_parts.shape, f32)
    reduced = [attn_owners.shape, critic_shape] + [mlp_owners.shape] * 2 + [code_owners.shape, edge_owners.shape]
    plane_scratch, _ = PlaneReduce.scratch(reduced, n_chip, n_dp)
    _, plane_sems = PlaneReduce.scratch(reduced[:4], n_chip, n_dp)
    _, late_sems = PlaneReduce.scratch(reduced[:3], n_chip, n_dp)
    attn_part, critic_part, mlp_part, _, code_part, edge_part = part_shapes(reduced, n_dp)
    last_parts = [attn_part, critic_part, code_part, mlp_part, mlp_part, attn_part, edge_part]
    place_scratch, _ = PlaceReduce.scratch([mlp_part] * 2 + last_parts, n_dp)
    _, place_sems = PlaceReduce.scratch([mlp_part] * 2 + last_parts, n_dp)
    back_inputs = [edge_all, attn_zero, mlp_zero, stream, mixed, context, logsum, middle, encoder_low, latent, picked]
    back_inputs.append(grad_decoder)
    local = [shape((128, D), f32)] * 2 + [attn_owners.shape, edge_owners.shape, code_owners.shape]
    local += [shape((length, D), f32), shape((length, 256), bf16), shape((length, 128), jnp.int32)]
    local += [shape((length, PIX_WIDE), bf16)] + [mlp_owners.shape] * 2
    results = pl.pallas_call(
        functools.partial(back_kernel, n_chip, n_dp, attn_owners, mlp_owners, edge_owners, code_owners),
        out_shape=[
            shape((LAYERS,) + attn_part.shape, bf16),
            shape((LAYERS, 2) + mlp_part.shape, bf16),
            edge_part,
            code_part,
            critic_shape,
            shape((8, 128), f32),
        ],
        in_specs=[vmem] * 6 + [anywhere] * 14,
        out_specs=[vmem] * 6,
        scratch_shapes=[
            scratch(a.dtype, *a.shape) for a in back_inputs[:3] + back_inputs[4:8] + back_inputs[11:] + local
        ]
        + back_scratch
        + plane_scratch
        + [scratch(p.dtype, *p.shape) for p in last_parts]
        + place_scratch
        + [scratch(f32, *critic_part.shape), scratch(f32, 8, 128)]
        + [scratch(f32, n_dp - 1, 8, 128), scratch(f32, 2 * n_chip - 1, 8, 128), scratch(f32, 8, 128)]
        + [scratch(f32, share * places_count, D)]
        + plane_sems
        + late_sems
        + place_sems
        + [dma((n_chip - 1,))] * 2
        + [dma(())] * 2
        + [dma((n_dp - 1,))] * 2
        + [dma((2 * n_chip - 1,))] * 2
        + [dma((len(back_inputs),))],
        compiler_params=params(1),
    )(pixels, info_row, grad_head, small, first_part, second_part, *back_inputs, grad_attn_one, critic_parts)
    attn_totals, mlp_totals, edge_total, code_total, critic_all, report = results

    critic_total, factor = critic_all.reshape(-1, D), report[0, 3]
    new_attn, new_mlp = update_layers(
        factor,
        (attn_weights, attn_first, attn_second),
        (mlp_weights, mlp_first, mlp_second),
        attn_owners.join(attn_totals),
        mlp_owners.join(mlp_totals),
    )
    edge_total = wide(edge_owners.join(edge_total)) * factor
    edge_grad = jnp.concatenate(
        [edge_total[:, :PIX], edge_total[:, PIX_WIDE : PIX_WIDE + PIX], edge_total[:, SIDE : SIDE + GAIN_ROW]], axis=1
    )
    gain_grad = edge_total[:, SIDE + GAIN_ROW : SIDE + GAIN_ROW + LAYERS * GAINS].T.reshape(LAYERS, GAINS, owned)
    code_parts = code_total.reshape(-1, 128 // LAT, LAT).transpose(1, 0, 2)
    code_grad = wide(code_parts.reshape(-1, LAT)) * factor
    new_gains = adam_update(layer_gains, gain_grad, gains_first, gains_second)
    new_edges = adam_update(edge_weights, edge_grad, edges_first, edges_second)
    new_codes = adam_update(codebook, code_grad, codebook_first, codebook_second)
    new_critic = adam_update(critic_weights, critic_total[: PIX + 2] * report[0, 4], critic_first, critic_second)
    losses, grad_norm = report[0, 1:3], report[0, 0]
    return (
        *new_attn[:3],
        *new_mlp[:3],
        *new_gains,
        *new_edges,
        *new_codes,
        *new_critic,
        losses,
        grad_norm,
        new_attn[3],
        new_mlp[3],
        low(new_edges[0]),
        low(new_codes[0]),
    )


def solution(mesh):
    return jax.shard_map(
        functools.partial(per_device, mesh),
        mesh=mesh,
        in_specs=(
            P(("fsdp", "dp"), None, None),
            P(("fsdp", "dp"), None),
            P(("fsdp", "dp"), None),
            P(("fsdp", "dp"), None),
            P(("fsdp", "dp"), None),
            P(None, "fsdp", None),
            P(None, "fsdp", None),
            P(None, None, "fsdp"),
            P("fsdp", None),
            P("fsdp", None),
            P(),
            P(None, "fsdp", None),
            P(None, "fsdp", None),
            P(None, "fsdp", None),
            P(None, "fsdp", None),
            P(None, None, "fsdp"),
            P(None, None, "fsdp"),
            P("fsdp", None),
            P("fsdp", None),
            P("fsdp", None),
            P("fsdp", None),
            P(),
            P(),
        ),
        out_specs=(
            P(None, "fsdp", None),
            P(None, "fsdp", None),
            P(None, "fsdp", None),
            P(None, "fsdp", None),
            P(None, "fsdp", None),
            P(None, "fsdp", None),
            P(None, None, "fsdp"),
            P(None, None, "fsdp"),
            P(None, None, "fsdp"),
            P("fsdp", None),
            P("fsdp", None),
            P("fsdp", None),
            P("fsdp", None),
            P("fsdp", None),
            P("fsdp", None),
            P(),
            P(),
            P(),
            P(),
            P(),
            P(None, "fsdp", None),
            P(None, "fsdp", None),
            P("fsdp", None),
            P("fsdp", None),
        ),
        check_vma=False,
    )
```
